32 devices in a mesh: wide: 8 (over z, x), narrow: 4 (over y, core).
Axes of the slice: x: 2, y: 2, z: 4, core: 2. Of those that a mesh axis runs over, the one named last changes fastest.
Arguments:
- dec_input: bfloat16 [24, 512, 768], P('wide', 'narrow'), may hold values from -6 to 6
- enc_out: bfloat16 [24, 4096, 768], P('wide', 'narrow'), may hold values from -6 to 6
- enc_len: int32 [24], P('wide'), may hold values from 512 to 4096, as said below
- cotangent: bfloat16 [24, 512, 768], P('wide', 'narrow'), may hold values from -6 to 6
- self_query: float32 [768, 768], P('wide'), may hold values from -0.0546875 to 0.0546875
- self_key: float32 [768, 768], P('wide'), may hold values from -0.21875 to 0.21875
- self_value: float32 [768, 768], P('wide'), may hold values from -0.21875 to 0.21875
- self_output: float32 [768, 768], P('wide'), may hold values from -0.4375 to 0.4375
- cross_query: float32 [768, 768], P('wide'), may hold values from -0.0546875 to 0.0546875
- cross_key: float32 [768, 768], P('wide'), may hold values from -0.21875 to 0.21875
- cross_value: float32 [768, 768], P('wide'), may hold values from -0.21875 to 0.21875
- cross_output: float32 [768, 768], P('wide'), may hold values from -0.875 to 0.875
- ffn_gate: float32 [768, 2048], P('wide'), may hold values from -0.21875 to 0.21875
- ffn_up: float32 [768, 2048], P('wide'), may hold values from -0.21875 to 0.21875
- ffn_down: float32 [2048, 768], P('wide'), may hold values from -0.125 to 0.125
- self_gain: float32 [768], P('wide'), may hold values from 0.5 to 1.5
- cross_gain: float32 [768], P('wide'), may hold values from 0.5 to 1.5
- ffn_gain: float32 [768], P('wide'), may hold values from 0.5 to 1.5
- bias_table: float32 [384], P('wide'), may hold values from -4 to 4
Outputs:
- layer_out: bfloat16 [24, 512, 768], P('wide', 'narrow')
- input_grad: bfloat16 [24, 512, 768], P('wide', 'narrow')
- enc_grad: bfloat16 [24, 4096, 768], P('wide', 'narrow')
- grad_self_query: float32 [768, 768], P('wide')
- grad_self_key: float32 [768, 768], P('wide')
- grad_self_value: float32 [768, 768], P('wide')
- grad_self_output: float32 [768, 768], P('wide')
- grad_cross_query: float32 [768, 768], P('wide')
- grad_cross_key: float32 [768, 768], P('wide')
- grad_cross_value: float32 [768, 768], P('wide')
- grad_cross_output: float32 [768, 768], P('wide')
- grad_ffn_gate: float32 [768, 2048], P('wide')
- grad_ffn_up: float32 [768, 2048], P('wide')
- grad_ffn_down: float32 [2048, 768], P('wide')
- grad_self_gain: float32 [768], P('wide')
- grad_cross_gain: float32 [768], P('wide')
- grad_ffn_gain: float32 [768], P('wide')
- grad_bias_table: float32 [384], P('wide')
The draws below stay inside these ranges and needn't reach their ends.
Inputs may be any that keep to these rules, and one draw needn't show every extreme that they name: `enc_len`: at least one example in every draw has exactly 4096 live encoder rows.
All inputs are finite; a program needn't handle non-finite values.
Results may differ from the reference program's by a relative error of at most 0.03.
The reference program's roundings to bfloat16 on the way count: a program that leaves them out, or rounds other values in their place, can miss the bound.
Values may be sent and summed in bfloat16 or wider, within the bound.
No kernel may reach another device: no remote copies, remote signals or barrier semaphores. Data moves between devices by JAX's collectives and lax.ppermute only.
A program may use at most 192 MiB of HBM per device.

```python
import math
import jax
import jax.numpy as jnp
from jax import lax

D = 768
HEADS = 12
HD = 64
FF = 2048
BUCKETS = 32
MAXDIST = 128
TGT = 512
ENC = 4096
EXAMPLES = 24


def draw_enc_len(key, part):
    short_key, pick_key = jax.random.split(jax.random.fold_in(key, 7))
    shorter = jax.random.randint(short_key, (EXAMPLES,), ENC // 8, 3 * ENC // 8 + 1)
    chosen = jax.random.randint(pick_key, (), 0, min(32, EXAMPLES))
    position = jnp.arange(EXAMPLES)
    return jnp.where(position % 32 == chosen, ENC, shorter).astype(jnp.int32)


def strengthened(entries, rng, source, target, parts, factor):
    def block_of(dim):
        return (jnp.arange(entries.shape[dim]) // (entries.shape[dim] // parts)).reshape((-1,) + (1,) * (entries.ndim - 1 - dim))

    first = jax.random.permutation(rng, parts)[block_of(target)]
    other_side = (block_of(target) + parts // 2) % parts
    return jnp.where((block_of(source) == first) | (block_of(source) == other_side), factor * entries, entries)


def level_of(key, dims, pieces, least, high):
    level, own = 1.0, jax.random.fold_in(key, 6)
    for axis_at, blocks in pieces:
        heights = jnp.exp(jax.random.uniform(jax.random.fold_in(own, axis_at), (blocks,), jnp.float32, least / len(pieces), high / len(pieces)))
        level = level * jnp.repeat(heights, dims[axis_at] // blocks).reshape([-1 if axis == axis_at else 1 for axis in range(len(dims))])
    return level


def centred(stream_key, dims, deviation, reach, shards=(), held_as=jnp.bfloat16):
    result = jax.random.normal(stream_key, dims, jnp.float32) * deviation
    if len(shards) > 0:
        result = level_of(stream_key, dims, shards, -0.22, 0.18) * result
    return jnp.clip(result, min=-reach, max=reach).astype(held_as)


def gaussian_with(own_key, dims, deviation, bound, shards, heavy, kind=jnp.bfloat16):
    entries = deviation * jax.random.normal(own_key, dims, jnp.float32)
    if shards:
        entries = entries * level_of(own_key, dims, shards, -0.22, 0.18)
    return jnp.clip(strengthened(entries, jax.random.fold_in(own_key, 3), *heavy), -bound, bound).astype(kind)


def setup_inputs(seed: int = 0) -> dict:
    arg_keys = jax.random.split(jax.random.key(seed), 20)
    return {
        "dec_input": gaussian_with(arg_keys[0], (EXAMPLES, TGT, D), 1.0, 6.0, ((0, 8), (1, 4)), (0, 2, 8, 2.0)),
        "enc_out": centred(arg_keys[1], (EXAMPLES, ENC, D), 1.0, 6.0, ((0, 8), (1, 4))),
        "enc_len": draw_enc_len(jax.random.fold_in(arg_keys[19], 71), 0),
        "cotangent": centred(arg_keys[3], (EXAMPLES, TGT, D), 1.0, 6.0, ((0, 8), (1, 4))),
        "self_query": centred(arg_keys[4], (D, D), (D * HD // 4) ** -0.5, 0.0546875, ((0, 8),), jnp.float32),
        "self_key": centred(arg_keys[5], (D, D), D ** -0.5, 0.21875, ((0, 8),), jnp.float32),
        "self_value": centred(arg_keys[6], (D, D), D ** -0.5, 0.21875, ((0, 8),), jnp.float32),
        "self_output": centred(arg_keys[7], (D, D), (D // 4) ** -0.5, 0.4375, ((0, 8),), jnp.float32),
        "cross_query": centred(arg_keys[8], (D, D), (D * HD // 4) ** -0.5, 0.0546875, ((0, 8),), jnp.float32),
        "cross_key": centred(arg_keys[9], (D, D), D ** -0.5, 0.21875, ((0, 8),), jnp.float32),
        "cross_value": centred(arg_keys[10], (D, D), D ** -0.5, 0.21875, ((0, 8),), jnp.float32),
        "cross_output": centred(arg_keys[11], (D, D), (D // 16) ** -0.5, 0.875, ((0, 8),), jnp.float32),
        "ffn_gate": centred(arg_keys[12], (D, FF), D ** -0.5, 0.21875, ((0, 8),), jnp.float32),
        "ffn_up": centred(arg_keys[13], (D, FF), D ** -0.5, 0.21875, ((0, 8),), jnp.float32),
        "ffn_down": centred(arg_keys[14], (FF, D), FF ** -0.5, 0.125, ((0, 8),), jnp.float32),
        "self_gain": jnp.clip(1.0 + 0.1 * jax.random.normal(arg_keys[15], (D,), jnp.float32), 0.5, 1.5),
        "cross_gain": jnp.clip(1.0 + 0.1 * jax.random.normal(arg_keys[16], (D,), jnp.float32), 0.5, 1.5),
        "ffn_gain": jnp.clip(1.0 + 0.1 * jax.random.normal(arg_keys[17], (D,), jnp.float32), 0.5, 1.5),
        "bias_table": centred(arg_keys[18], (BUCKETS * HEADS,), 1.0, 4.0, ((0, 8),), jnp.float32),
    }


@jax.custom_vjp
def low(v):
    return lax.optimization_barrier(v.astype(jnp.bfloat16)).astype(jnp.float32)

@jax.custom_vjp
def low_back(v):
    return v

def low_keep(v):
    return (low(v), None)

def low_pass(kept, grad):
    return (grad,)

def back_keep(v):
    return (v, None)

def back_low(kept, grad):
    return (low(grad),)
low.defvjp(low_keep, low_pass)
low_back.defvjp(back_keep, back_low)
NEG_FILL = -1000000000.0
NORM_EPS = 1e-06
FULL_ACCURACY = lax.Precision.HIGHEST

def bucket_edges():
    exact = BUCKETS // 2
    edges = []
    for target in range(exact + 1, BUCKETS):
        for distance in range(exact, MAXDIST + 1):
            scaled = math.log(distance / exact) / math.log(MAXDIST / exact) * (BUCKETS - exact)
            grown = min(exact + math.floor(scaled), BUCKETS - 1)
            if grown >= target:
                edges.append(distance)
                break
    return edges

def bucket_of(distance):
    found = jnp.minimum(distance, BUCKETS // 2)
    for edge in bucket_edges():
        found = found + (distance >= edge).astype(found.dtype)
    return found

def root_norm(values, gain):
    return values * lax.rsqrt(lax.optimization_barrier(jnp.mean(values * values, axis=-1, keepdims=True)) + NORM_EPS) * gain

def matmul(left, right):
    return jnp.dot(left, right, precision=FULL_ACCURACY, preferred_element_type=jnp.float32)

def contract(form, left, right):
    return jnp.einsum(form, left, right, precision=FULL_ACCURACY, preferred_element_type=jnp.float32)

def attend(query_heads_all, key_heads_all, values, relative_position_bias, allowed):
    attention_scores = low_back(contract('qhd,khd->hqk', query_heads_all, key_heads_all)) + relative_position_bias
    attention_scores = jnp.where(allowed, attention_scores, NEG_FILL)
    attention_weight = low(jax.nn.softmax(attention_scores, axis=-1))
    return contract('hqk,khd->qhd', attention_weight, values)

def example_layer(rows, memory, length, params):
    self_query, self_key, self_value, self_output, cross_query, cross_key, cross_value, cross_output, ffn_gate, ffn_up, ffn_down, self_gain, cross_gain, ffn_gain, bias_table = params
    normed = low(root_norm(rows, self_gain))
    query_heads_all = low(low_back(matmul(normed, self_query))).reshape(TGT, HEADS, HD)
    key_heads_all = low(low_back(matmul(normed, self_key))).reshape(TGT, HEADS, HD)
    values = low(low_back(matmul(normed, self_value))).reshape(TGT, HEADS, HD)
    position = jnp.arange(TGT)
    distance = jnp.maximum(position[:, None] - position[None, :], 0)
    bucket_bias_lookup = bias_table.reshape(BUCKETS, HEADS)
    relative_position_bias = jnp.transpose(bucket_bias_lookup[bucket_of(distance)], (2, 0, 1))
    causal = (position[None, :] <= position[:, None])[None]
    mixed = low(low_back(attend(query_heads_all, key_heads_all, values, relative_position_bias, causal).reshape(TGT, D)))
    first = rows + low_back(matmul(mixed, self_output))
    normed_two = low(root_norm(first, cross_gain))
    cross_queries = low(low_back(matmul(normed_two, cross_query))).reshape(TGT, HEADS, HD)
    memory_keys = low(low_back(matmul(memory, cross_key))).reshape(ENC, HEADS, HD)
    memory_values = low(low_back(matmul(memory, cross_value))).reshape(ENC, HEADS, HD)
    live = (jnp.arange(ENC) < length)[None, None, :]
    mixed_two = low(low_back(attend(cross_queries, memory_keys, memory_values, 0.0, live).reshape(TGT, D)))
    second = first + low_back(matmul(mixed_two, cross_output))
    normed_three = low(root_norm(second, ffn_gain))
    gate_pre = low_back(matmul(normed_three, ffn_gate))
    up_pre = low_back(matmul(normed_three, ffn_up))
    hidden = low(jax.nn.gelu(gate_pre, approximate=True) * up_pre)
    return second + low_back(matmul(hidden, ffn_down))

def reference(dec_input, enc_out, enc_len, cotangent, self_query, self_key, self_value, self_output, cross_query, cross_key, cross_value, cross_output, ffn_gate, ffn_up, ffn_down, self_gain, cross_gain, ffn_gain, bias_table):

    def forward(rows_all, memory_all, *masters):
        params = tuple((low(master) for master in masters))

        def step(carry, item):
            rows, memory, length = item
            return (carry, jax.checkpoint(example_layer)(rows, memory, length, params))
        unused, outputs = lax.scan(step, 0, (rows_all, memory_all, enc_len))
        return outputs
    outputs, pull = jax.vjp(forward, dec_input.astype(jnp.float32), enc_out.astype(jnp.float32), self_query, self_key, self_value, self_output, cross_query, cross_key, cross_value, cross_output, ffn_gate, ffn_up, ffn_down, self_gain, cross_gain, ffn_gain, bias_table)
    grads = pull(cotangent.astype(jnp.float32))
    return (outputs.astype(jnp.bfloat16), grads[0].astype(jnp.bfloat16), grads[1].astype(jnp.bfloat16), grads[2], grads[3], grads[4], grads[5], grads[6], grads[7], grads[8], grads[9], grads[10], grads[11], grads[12], grads[13], grads[14], grads[15], grads[16])
```

```python
import functools
import math

import jax
import jax.numpy as jnp
import numpy as np
from jax import lax
from jax.experimental import pallas as pl
from jax.experimental.pallas import tpu as pltpu
from jax.sharding import PartitionSpec as P

HD = 64
BUCKETS = 32
MAXDIST = 128
NORM_EPS = 1e-06
MASKED = -1e30
LANES = 128
ROW_BLOCK = 512
FULL_ACCURACY = lax.Precision.HIGHEST
F32 = jnp.float32
BF16 = jnp.bfloat16

PAIR = ((0, 1), (1, 0), (2, 3), (3, 2))
ACROSS = ((0, 2), (2, 0), (1, 3), (3, 1))


def bucket_table(length):
    exact = BUCKETS // 2
    hot = np.zeros((BUCKETS, length), np.float32)
    for distance in range(length):
        bucket = distance
        if distance >= exact:
            scaled = math.log(distance / exact) / math.log(MAXDIST / exact) * (BUCKETS - exact)
            bucket = min(exact + math.floor(scaled), BUCKETS - 1)
        hot[bucket, distance] = 1.0
    return hot


def dot(left, right, contract=(1, 0)):
    return lax.dot_general(
        left, right, (((contract[0],), (contract[1],)), ((), ())), preferred_element_type=F32
    )


def root_norm(values, gain):
    return values * lax.rsqrt(jnp.mean(values * values, axis=-1, keepdims=True) + NORM_EPS) * gain


def pair_swap(value):
    return lax.ppermute(value, "narrow", PAIR)


def across_swap(value):
    return lax.ppermute(value, "narrow", ACROSS)


def in_order(flag, mine, other):
    first = flag == 0
    return jnp.where(first, mine, other), jnp.where(first, other, mine)


def narrow_gather(value, axis, row, core):
    low, high = in_order(row, value, across_swap(value))
    column = jnp.stack([low, high], axis)
    low, high = in_order(core, column, pair_swap(column))
    full = jnp.stack([low, high], axis + 1)
    shape = list(value.shape)
    shape[axis] *= 4
    return full.reshape(shape)


def part_of(value, index, parts, axis):
    size = value.shape[axis] // parts
    return lax.dynamic_slice_in_dim(value, index * size, size, axis)


def transpose_chunks(chunks_ref, out_ref):
    for i in range(chunks_ref.shape[0]):
        out_ref[LANES * i : LANES * (i + 1), :] = chunks_ref[i].T


def position_bias(vec_ref, bias_ref):
    heads, size, _ = bias_ref.shape
    key = lax.broadcasted_iota(jnp.int32, (size, size), 0)
    query = lax.broadcasted_iota(jnp.int32, (size, size), 1)
    for h in range(heads):
        rows = jnp.broadcast_to(vec_ref[h : h + 1, :], (size, size))
        rolled = pltpu.roll(rows, 0, 1, stride=1, stride_axis=0)
        bias_ref[h] = jnp.where(key <= query, rolled, MASKED)


def self_forward_kernel(
    x_ref, gain_ref, chunks_ref, vec_ref, n1_ref, qkv_ref, out_ref, lse_ref, wt_ref, bias_ref
):
    heads = bias_ref.shape[0]
    width = heads * HD

    @pl.when(pl.program_id(0) == 0)
    def _():
        transpose_chunks(chunks_ref, wt_ref)
        position_bias(vec_ref, bias_ref)

    normed = root_norm(x_ref[0].astype(F32), gain_ref[...]).astype(BF16)
    n1_ref[0] = normed
    qkv = dot(wt_ref[...], normed, (1, 1)).astype(BF16)
    qkv_ref[0] = qkv
    lse_ref[...] = jnp.zeros_like(lse_ref)
    for h in range(heads):
        q, k, v = (qkv[width * part + HD * h : width * part + HD * (h + 1)] for part in range(3))
        s = dot(k, q, (0, 0)) + bias_ref[h]
        peak = jnp.max(s, axis=0, keepdims=True)
        raised = jnp.exp(s - peak)
        total = jnp.sum(raised, axis=0, keepdims=True)
        weight = (raised * (1.0 / total)).astype(BF16)
        out_ref[0, HD * h : HD * (h + 1), :] = dot(v, weight).astype(BF16)
        lse_ref[0, h : h + 1, :] = peak + jnp.log(total)


def self_forward(x, gain, chunks, vec, heads):
    examples, length, model = x.shape
    feats = chunks.shape[0] * LANES
    whole = lambda *shape: pl.BlockSpec(shape, lambda e: (0,) * len(shape))
    per = lambda *shape: pl.BlockSpec((1, *shape), lambda e: (e, 0, 0))
    return pl.pallas_call(
        self_forward_kernel,
        grid=(examples,),
        in_specs=[
            per(length, model),
            whole(1, model),
            whole(*chunks.shape),
            whole(*vec.shape),
        ],
        out_specs=[
            per(length, model),
            per(feats, length),
            per(heads * HD, length),
            per(8, length),
        ],
        out_shape=[
            jax.ShapeDtypeStruct((examples, length, model), BF16),
            jax.ShapeDtypeStruct((examples, feats, length), BF16),
            jax.ShapeDtypeStruct((examples, heads * HD, length), BF16),
            jax.ShapeDtypeStruct((examples, 8, length), F32),
        ],
        scratch_shapes=[
            pltpu.VMEM((feats, model), BF16),
            pltpu.VMEM((heads, length, length), F32),
        ],
        compiler_params=pltpu.CompilerParams(vmem_limit_bytes=48 << 20),
        name="self_forward",
    )(x, gain, chunks, vec)


def self_backward_kernel(
    n1_ref, qkv_ref, do_ref, lse_ref, chunks_ref, vec_ref,
    dn_ref, gw_ref, dvec_ref,
    wt_ref, bias_ref, dsum_ref, dqkv_ref,
):
    heads, size, _ = bias_ref.shape
    width = heads * HD
    e = pl.program_id(0)

    @pl.when(e == 0)
    def _():
        transpose_chunks(chunks_ref, wt_ref)
        position_bias(vec_ref, bias_ref)
        dsum_ref[...] = jnp.zeros_like(dsum_ref)
        gw_ref[...] = jnp.zeros_like(gw_ref)
        dqkv_ref[...] = jnp.zeros_like(dqkv_ref)

    for h in range(heads):
        q, k, v = (
            qkv_ref[0, width * part + HD * h : width * part + HD * (h + 1), :] for part in range(3)
        )
        do = do_ref[0, HD * h : HD * (h + 1), :]
        s = dot(k, q, (0, 0)) + bias_ref[h]
        p = jnp.exp(s - lse_ref[0, h : h + 1, :])
        dp = dot(v, do, (0, 0))
        inner = jnp.sum(p * dp, axis=0, keepdims=True)
        ds = p * (dp - inner)
        dsum_ref[h] += ds
        ds = ds.astype(BF16)
        at = lambda part: slice(width * part + HD * h, width * part + HD * (h + 1))
        dqkv_ref[:, at(0)] = dot(k, ds).T.astype(BF16)
        dqkv_ref[:, at(1)] = dot(ds, q, (1, 1)).astype(BF16)
        dqkv_ref[:, at(2)] = dot(p.astype(BF16), do, (1, 1)).astype(BF16)
    dqkv = dqkv_ref[...]
    dn_ref[0] = dot(dqkv, wt_ref[...])
    gw_ref[...] += dot(n1_ref[0], dqkv, (0, 0))

    @pl.when(e == pl.num_programs(0) - 1)
    def _():
        dvec_ref[...] = jnp.zeros_like(dvec_ref)
        for h in range(heads):
            back, count = dsum_ref[h], size
            while count > 8:
                count //= 2
                back = back[:count] + pltpu.roll(back[count:], size - count, 1)
            total = back[:1]
            for r in range(1, count):
                total = total + pltpu.roll(back[r : r + 1], size - r, 1)
            dvec_ref[h : h + 1, :] = total


def self_backward(n1, qkv, do, lse, chunks, vec, heads):
    examples, length, model = n1.shape
    feats = chunks.shape[0] * LANES
    whole = lambda *shape: pl.BlockSpec(shape, lambda e: (0,) * len(shape))
    per = lambda *shape: pl.BlockSpec((1, *shape), lambda e: (e, 0, 0))
    return pl.pallas_call(
        self_backward_kernel,
        grid=(examples,),
        in_specs=[
            per(length, model),
            per(feats, length),
            per(heads * HD, length),
            per(8, length),
            whole(*chunks.shape),
            whole(*vec.shape),
        ],
        out_specs=[per(length, model), whole(model, feats), whole(8, length)],
        out_shape=[
            jax.ShapeDtypeStruct((examples, length, model), F32),
            jax.ShapeDtypeStruct((model, feats), F32),
            jax.ShapeDtypeStruct((8, length), F32),
        ],
        scratch_shapes=[
            pltpu.VMEM((feats, model), BF16),
            pltpu.VMEM((heads, length, length), F32),
            pltpu.VMEM((heads, length, length), F32),
            pltpu.VMEM((length, feats), BF16),
        ],
        compiler_params=pltpu.CompilerParams(vmem_limit_bytes=48 << 20),
        name="self_backward",
    )(n1, qkv, do, lse, chunks, vec)


def memory_project_kernel(live_ref, own_ref, other_ref, chunks_ref, k_ref, v_ref, wt_ref):
    e, j = pl.program_id(0), pl.program_id(1)
    blocks = pl.num_programs(1)
    half = wt_ref.shape[0] // 2

    @pl.when((e == 0) & (j == 0))
    def _():
        transpose_chunks(chunks_ref, wt_ref)

    def project(rows):
        both = dot(wt_ref[...], rows, (1, 1)).astype(BF16)
        k_ref[0] = both[:half]
        v_ref[0] = both[half:]

    @pl.when((live_ref[e, j] > 0) & (j < blocks // 2))
    def _():
        project(own_ref[0])

    @pl.when((live_ref[e, j] > 0) & (j >= blocks // 2))
    def _():
        project(other_ref[0])


def memory_project(live, own, other, chunks):
    examples, rows, model = own.shape
    half = rows // ROW_BLOCK
    feats = chunks.shape[0] * LANES // 2
    row_spec = lambda first: pl.BlockSpec(
        (1, ROW_BLOCK, model), lambda e, j, live: (e, jnp.clip(j - first, 0, half - 1), 0)
    )
    out_spec = pl.BlockSpec((1, feats, ROW_BLOCK), lambda e, j, live: (e, 0, j))
    out = jax.ShapeDtypeStruct((examples, feats, 2 * rows), BF16)
    return pl.pallas_call(
        memory_project_kernel,
        grid_spec=pltpu.PrefetchScalarGridSpec(
            num_scalar_prefetch=1,
            grid=(examples, 2 * half),
            in_specs=[
                row_spec(0),
                row_spec(half),
                pl.BlockSpec(chunks.shape, lambda e, j, live: (0, 0, 0)),
            ],
            out_specs=[out_spec, out_spec],
            scratch_shapes=[pltpu.VMEM((2 * feats, model), BF16)],
        ),
        out_shape=[out, out],
        compiler_params=pltpu.CompilerParams(vmem_limit_bytes=48 << 20),
        name="memory_project",
    )(live, own, other, chunks)


def cross_forward_kernel(live_ref, q_ref, k_ref, v_ref, o_ref, lse_ref, peak_ref, total_ref, acc_ref):
    e, j = pl.program_id(0), pl.program_id(1)
    heads = acc_ref.shape[0] // HD
    live = live_ref[e, j]

    @pl.when(j == 0)
    def _():
        peak_ref[...] = jnp.full_like(peak_ref, MASKED)
        total_ref[...] = jnp.zeros_like(total_ref)
        acc_ref[...] = jnp.zeros_like(acc_ref)

    def block(partial):
        for h in range(heads):
            at = slice(HD * h, HD * (h + 1))
            s = dot(k_ref[0, at, :], q_ref[0, at, :], (0, 0))
            if partial:
                s = jnp.where(lax.broadcasted_iota(jnp.int32, s.shape, 0) < live, s, MASKED)
            before = peak_ref[h : h + 1, :]
            peak = jnp.maximum(before, jnp.max(s, axis=0, keepdims=True))
            p = jnp.exp(s - peak)
            shrink = jnp.exp(before - peak)
            peak_ref[h : h + 1, :] = peak
            total_ref[h : h + 1, :] = total_ref[h : h + 1, :] * shrink + jnp.sum(p, axis=0, keepdims=True)
            acc_ref[at, :] = acc_ref[at, :] * shrink + dot(v_ref[0, at, :], p.astype(BF16))

    @pl.when(live == ROW_BLOCK)
    def _():
        block(False)

    @pl.when((live > 0) & (live < ROW_BLOCK))
    def _():
        block(True)

    @pl.when(j == pl.num_programs(1) - 1)
    def _():
        total = total_ref[...]
        some = total > 0
        inverse = jnp.where(some, 1.0 / jnp.where(some, total, 1.0), 0.0)
        lse_ref[0] = jnp.where(some, peak_ref[...] + jnp.log(jnp.where(some, total, 1.0)), MASKED)
        for h in range(heads):
            at = slice(HD * h, HD * (h + 1))
            o_ref[0, at, :] = (acc_ref[at, :] * inverse[h : h + 1, :]).astype(o_ref.dtype)


def cross_forward(live, q, k, v):
    examples, feats, length = q.shape
    rows = k.shape[2]
    q_spec = pl.BlockSpec((1, feats, length), lambda e, j, live: (e, 0, 0))
    k_spec = pl.BlockSpec((1, feats, ROW_BLOCK), lambda e, j, live: (e, 0, j))
    l_spec = pl.BlockSpec((1, 8, length), lambda e, j, live: (e, 0, 0))
    return pl.pallas_call(
        cross_forward_kernel,
        grid_spec=pltpu.PrefetchScalarGridSpec(
            num_scalar_prefetch=1,
            grid=(examples, rows // ROW_BLOCK),
            in_specs=[q_spec, k_spec, k_spec],
            out_specs=[q_spec, l_spec],
            scratch_shapes=[
                pltpu.VMEM((8, length), F32),
                pltpu.VMEM((8, length), F32),
                pltpu.VMEM((feats, length), F32),
            ],
        ),
        out_shape=[
            jax.ShapeDtypeStruct((examples, feats, length), F32),
            jax.ShapeDtypeStruct((examples, 8, length), F32),
        ],
        compiler_params=pltpu.CompilerParams(vmem_limit_bytes=48 << 20),
        name="cross_forward",
    )(live, q, k, v)


def cross_backward_kernel(
    live_ref, q_ref, do_ref, lse_ref, inner_ref, k_ref, v_ref, dq_ref, dk_ref, dv_ref, acc_ref
):
    e, j = pl.program_id(0), pl.program_id(1)
    heads = acc_ref.shape[0] // HD
    live = live_ref[e, j]

    @pl.when(j == 0)
    def _():
        acc_ref[...] = jnp.zeros_like(acc_ref)

    def block(partial):
        for h in range(heads):
            at = slice(HD * h, HD * (h + 1))
            q, do, k, v = q_ref[0, at, :], do_ref[0, at, :], k_ref[0, at, :], v_ref[0, at, :]
            s = dot(k, q, (0, 0))
            p = jnp.exp(s - lse_ref[0, h : h + 1, :])
            if partial:
                p = jnp.where(lax.broadcasted_iota(jnp.int32, s.shape, 0) < live, p, 0.0)
            dp = dot(v, do, (0, 0))
            ds = (p * (dp - inner_ref[0, h : h + 1, :])).astype(BF16)
            acc_ref[at, :] += dot(k, ds)
            dk_ref[0, :, at] = dot(ds, q, (1, 1)).astype(BF16)
            dv_ref[0, :, at] = dot(p.astype(BF16), do, (1, 1)).astype(BF16)

    @pl.when(live == ROW_BLOCK)
    def _():
        block(False)

    @pl.when((live > 0) & (live < ROW_BLOCK))
    def _():
        block(True)

    @pl.when(j == pl.num_programs(1) - 1)
    def _():
        dq_ref[0] = acc_ref[...].T


def cross_backward(live, q, do, lse, inner, k, v):
    examples, feats, length = q.shape
    rows = k.shape[2]
    q_spec = pl.BlockSpec((1, feats, length), lambda e, j, live: (e, 0, 0))
    k_spec = pl.BlockSpec((1, feats, ROW_BLOCK), lambda e, j, live: (e, 0, j))
    l_spec = pl.BlockSpec((1, 8, length), lambda e, j, live: (e, 0, 0))
    d_spec = pl.BlockSpec((1, ROW_BLOCK, feats), lambda e, j, live: (e, j, 0))
    return pl.pallas_call(
        cross_backward_kernel,
        grid_spec=pltpu.PrefetchScalarGridSpec(
            num_scalar_prefetch=1,
            grid=(examples, rows // ROW_BLOCK),
            in_specs=[q_spec, q_spec, l_spec, l_spec, k_spec, k_spec],
            out_specs=[
                pl.BlockSpec((1, length, feats), lambda e, j, live: (e, 0, 0)),
                d_spec,
                d_spec,
            ],
            scratch_shapes=[pltpu.VMEM((feats, length), F32)],
        ),
        out_shape=[
            jax.ShapeDtypeStruct((examples, length, feats), F32),
            jax.ShapeDtypeStruct((examples, rows, feats), BF16),
            jax.ShapeDtypeStruct((examples, rows, feats), BF16),
        ],
        compiler_params=pltpu.CompilerParams(vmem_limit_bytes=48 << 20),
        name="cross_backward",
    )(live, q, do, lse, inner, k, v)


def memory_backward_kernel(live_ref, rows_ref, dk_ref, dv_ref, chunks_ref, *refs):
    *add_ref, out_ref, gk_ref, gv_ref, wt_ref = refs
    e, j = pl.program_id(0), pl.program_id(1)
    half = wt_ref.shape[0] // 2

    @pl.when((e == 0) & (j == 0))
    def _():
        transpose_chunks(chunks_ref, wt_ref)
        gk_ref[...] = jnp.zeros_like(gk_ref)
        gv_ref[...] = jnp.zeros_like(gv_ref)

    @pl.when(live_ref[e, j] > 0)
    def _():
        rows, dk, dv = rows_ref[0], dk_ref[0], dv_ref[0]
        gk_ref[...] += dot(rows, dk, (0, 0))
        gv_ref[...] += dot(rows, dv, (0, 0))
        back = dot(dk, wt_ref[:half]) + dot(dv, wt_ref[half:])
        if add_ref:
            back = back + add_ref[0][0].astype(F32)
        out_ref[0] = back.astype(BF16)

    @pl.when(live_ref[e, j] == 0)
    def _():
        out_ref[0] = jnp.zeros_like(out_ref[0])


def memory_backward(live, rows, dk, dv, first, chunks, add=None):
    examples, count, model = rows.shape
    feats = dk.shape[2]
    row_spec = pl.BlockSpec((1, ROW_BLOCK, model), lambda e, j, live: (e, j, 0))
    d_spec = pl.BlockSpec((1, ROW_BLOCK, feats), lambda e, j, live: (e, j + first, 0))
    g_spec = pl.BlockSpec((model, feats), lambda e, j, live: (0, 0))
    grad = jax.ShapeDtypeStruct((model, feats), F32)
    extra = () if add is None else (add,)
    return pl.pallas_call(
        memory_backward_kernel,
        grid_spec=pltpu.PrefetchScalarGridSpec(
            num_scalar_prefetch=1,
            grid=(examples, count // ROW_BLOCK),
            in_specs=[
                row_spec,
                d_spec,
                d_spec,
                pl.BlockSpec(chunks.shape, lambda e, j, live: (0, 0, 0)),
            ]
            + [row_spec] * len(extra),
            out_specs=[row_spec, g_spec, g_spec],
            scratch_shapes=[pltpu.VMEM((2 * feats, model), BF16)],
        ),
        out_shape=[jax.ShapeDtypeStruct(rows.shape, BF16), grad, grad],
        compiler_params=pltpu.CompilerParams(vmem_limit_bytes=48 << 20),
        name="memory_backward",
    )(live, rows, dk, dv, chunks, *extra)


def to_chunks(rows):
    count, width = rows.shape
    return jnp.transpose(rows.reshape(count, width // LANES, LANES), (1, 0, 2))


def from_chunks(chunks):
    count, rows, lanes = chunks.shape
    return jnp.transpose(chunks, (1, 0, 2)).reshape(rows, count * lanes)


def norm_pull(values, gain, grad):
    unused, pull = jax.vjp(root_norm, values, gain)
    return pull(grad)


def local(
    dec_input,
    enc_out,
    enc_len,
    cotangent,
    self_query,
    self_key,
    self_value,
    self_output,
    cross_query,
    cross_key,
    cross_value,
    cross_output,
    ffn_gate,
    ffn_up,
    ffn_down,
    self_gain,
    cross_gain,
    ffn_gain,
    bias_table,
):
    place = lax.axis_index("narrow")
    row, core = place // 2, place % 2
    wide = lax.axis_size("wide")
    examples, own, model = dec_input.shape
    length = 4 * own
    heads = model // HD
    own_heads = heads // 4
    memory_rows = enc_out.shape[1]
    share = self_query.shape[0]

    own_qkv = jnp.concatenate(
        [part_of(w.astype(BF16), place, 4, 1) for w in (self_query, self_key, self_value)], 1
    )
    own_qkv = jnp.pad(own_qkv, ((0, 0), (0, -own_qkv.shape[1] % LANES)))
    pair_qkv = [part_of(w.astype(BF16), core, 2, 1) for w in (cross_query, cross_key, cross_value)]
    small = jnp.stack([self_gain, cross_gain, ffn_gain, jnp.pad(bias_table, (0, share - bias_table.shape[0]))], 1)
    small = jnp.pad(small.astype(BF16), ((0, 0), (0, LANES - 4)))
    packed = [own_qkv, *pair_qkv, self_output.astype(BF16), cross_output.astype(BF16), small]
    counts = [p.shape[1] // LANES for p in packed]
    gathered = lax.all_gather(jnp.concatenate([to_chunks(p) for p in packed], 0), "wide", axis=1, tiled=True)
    bounds = np.cumsum([0, *counts])
    c_self, c_query, c_key, c_value, c_so, c_co, c_small = (
        gathered[a:b] for a, b in zip(bounds[:-1], bounds[1:])
    )
    c_memory = gathered[bounds[2] : bounds[4]]
    self_out_w, cross_out_w, cross_query_w = from_chunks(c_so), from_chunks(c_co), from_chunks(c_query)
    small_rows = c_small[0, :, :4].astype(F32).T
    gain_one, gain_two, gain_three = (small_rows[i : i + 1] for i in range(3))
    table = small_rows[3].reshape(wide, share)[:, : bias_table.shape[0]].reshape(BUCKETS, heads)

    both = ("wide", "narrow")
    quarter = lambda w: part_of(w.astype(BF16), place, 4, 0)
    gate_up = lax.all_gather(jnp.stack([quarter(ffn_gate), quarter(ffn_up)]), both, axis=1, tiled=True)
    gate_w, up_w = gate_up[0], gate_up[1]
    down_w = lax.all_gather(quarter(ffn_down), both, axis=0, tiled=True)

    enc_other = pair_swap(enc_out)
    starts = (place * memory_rows + np.arange(memory_rows // ROW_BLOCK) * ROW_BLOCK).astype(jnp.int32)
    other_starts = starts + (1 - 2 * core) * memory_rows
    block_starts = jnp.concatenate([starts, other_starts])
    live = jnp.clip(enc_len[:, None] - block_starts[None, :], 0, ROW_BLOCK)

    x_all = narrow_gather(dec_input, 1, row, core)
    hot = jnp.asarray(bucket_table(length))
    distance_bias = jnp.dot(table.T, hot, precision=FULL_ACCURACY)
    vec = jnp.pad(part_of(distance_bias, place, 4, 0), ((0, 8 - own_heads), (0, 0)))
    n1, qkv, self_o, self_lse = self_forward(x_all, gain_one, c_self, vec, own_heads)
    self_o_all = narrow_gather(self_o, 1, row, core)
    x1_all = x_all.astype(F32) + jnp.einsum("eft,fd->etd", self_o_all, self_out_w, preferred_element_type=F32)
    n2_all = root_norm(x1_all, gain_two[0]).astype(BF16)
    cross_q = jnp.einsum("df,etd->eft", cross_query_w, n2_all, preferred_element_type=F32).astype(BF16)

    keys, values = memory_project(live, enc_out, enc_other, c_memory)
    part_o, part_lse = cross_forward(live, cross_q, keys, values)
    other_lse = across_swap(part_lse)
    lse = jnp.logaddexp(part_lse, other_lse)
    feats = part_o.shape[1]

    def spread(per_head):
        pieces = per_head[:, : feats // HD, None, :]
        return jnp.broadcast_to(pieces, (examples, feats // HD, HD, per_head.shape[2])).reshape(
            examples, feats, per_head.shape[2]
        )

    sent = part_of(part_o, 1 - row, 2, 2).astype(BF16)
    came = across_swap(sent).astype(F32)
    kept = part_of(part_o, row, 2, 2)
    chip_lse = part_of(lse, row, 2, 2)
    own_weight = jnp.exp(part_of(part_lse, row, 2, 2) - chip_lse)
    other_weight = jnp.exp(part_of(other_lse, row, 2, 2) - chip_lse)
    chip_o = (kept * spread(own_weight) + came * spread(other_weight)).astype(BF16)
    low, high = in_order(core, part_of(chip_o, core, 2, 2), pair_swap(part_of(chip_o, 1 - core, 2, 2)))
    oc = jnp.concatenate([low, high], 1)

    x1 = part_of(x1_all, place, 4, 1)
    x2 = x1 + jnp.einsum("eft,fd->etd", oc, cross_out_w, preferred_element_type=F32)
    n3 = root_norm(x2, gain_three[0]).astype(BF16)
    project = lambda a, w: jnp.einsum("etd,df->etf", a, w, preferred_element_type=F32)
    project_back = lambda a, w: jnp.einsum("etf,df->etd", a, w, preferred_element_type=F32)
    weight_grad = lambda a, g: jnp.einsum("etd,etf->df", a, g, preferred_element_type=F32)
    gate_pre = project(n3, gate_w)
    up_pre = project(n3, up_w)
    gated = lambda a, u: jax.nn.gelu(a, approximate=True) * u
    hidden, gated_pull = jax.vjp(gated, gate_pre, up_pre)
    hidden = hidden.astype(BF16)
    layer_out = (x2 + project(hidden, down_w)).astype(BF16)
    dy = cotangent.astype(F32)
    grad_down = weight_grad(hidden, cotangent)
    da, du = gated_pull(project_back(cotangent, down_w))
    da, du = da.astype(BF16), du.astype(BF16)
    grad_gate = weight_grad(n3, da)
    grad_up = weight_grad(n3, du)
    dn3 = project_back(da, gate_w) + project_back(du, up_w)
    dx2, grad_gain_three = norm_pull(x2, gain_three[0], dn3)
    dx2 = dx2 + dy
    dx2r = dx2.astype(BF16)
    grad_cross_output = jnp.einsum("eft,etd->fd", oc, dx2r, preferred_element_type=F32)

    doc = jnp.einsum("fd,etd->eft", cross_out_w, dx2r, preferred_element_type=F32).astype(BF16)
    inner = jnp.sum(
        (doc.astype(F32) * oc.astype(F32)).reshape(examples, heads, HD, own), axis=2
    )

    def to_heads(value):
        low, high = in_order(core, part_of(value, core, 2, 1), pair_swap(part_of(value, 1 - core, 2, 1)))
        chip = jnp.concatenate([low, high], 2)
        low, high = in_order(row, chip, across_swap(chip))
        return jnp.concatenate([low, high], 2)

    doc_heads = to_heads(doc)
    inner_heads = jnp.pad(to_heads(inner), ((0, 0), (0, 8 - heads // 2), (0, 0)))
    part_dq, dk, dv = cross_backward(live, cross_q, doc_heads, lse, inner_heads, keys, values)
    half_blocks = memory_rows // ROW_BLOCK
    other_grad, gk_other, gv_other = memory_backward(
        live[:, half_blocks:], enc_other, dk, dv, half_blocks, c_memory
    )
    enc_grad, gk_own, gv_own = memory_backward(
        live[:, :half_blocks], enc_out, dk, dv, 0, c_memory, pair_swap(other_grad)
    )
    grad_cross_key, grad_cross_value = gk_own + gk_other, gv_own + gv_other
    grad_cross_query = jnp.einsum("etd,etf->df", n2_all, part_dq.astype(BF16), preferred_element_type=F32)
    chip_dq = part_of(part_dq, row, 2, 1) + across_swap(
        part_of(part_dq, 1 - row, 2, 1).astype(BF16)
    ).astype(F32)
    chip_dn2 = project_back(chip_dq.astype(BF16), cross_query_w)
    dn2 = part_of(chip_dn2, core, 2, 1) + pair_swap(
        part_of(chip_dn2, 1 - core, 2, 1).astype(BF16)
    ).astype(F32)
    dx1, grad_gain_two = norm_pull(x1, gain_two[0], dn2)
    dx1 = dx1 + dx2
    dx1r = dx1.astype(BF16)
    own_o = part_of(self_o_all, place, 4, 2)
    grad_self_output = jnp.einsum("eft,etd->fd", own_o, dx1r, preferred_element_type=F32)

    do = jnp.einsum("fd,etd->eft", self_out_w, dx1r, preferred_element_type=F32).astype(BF16)
    low, high = in_order(row, part_of(do, row, 2, 1), across_swap(part_of(do, 1 - row, 2, 1)))
    column = jnp.stack([low, high], 2)
    low, high = in_order(core, part_of(column, core, 2, 1), pair_swap(part_of(column, 1 - core, 2, 1)))
    do_heads = jnp.stack([low, high], 3).reshape(examples, own_heads * HD, length)
    part_dn1, grad_self, dvec = self_backward(n1, qkv, do_heads, self_lse, c_self, vec, own_heads)
    by_core = part_dn1.reshape(examples, 2, 2, own, model)
    column = part_of(by_core, core, 2, 2) + pair_swap(part_of(by_core, 1 - core, 2, 2).astype(BF16)).astype(F32)
    dn1 = part_of(column, row, 2, 1) + across_swap(part_of(column, 1 - row, 2, 1).astype(BF16)).astype(F32)
    dn1 = dn1.reshape(examples, own, model)
    grad_in, grad_gain_one = norm_pull(dec_input.astype(F32), gain_one[0], dn1)
    input_grad = (dx1 + grad_in).astype(BF16)

    own_table = jnp.dot(hot, dvec[:own_heads].T, precision=FULL_ACCURACY)
    grad_table = lax.dynamic_update_slice_in_dim(
        jnp.zeros((BUCKETS, heads), F32), own_table, place * own_heads, 1
    )
    table_rows = jnp.pad(
        grad_table.reshape(wide, bias_table.shape[0]), ((0, 0), (0, share - bias_table.shape[0]))
    ).reshape(-1)
    small = jnp.stack([grad_gain_one, grad_gain_two, grad_gain_three, table_rows], 1)
    small = jnp.pad(small, ((0, 0), (0, LANES - 4)))
    scatter = functools.partial(lax.psum_scatter, scatter_dimension=0, tiled=True)
    shared = [grad_gate, grad_up, grad_self_output, grad_cross_output, small]
    shared_sum = scatter(jnp.concatenate([g.astype(BF16) for g in shared], 1), both)
    down_sum = scatter(grad_down.astype(BF16), both)
    columns_sum = scatter(
        jnp.concatenate([g.astype(BF16) for g in (grad_self, grad_cross_query, grad_cross_key, grad_cross_value)], 1),
        "wide",
    )
    shared_sum = narrow_gather(shared_sum, 0, row, core).astype(F32)
    down_sum = narrow_gather(down_sum, 0, row, core).astype(F32)
    bounds = np.cumsum([0, *(g.shape[1] for g in shared)])
    gate_sum, up_sum, so_sum, co_sum, small_sum = (
        shared_sum[:, a:b] for a, b in zip(bounds[:-1], bounds[1:])
    )
    self_width = grad_self.shape[1]
    self_sum = narrow_gather(columns_sum[None, :, :self_width], 0, row, core)
    q_sum, k_sum, v_sum = (
        jnp.concatenate([self_sum[i, :, own_heads * HD * part : own_heads * HD * (part + 1)] for i in range(4)], 1)
        for part in range(3)
    )
    cross_sum = columns_sum[:, self_width:].astype(F32)
    cross_sum = (cross_sum + across_swap(columns_sum[:, self_width:]).astype(F32)).astype(BF16)
    low, high = in_order(core, cross_sum, pair_swap(cross_sum))
    cq_sum, ck_sum, cv_sum = (
        jnp.concatenate([part[:, feats * i : feats * (i + 1)] for part in (low, high)], 1) for i in range(3)
    )
    f = lambda a: a.astype(F32)
    return (
        layer_out,
        input_grad,
        enc_grad,
        f(q_sum),
        f(k_sum),
        f(v_sum),
        so_sum,
        f(cq_sum),
        f(ck_sum),
        f(cv_sum),
        co_sum,
        gate_sum,
        up_sum,
        down_sum,
        small_sum[:, 0],
        small_sum[:, 1],
        small_sum[:, 2],
        small_sum[: bias_table.shape[0], 3],
    )


def solution(mesh):
    rows = P("wide", "narrow", None)
    weight, vector = P("wide", None), P("wide")
    return jax.shard_map(
        local,
        mesh=mesh,
        in_specs=(rows, rows, vector, rows, *[weight] * 11, *[vector] * 4),
        out_specs=(rows, rows, rows, *[weight] * 11, *[vector] * 4),
        check_vma=False,
    )
```

```python
import functools
import math

import jax
import jax.numpy as jnp
import numpy as np
from jax import lax
from jax.experimental import pallas as pl
from jax.experimental.pallas import tpu as pltpu
from jax.sharding import PartitionSpec as P

HD = 64
BUCKETS = 32
MAXDIST = 128
NORM_EPS = 1e-06
MASKED = -1e30
LANES = 128
ROW_BLOCK = 512
PEAK_FLOPS = 1.15e15
FULL_ACCURACY = lax.Precision.HIGHEST
F32 = jnp.float32
BF16 = jnp.bfloat16

PAIR = ((0, 1), (1, 0), (2, 3), (3, 2))
ACROSS = ((0, 2), (2, 0), (1, 3), (3, 1))


def bucket_table(length):
    exact = BUCKETS // 2
    hot = np.zeros((BUCKETS, length), np.float32)
    for distance in range(length):
        bucket = distance
        if distance >= exact:
            scaled = math.log(distance / exact) / math.log(MAXDIST / exact) * (BUCKETS - exact)
            bucket = min(exact + math.floor(scaled), BUCKETS - 1)
        hot[bucket, distance] = 1.0
    return hot


def dot(left, right, contract=(1, 0)):
    return lax.dot_general(
        left, right, (((contract[0],), (contract[1],)), ((), ())), preferred_element_type=F32
    )


def root_norm(values, gain):
    return values * lax.rsqrt(jnp.mean(values * values, axis=-1, keepdims=True) + NORM_EPS) * gain


def pair_swap(value):
    return lax.ppermute(value, "narrow", PAIR)


def across_swap(value):
    return lax.ppermute(value, "narrow", ACROSS)


def in_order(flag, mine, other):
    first = flag == 0
    return jnp.where(first, mine, other), jnp.where(first, other, mine)


def narrow_gather(value, axis, row, core):
    low, high = in_order(row, value, across_swap(value))
    column = jnp.stack([low, high], axis)
    low, high = in_order(core, column, pair_swap(column))
    full = jnp.stack([low, high], axis + 1)
    shape = list(value.shape)
    shape[axis] *= 4
    return full.reshape(shape)


def plus(mine, came):
    return (mine.astype(F32) + came.astype(F32)).astype(mine.dtype)


def part_of(value, index, parts, axis):
    size = value.shape[axis] // parts
    return lax.dynamic_slice_in_dim(value, index * size, size, axis)


LINE = 4
BESIDE = tuple((i, i ^ 1) for i in range(2 * LINE))


def along(step):
    return [(2 * z + x, 2 * ((z + step) % LINE) + x) for z in range(LINE) for x in range(2)]


def by_planes():
    return lax.axis_size("wide") == 2 * LINE


def assemble_kernel(widths, order_ref, *refs):
    pieces, outs = refs[: 2 * LINE], refs[2 * LINE :]
    for i, piece in enumerate(pieces):
        at = 0
        for width, out in zip(widths, outs):
            out[order_ref[i]] = piece[:, at : at + width]
            at += width


def after(value, *others):
    return lax.optimization_barrier((value, *others))[0]


def wide_gather(block, widths, first=()):
    rows = block.shape[0]
    if not by_planes():
        full = lax.all_gather(block, "wide", axis=0, tiled=True)
        bounds = np.cumsum([0, *widths])
        return [full[:, a:b] for a, b in zip(bounds[:-1], bounds[1:])]
    z, x = lax.axis_index("wide") // 2, lax.axis_index("wide") % 2
    line = [block] + [lax.ppermute(block, "wide", along(step)) for step in range(1, LINE)]
    line = after(line, *first)
    pieces = line + [lax.ppermute(piece, "wide", BESIDE) for piece in line]
    places = (z - np.arange(LINE)) % LINE * 2
    order = jnp.concatenate([places + x, places + 1 - x]).astype(jnp.int32)
    outs = pl.pallas_call(
        functools.partial(assemble_kernel, widths),
        in_specs=[pl.BlockSpec(memory_space=pltpu.SMEM)] + [pl.BlockSpec(memory_space=pltpu.VMEM)] * len(pieces),
        out_specs=[pl.BlockSpec(memory_space=pltpu.VMEM)] * len(widths),
        out_shape=[jax.ShapeDtypeStruct((2 * LINE, rows, width), block.dtype) for width in widths],
        compiler_params=pltpu.CompilerParams(vmem_limit_bytes=16 << 20),
        name="assemble",
    )(order, *pieces)
    return [out.reshape(2 * LINE * rows, out.shape[2]) for out in outs]


def shared_gather(block, row, first=()):
    rows, width = block.shape
    (full,) = wide_gather(part_of(block, row, 2, 0), (width,), first)
    halves = full.reshape(-1, rows // 2, width)
    return jnp.stack(in_order(row, halves, across_swap(halves)), 1).reshape(-1, width)


def pick(value, index, axis):
    return lax.dynamic_index_in_dim(value, index, axis, keepdims=False)


def wide_scatter_x(blocks):
    if not by_planes():
        return blocks
    x = lax.axis_index("wide") % 2
    planes = blocks.reshape(LINE, 2, *blocks.shape[1:])
    return plus(pick(planes, x, 1), lax.ppermute(pick(planes, 1 - x, 1), "wide", BESIDE))


def wide_scatter_z(planes):
    if not by_planes():
        shape = planes.shape
        return lax.psum_scatter(
            planes.reshape(shape[0] * shape[1], *shape[2:]), "wide", scatter_dimension=0, tiled=True
        )
    z = lax.axis_index("wide") // 2
    total = pick(planes, z, 0).astype(F32)
    for step in range(1, LINE):
        sent = pick(planes, (z + step) % LINE, 0)
        total = total + lax.ppermute(sent, "wide", along(step)).astype(F32)
    return total.astype(planes.dtype)


def wide_scatter(blocks):
    return wide_scatter_z(wide_scatter_x(blocks))


def transpose_columns(weight_ref, out_ref):
    for i in range(0, weight_ref.shape[1], LANES):
        out_ref[i : i + LANES, :] = weight_ref[:, i : i + LANES].T


def cost(flops, moved):
    return pl.CostEstimate(flops=int(flops), bytes_accessed=int(moved), transcendentals=0)


def position_bias(vec_ref, bias_ref):
    heads, size, _ = bias_ref.shape
    key = lax.broadcasted_iota(jnp.int32, (size, size), 0)
    query = lax.broadcasted_iota(jnp.int32, (size, size), 1)
    for h in range(heads):
        rows = jnp.broadcast_to(vec_ref[h : h + 1, :], (size, size))
        rolled = pltpu.roll(rows, 0, 1, stride=1, stride_axis=0)
        bias_ref[h] = jnp.where(key <= query, rolled, MASKED)


def self_forward_kernel(
    x_ref, gain_ref, w_ref, vec_ref, n1_ref, qkv_ref, out_ref, lse_ref, wt_ref, bias_ref
):
    heads = bias_ref.shape[0]
    width = heads * HD

    @pl.when(pl.program_id(0) == 0)
    def _():
        transpose_columns(w_ref, wt_ref)
        position_bias(vec_ref, bias_ref)

    normed = root_norm(x_ref[0].astype(F32), gain_ref[...]).astype(BF16)
    n1_ref[0] = normed
    qkv = dot(wt_ref[...], normed, (1, 1)).astype(BF16)
    qkv_ref[0] = qkv
    lse_ref[...] = jnp.zeros_like(lse_ref)
    for h in range(heads):
        q, k, v = (qkv[width * part + HD * h : width * part + HD * (h + 1)] for part in range(3))
        s = dot(k, q, (0, 0)) + bias_ref[h]
        peak = jnp.max(s, axis=0, keepdims=True)
        raised = jnp.exp(s - peak)
        total = jnp.sum(raised, axis=0, keepdims=True)
        weight = (raised * (1.0 / total)).astype(BF16)
        out_ref[0, HD * h : HD * (h + 1), :] = dot(v, weight).astype(BF16)
        lse_ref[0, h : h + 1, :] = peak + jnp.log(total)


def self_forward(x, gain, weight, vec, heads):
    examples, length, model = x.shape
    feats = weight.shape[1]
    whole = lambda *shape: pl.BlockSpec(shape, lambda e: (0,) * len(shape))
    per = lambda *shape: pl.BlockSpec((1, *shape), lambda e: (e, 0, 0))
    return pl.pallas_call(
        self_forward_kernel,
        grid=(examples,),
        in_specs=[
            per(length, model),
            whole(1, model),
            whole(*weight.shape),
            whole(*vec.shape),
        ],
        out_specs=[
            per(length, model),
            per(feats, length),
            per(heads * HD, length),
            per(8, length),
            whole(feats, model),
        ],
        out_shape=[
            jax.ShapeDtypeStruct((examples, length, model), BF16),
            jax.ShapeDtypeStruct((examples, feats, length), BF16),
            jax.ShapeDtypeStruct((examples, heads * HD, length), BF16),
            jax.ShapeDtypeStruct((examples, 8, length), F32),
            jax.ShapeDtypeStruct((feats, model), BF16),
        ],
        scratch_shapes=[pltpu.VMEM((heads, length, length), F32)],
        compiler_params=pltpu.CompilerParams(vmem_limit_bytes=48 << 20),
        cost_estimate=cost(9e-6 * PEAK_FLOPS, 8e6),
        name="self_forward",
    )(x, gain, weight, vec)


def self_backward_kernel(
    n1_ref, qkv_ref, do_ref, lse_ref, wt_ref, vec_ref,
    dn_ref, gw_ref, dvec_ref,
    bias_ref, dsum_ref, dqkv_ref,
):
    heads, size, _ = bias_ref.shape
    width = heads * HD
    e = pl.program_id(0)

    @pl.when(e == 0)
    def _():
        position_bias(vec_ref, bias_ref)
        dsum_ref[...] = jnp.zeros_like(dsum_ref)
        gw_ref[...] = jnp.zeros_like(gw_ref)
        dqkv_ref[...] = jnp.zeros_like(dqkv_ref)

    for h in range(heads):
        q, k, v = (
            qkv_ref[0, width * part + HD * h : width * part + HD * (h + 1), :] for part in range(3)
        )
        do = do_ref[0, HD * h : HD * (h + 1), :]
        s = dot(k, q, (0, 0)) + bias_ref[h]
        p = jnp.exp(s - lse_ref[0, h : h + 1, :])
        dp = dot(v, do, (0, 0))
        inner = jnp.sum(p * dp, axis=0, keepdims=True)
        ds = p * (dp - inner)
        dsum_ref[h] += ds
        ds = ds.astype(BF16)
        at = lambda part: slice(width * part + HD * h, width * part + HD * (h + 1))
        dqkv_ref[:, at(0)] = dot(k, ds).T.astype(BF16)
        dqkv_ref[:, at(1)] = dot(ds, q, (1, 1)).astype(BF16)
        dqkv_ref[:, at(2)] = dot(p.astype(BF16), do, (1, 1)).astype(BF16)
    dqkv = dqkv_ref[...]
    dn_ref[0] = dot(dqkv, wt_ref[...])
    gw_ref[...] += dot(n1_ref[0], dqkv, (0, 0))

    @pl.when(e == pl.num_programs(0) - 1)
    def _():
        dvec_ref[...] = jnp.zeros_like(dvec_ref)
        for h in range(heads):
            back, count = dsum_ref[h], size
            while count > 8:
                count //= 2
                back = back[:count] + pltpu.roll(back[count:], size - count, 1)
            total = back[:1]
            for r in range(1, count):
                total = total + pltpu.roll(back[r : r + 1], size - r, 1)
            dvec_ref[h : h + 1, :] = total


def self_backward(n1, qkv, do, lse, wt, vec, heads):
    examples, length, model = n1.shape
    feats = wt.shape[0]
    whole = lambda *shape: pl.BlockSpec(shape, lambda e: (0,) * len(shape))
    per = lambda *shape: pl.BlockSpec((1, *shape), lambda e: (e, 0, 0))
    return pl.pallas_call(
        self_backward_kernel,
        grid=(examples,),
        in_specs=[
            per(length, model),
            per(feats, length),
            per(heads * HD, length),
            per(8, length),
            whole(*wt.shape),
            whole(*vec.shape),
        ],
        out_specs=[per(length, model), whole(model, feats), whole(8, length)],
        out_shape=[
            jax.ShapeDtypeStruct((examples, length, model), F32),
            jax.ShapeDtypeStruct((model, feats), F32),
            jax.ShapeDtypeStruct((8, length), F32),
        ],
        scratch_shapes=[
            pltpu.VMEM((heads, length, length), F32),
            pltpu.VMEM((heads, length, length), F32),
            pltpu.VMEM((length, feats), BF16),
        ],
        compiler_params=pltpu.CompilerParams(vmem_limit_bytes=48 << 20),
        cost_estimate=cost(16e-6 * PEAK_FLOPS, 12e6),
        name="self_backward",
    )(n1, qkv, do, lse, wt, vec)


def work_list(live):
    examples, blocks = live.shape
    flat = live.reshape(-1)
    index = jnp.arange(flat.shape[0], dtype=jnp.int32)
    block = index % blocks
    visit = (flat > 0) | (block == 0)
    before = jnp.sum(jnp.where(visit[None, :] & (index[None, :] < index[:, None]), 1, 0), axis=1)
    ends = visit & ~jnp.any(
        visit[None, :] & (index[None, :] > index[:, None]) & (index[None, :] // blocks == index[:, None] // blocks), axis=1
    )
    chosen = (before[None, :] == index[:, None]) & visit[None, :]
    take = lambda values: jnp.sum(jnp.where(chosen, values[None, :], 0), axis=1)
    final = jnp.max(jnp.where(visit, index, 0))
    found = jnp.any(chosen, axis=1)
    at = jnp.where(found, take(index), final)
    rows = [at // blocks, at % blocks, take(flat), found & (at % blocks == 0), take(ends.astype(jnp.int32))]
    return jnp.stack([r.astype(jnp.int32) for r in rows])


def memory_project_kernel(work_ref, own_ref, other_ref, w_ref, k_ref, v_ref, wt_ref):
    i = pl.program_id(0)
    block, live = work_ref[1, i], work_ref[2, i]
    half = wt_ref.shape[0] // 2
    own_blocks = 2

    @pl.when(i == 0)
    def _():
        transpose_columns(w_ref, wt_ref)

    def project(rows):
        both = dot(wt_ref[...], rows, (1, 1)).astype(BF16)
        k_ref[0] = both[:half]
        v_ref[0] = both[half:]

    @pl.when((live > 0) & (block < own_blocks))
    def _():
        project(own_ref[0])

    @pl.when((live > 0) & (block >= own_blocks))
    def _():
        project(other_ref[0])


def memory_project(work, own, other, weight):
    examples, rows, model = own.shape
    half = rows // ROW_BLOCK
    feats = weight.shape[1] // 2
    row_spec = lambda first: pl.BlockSpec(
        (1, ROW_BLOCK, model), lambda i, work: (work[0, i], jnp.clip(work[1, i] - first, 0, half - 1), 0)
    )
    out_spec = pl.BlockSpec((1, feats, ROW_BLOCK), lambda i, work: (work[0, i], 0, work[1, i]))
    out = jax.ShapeDtypeStruct((examples, feats, 2 * rows), BF16)
    w_spec = lambda *shape: pl.BlockSpec(shape, lambda i, work: (0, 0))
    return pl.pallas_call(
        memory_project_kernel,
        grid_spec=pltpu.PrefetchScalarGridSpec(
            num_scalar_prefetch=1,
            grid=(work.shape[1],),
            in_specs=[row_spec(0), row_spec(half), w_spec(*weight.shape)],
            out_specs=[out_spec, out_spec, w_spec(2 * feats, model)],
        ),
        out_shape=[out, out, jax.ShapeDtypeStruct((2 * feats, model), BF16)],
        compiler_params=pltpu.CompilerParams(vmem_limit_bytes=48 << 20),
        cost_estimate=cost(12e-6 * PEAK_FLOPS, 12e6),
        name="memory_project",
    )(work, own, other, weight)


def cross_forward_kernel(work_ref, q_ref, k_ref, v_ref, o_ref, lse_ref, peak_ref, total_ref, acc_ref):
    i = pl.program_id(0)
    heads = acc_ref.shape[0] // HD
    live = work_ref[2, i]

    @pl.when(work_ref[3, i] == 1)
    def _():
        peak_ref[...] = jnp.full_like(peak_ref, MASKED)
        total_ref[...] = jnp.zeros_like(total_ref)
        acc_ref[...] = jnp.zeros_like(acc_ref)

    def block(partial):
        for h in range(heads):
            at = slice(HD * h, HD * (h + 1))
            s = dot(k_ref[0, at, :], q_ref[0, at, :], (0, 0))
            if partial:
                s = jnp.where(lax.broadcasted_iota(jnp.int32, s.shape, 0) < live, s, MASKED)
            before = peak_ref[h : h + 1, :]
            peak = jnp.maximum(before, jnp.max(s, axis=0, keepdims=True))
            p = jnp.exp(s - peak)
            shrink = jnp.exp(before - peak)
            peak_ref[h : h + 1, :] = peak
            total_ref[h : h + 1, :] = total_ref[h : h + 1, :] * shrink + jnp.sum(p, axis=0, keepdims=True)
            acc_ref[at, :] = acc_ref[at, :] * shrink + dot(v_ref[0, at, :], p.astype(BF16))

    @pl.when(live == ROW_BLOCK)
    def _():
        block(False)

    @pl.when((live > 0) & (live < ROW_BLOCK))
    def _():
        block(True)

    @pl.when(work_ref[4, i] == 1)
    def _():
        total = total_ref[...]
        some = total > 0
        inverse = jnp.where(some, 1.0 / jnp.where(some, total, 1.0), 0.0)
        lse_ref[0] = jnp.where(some, peak_ref[...] + jnp.log(jnp.where(some, total, 1.0)), MASKED)
        for h in range(heads):
            at = slice(HD * h, HD * (h + 1))
            o_ref[0, at, :] = (acc_ref[at, :] * inverse[h : h + 1, :]).astype(o_ref.dtype)


def cross_forward(work, q, k, v):
    examples, feats, length = q.shape
    q_spec = pl.BlockSpec((1, feats, length), lambda i, work: (work[0, i], 0, 0))
    k_spec = pl.BlockSpec((1, feats, ROW_BLOCK), lambda i, work: (work[0, i], 0, work[1, i]))
    l_spec = pl.BlockSpec((1, 8, length), lambda i, work: (work[0, i], 0, 0))
    return pl.pallas_call(
        cross_forward_kernel,
        grid_spec=pltpu.PrefetchScalarGridSpec(
            num_scalar_prefetch=1,
            grid=(work.shape[1],),
            in_specs=[q_spec, k_spec, k_spec],
            out_specs=[q_spec, l_spec],
            scratch_shapes=[
                pltpu.VMEM((8, length), F32),
                pltpu.VMEM((8, length), F32),
                pltpu.VMEM((feats, length), F32),
            ],
        ),
        out_shape=[
            jax.ShapeDtypeStruct((examples, feats, length), BF16),
            jax.ShapeDtypeStruct((examples, 8, length), F32),
        ],
        compiler_params=pltpu.CompilerParams(vmem_limit_bytes=48 << 20),
        cost_estimate=cost(30e-6 * PEAK_FLOPS, 16e6),
        name="cross_forward",
    )(work, q, k, v)


def cross_backward_kernel(
    work_ref, q_ref, do_ref, lse_ref, inner_ref, k_ref, v_ref, dq_ref, dkv_ref, acc_ref
):
    i = pl.program_id(0)
    feats = acc_ref.shape[0]
    heads = feats // HD
    live = work_ref[2, i]

    @pl.when(work_ref[3, i] == 1)
    def _():
        acc_ref[...] = jnp.zeros_like(acc_ref)

    def block(partial):
        for h in range(heads):
            at = slice(HD * h, HD * (h + 1))
            q, do, k, v = q_ref[0, at, :], do_ref[0, at, :], k_ref[0, at, :], v_ref[0, at, :]
            s = dot(k, q, (0, 0))
            p = jnp.exp(s - lse_ref[0, h : h + 1, :])
            if partial:
                p = jnp.where(lax.broadcasted_iota(jnp.int32, s.shape, 0) < live, p, 0.0)
            dp = dot(v, do, (0, 0))
            ds = (p * (dp - inner_ref[0, h : h + 1, :])).astype(BF16)
            acc_ref[at, :] += dot(k, ds)
            dkv_ref[0, :, at] = dot(ds, q, (1, 1)).astype(BF16)
            dkv_ref[0, :, feats + HD * h : feats + HD * (h + 1)] = dot(p.astype(BF16), do, (1, 1)).astype(BF16)

    @pl.when(live == ROW_BLOCK)
    def _():
        block(False)

    @pl.when((live > 0) & (live < ROW_BLOCK))
    def _():
        block(True)

    @pl.when(work_ref[4, i] == 1)
    def _():
        dq_ref[0] = acc_ref[...].T.astype(BF16)


def cross_backward(work, q, do, lse, inner, k, v):
    examples, feats, length = q.shape
    rows = k.shape[2]
    q_spec = pl.BlockSpec((1, feats, length), lambda i, work: (work[0, i], 0, 0))
    k_spec = pl.BlockSpec((1, feats, ROW_BLOCK), lambda i, work: (work[0, i], 0, work[1, i]))
    l_spec = pl.BlockSpec((1, 8, length), lambda i, work: (work[0, i], 0, 0))
    d_spec = pl.BlockSpec((1, ROW_BLOCK, 2 * feats), lambda i, work: (work[0, i], work[1, i], 0))
    return pl.pallas_call(
        cross_backward_kernel,
        grid_spec=pltpu.PrefetchScalarGridSpec(
            num_scalar_prefetch=1,
            grid=(work.shape[1],),
            in_specs=[q_spec, q_spec, l_spec, l_spec, k_spec, k_spec],
            out_specs=[
                pl.BlockSpec((1, length, feats), lambda i, work: (work[0, i], 0, 0)),
                d_spec,
            ],
            scratch_shapes=[pltpu.VMEM((feats, length), F32)],
        ),
        out_shape=[
            jax.ShapeDtypeStruct((examples, length, feats), BF16),
            jax.ShapeDtypeStruct((examples, rows, 2 * feats), BF16),
        ],
        compiler_params=pltpu.CompilerParams(vmem_limit_bytes=48 << 20),
        cost_estimate=cost(45e-6 * PEAK_FLOPS, 24e6),
        name="cross_backward",
    )(work, q, do, lse, inner, k, v)


def memory_backward_kernel(
    live_ref, own_ref, other_ref, dkv_ref, wt_ref, out_ref, out_other_ref, g_ref, sum_ref
):
    e, j = pl.program_id(0), pl.program_id(1)
    own_blocks = pl.num_programs(1) // 2

    @pl.when((e == 0) & (j == 0))
    def _():
        sum_ref[...] = jnp.zeros_like(sum_ref)

    for mine, rows_ref, to_ref in ((j < own_blocks, own_ref, out_ref), (j >= own_blocks, other_ref, out_other_ref)):

        @pl.when(mine & (live_ref[e, j] > 0))
        def _():
            dkv = dkv_ref[0]
            sum_ref[...] += dot(rows_ref[0], dkv, (0, 0))
            to_ref[0] = dot(dkv, wt_ref[...]).astype(BF16)

        @pl.when(mine & (live_ref[e, j] == 0))
        def _():
            to_ref[0] = jnp.zeros_like(to_ref[0])

    @pl.when((e == pl.num_programs(0) - 1) & (j == pl.num_programs(1) - 1))
    def _():
        g_ref[...] = sum_ref[...].astype(BF16)


def memory_backward(live, own, other, dkv, wt):
    examples, count, model = own.shape
    width = dkv.shape[2]
    half = count // ROW_BLOCK
    row_spec = lambda first: pl.BlockSpec(
        (1, ROW_BLOCK, model), lambda e, j, live: (e, jnp.clip(j - first, 0, half - 1), 0)
    )
    d_spec = pl.BlockSpec((1, ROW_BLOCK, width), lambda e, j, live: (e, j, 0))
    w_spec = pl.BlockSpec(wt.shape, lambda e, j, live: (0, 0))
    return pl.pallas_call(
        memory_backward_kernel,
        grid_spec=pltpu.PrefetchScalarGridSpec(
            num_scalar_prefetch=1,
            grid=(examples, 2 * half),
            in_specs=[row_spec(0), row_spec(half), d_spec, w_spec],
            out_specs=[row_spec(0), row_spec(half), pl.BlockSpec((model, width), lambda e, j, live: (0, 0))],
            scratch_shapes=[pltpu.VMEM((model, width), F32)],
        ),
        out_shape=[
            jax.ShapeDtypeStruct(own.shape, BF16),
            jax.ShapeDtypeStruct(own.shape, BF16),
            jax.ShapeDtypeStruct((model, width), BF16),
        ],
        compiler_params=pltpu.CompilerParams(vmem_limit_bytes=48 << 20),
        cost_estimate=cost(18e-6 * PEAK_FLOPS, 30e6),
        name="memory_backward",
    )(live, own, other, dkv, wt)


def place_index(place_ref, flip):
    return jnp.bitwise_xor(place_ref[0], flip)


def strip(index, size):
    return pl.ds(pl.multiple_of(index * size, size), size)


def self_output_kernel(
    place_ref, x_ref, o0_ref, o1_ref, o2_ref, o3_ref, mine_ref, other_ref, gain_ref,
    n2_ref, q_ref, x1_ref, own_o_ref, wo_ref, wq_ref,
    rows_ref,
):
    core = jnp.bitwise_and(place_ref[0], 1)
    feats = wq_ref.shape[1]
    width = o0_ref.shape[1]
    own = x1_ref.shape[1]

    @pl.when(pl.program_id(0) == 0)
    def _():
        for i, from_ref in ((core, mine_ref), (1 - core, other_ref)):
            wo_ref[:, strip(i, feats)] = from_ref[:, feats:]
        for i, from_ref in enumerate((mine_ref, other_ref)):
            for at in range(0, feats, LANES):
                wq_ref[i, at : at + LANES, :] = from_ref[:, at : at + LANES].T

    x1 = x_ref[0].astype(F32)
    for flip, o_ref in enumerate((o0_ref, o1_ref, o2_ref, o3_ref)):
        heads = strip(place_index(place_ref, flip), width)
        x1 += dot(o_ref[0], wo_ref[heads, :], (0, 0))
        own_o_ref[0, heads, :] = o_ref[0, :, strip(place_ref[0], own)]
    n2 = root_norm(x1, gain_ref[...]).astype(BF16)
    n2_ref[0] = n2
    q_ref[0] = dot(wq_ref[0], n2, (1, 1)).astype(BF16)
    rows_ref[...] = x1
    x1_ref[0] = rows_ref[strip(place_ref[0], own), :]


def self_output_stage(place, x, pieces, mine, other, gain):
    examples, length, model = x.shape
    own, feats, width = length // 4, model // 2, pieces[0].shape[1]
    whole = lambda *shape: pl.BlockSpec(shape, lambda e: (0,) * len(shape))
    per = lambda *shape: pl.BlockSpec((1, *shape), lambda e: (e, 0, 0))
    array = jax.ShapeDtypeStruct
    return pl.pallas_call(
        self_output_kernel,
        grid=(examples,),
        in_specs=[pl.BlockSpec(memory_space=pltpu.SMEM), per(length, model)]
        + [per(width, length)] * 4
        + [whole(*mine.shape), whole(*other.shape), whole(1, model)],
        out_specs=[
            per(length, model),
            per(feats, length),
            per(own, model),
            per(model, own),
            whole(model, model),
            whole(2, feats, model),
        ],
        out_shape=[
            array((examples, length, model), BF16),
            array((examples, feats, length), BF16),
            array((examples, own, model), F32),
            array((examples, model, own), BF16),
            array((model, model), BF16),
            array((2, feats, model), BF16),
        ],
        scratch_shapes=[pltpu.VMEM((length, model), F32)],
        compiler_params=pltpu.CompilerParams(vmem_limit_bytes=48 << 20),
        cost_estimate=cost(6e-6 * PEAK_FLOPS, 10e6),
        name="self_output_stage",
    )(place, x, *pieces, mine, other, gain)


def combine_kernel(place_ref, o_ref, came_ref, lse_ref, other_lse_ref, chip_ref, total_ref):
    row = lax.shift_right_logical(place_ref[0], 1)
    here = strip(row, came_ref.shape[2])
    one, two = lse_ref[0], other_lse_ref[0]
    peak = jnp.maximum(one, two)
    total_ref[0] = peak + jnp.log(jnp.exp(one - peak) + jnp.exp(two - peak))
    own_weight = jnp.exp(lse_ref[0, :, here] - total_ref[0, :, here])
    other_weight = jnp.exp(other_lse_ref[0, :, here] - total_ref[0, :, here])
    for h in range(o_ref.shape[1] // HD):
        at = slice(HD * h, HD * (h + 1))
        one = o_ref[0, at, here].astype(F32) * own_weight[h : h + 1, :]
        chip_ref[0, at, :] = (one + came_ref[0, at, :].astype(F32) * other_weight[h : h + 1, :]).astype(BF16)


def combine(place, o, came, lse, other_lse):
    examples, feats, length = o.shape
    per = lambda *shape: pl.BlockSpec((1, *shape), lambda e: (e, 0, 0))
    return pl.pallas_call(
        combine_kernel,
        grid=(examples,),
        in_specs=[
            pl.BlockSpec(memory_space=pltpu.SMEM),
            per(feats, length),
            per(feats, length // 2),
            per(8, length),
            per(8, length),
        ],
        out_specs=[per(feats, length // 2), per(8, length)],
        out_shape=[
            jax.ShapeDtypeStruct((examples, feats, length // 2), BF16),
            jax.ShapeDtypeStruct((examples, 8, length), F32),
        ],
        compiler_params=pltpu.CompilerParams(vmem_limit_bytes=24 << 20),
        cost_estimate=cost(2e-6 * PEAK_FLOPS, 3e6),
        name="combine",
    )(place, o, came, lse, other_lse)


def norm_back(values, gain, grad):
    scale = lax.rsqrt(jnp.mean(values * values, axis=-1, keepdims=True) + NORM_EPS)
    pulled = grad * gain
    inner = jnp.mean(values * pulled, axis=-1, keepdims=True)
    back = scale * pulled - values * (scale * scale * scale * inner)
    return back, jnp.sum(grad * values * scale, axis=0, keepdims=True)


def feed_forward_kernel(
    place_ref, x1_ref, mine_ref, other_ref, dy_ref, gain_ref, wo_ref, gate_ref, up_ref, down_ref,
    out_ref, dx2_ref, doc_mine_ref, doc_other_ref, inner_mine_ref, inner_other_ref,
    g_ref, g_sent_ref, g_down_ref, g_down_sent_ref, g_out_ref, g_out_sent_ref, g_gain_ref,
    x2_ref, n3_ref, sum_ref, dn3_ref, g_full_ref, *, piece,
):
    i = pl.program_id(0)
    core = jnp.bitwise_and(place_ref[0], 1)
    examples, feats, own = mine_ref.shape

    def deal(low, high, keep_ref, sent_ref):
        keep_ref[...] = jnp.where(core == 0, low, high).astype(BF16)
        sent_ref[...] = jnp.where(core == 0, high, low).astype(BF16)
    sides = ((core, mine_ref, doc_mine_ref, inner_mine_ref), (1 - core, other_ref, doc_other_ref, inner_other_ref))

    @pl.when(i == 0)
    def _():
        for e in range(examples):
            x2 = x1_ref[own * e : own * (e + 1), :]
            for side, o_ref, *_ in sides:
                x2 += dot(o_ref[e], wo_ref[strip(side, feats), :], (0, 0))
            x2_ref[own * e : own * (e + 1), :] = x2
        n3_ref[...] = root_norm(x2_ref[...], gain_ref[...]).astype(BF16)
        sum_ref[...] = jnp.zeros_like(sum_ref)
        dn3_ref[...] = jnp.zeros_like(dn3_ref)

    n3, dy = n3_ref[...], dy_ref[...]
    a, u = dot(n3, gate_ref[...]), dot(n3, up_ref[...])
    dh = dot(dy, down_ref[...], (1, 1))
    root = math.sqrt(2 / math.pi)
    bent = jnp.tanh(root * (a + 0.044715 * (a * a * a)))
    rise = 0.5 * (1.0 + bent)
    gelu = a * rise
    slope = rise + 0.5 * a * (1.0 - bent * bent) * (root * (1.0 + 3 * 0.044715 * (a * a)))
    hidden = (gelu * u).astype(BF16)
    da = (dh * u * slope).astype(BF16)
    du = (dh * gelu).astype(BF16)
    sum_ref[...] += dot(hidden, down_ref[...])
    g_down = dot(hidden, dy, (0, 0))
    pieces = g_down.reshape(g_down.shape[0] // (2 * piece), 2, piece, g_down.shape[1])
    deal(*(pieces[:, side].reshape(g_down_ref.shape) for side in range(2)), g_down_ref, g_down_sent_ref)
    deal(dot(n3, da, (0, 0)), dot(n3, du, (0, 0)), g_ref, g_sent_ref)
    dn3_ref[...] += dot(da, gate_ref[...], (1, 1)) + dot(du, up_ref[...], (1, 1))

    @pl.when(i == pl.num_programs(0) - 1)
    def _():
        x2 = x2_ref[...]
        out_ref[...] = (x2 + sum_ref[...]).astype(BF16)
        back, g_gain = norm_back(x2, gain_ref[...], dn3_ref[...])
        g_gain_ref[...] = g_gain
        dx2 = dy_ref[...].astype(F32) + back
        dx2_ref[...] = dx2
        n3_ref[...] = dx2.astype(BF16)
        for side, o_ref, doc_ref, inner_ref in sides:
            heads = strip(side, feats)
            total = jnp.zeros((feats, wo_ref.shape[1]), F32)
            inner_ref[...] = jnp.zeros_like(inner_ref)
            for e in range(examples):
                dx2r = n3_ref[own * e : own * (e + 1), :]
                total += dot(o_ref[e], dx2r)
                doc = dot(wo_ref[heads, :], dx2r, (1, 1)).astype(BF16)
                doc_ref[e] = doc
                product = doc.astype(F32) * o_ref[e].astype(F32)
                for h in range(feats // HD):
                    inner_ref[e, h : h + 1, :] = jnp.sum(product[HD * h : HD * (h + 1)], axis=0, keepdims=True)
            g_full_ref[heads, :] = total
        deal(g_full_ref[:, :feats], g_full_ref[:, feats:], g_out_ref, g_out_sent_ref)


def feed_forward(place, x1, mine, other, dy, gain, wide_w, down, piece):
    tokens, model = x1.shape
    examples, feats, own = mine.shape
    hidden = down.shape[0]
    part = 256
    whole = lambda *shape: pl.BlockSpec(shape, lambda i: (0,) * len(shape))
    first = model // part
    array = jax.ShapeDtypeStruct
    return pl.pallas_call(
        functools.partial(feed_forward_kernel, piece=piece),
        grid=(hidden // part,),
        in_specs=[
            pl.BlockSpec(memory_space=pltpu.SMEM),
            whole(tokens, model),
            whole(*mine.shape),
            whole(*other.shape),
            whole(tokens, model),
            whole(1, model),
            whole(model, model),
            pl.BlockSpec((model, part), lambda i: (0, first + i)),
            pl.BlockSpec((model, part), lambda i: (0, first + hidden // part + i)),
            pl.BlockSpec((part, model), lambda i: (i, 0)),
        ],
        out_specs=[
            whole(tokens, model),
            whole(tokens, model),
            whole(*mine.shape),
            whole(*mine.shape),
            whole(examples, 8, own),
            whole(examples, 8, own),
            *[pl.BlockSpec((model, part), lambda i: (0, i))] * 2,
            *[pl.BlockSpec((part // 2, model), lambda i: (i, 0))] * 2,
            *[whole(model, feats)] * 2,
            whole(1, model),
        ],
        out_shape=[
            array((tokens, model), BF16),
            array((tokens, model), F32),
            array(mine.shape, BF16),
            array(mine.shape, BF16),
            array((examples, 8, own), F32),
            array((examples, 8, own), F32),
            *[array((model, hidden), BF16)] * 2,
            *[array((hidden // 2, model), BF16)] * 2,
            *[array((model, feats), BF16)] * 2,
            array((1, model), F32),
        ],
        scratch_shapes=[
            pltpu.VMEM((tokens, model), F32),
            pltpu.VMEM((tokens, model), BF16),
            pltpu.VMEM((tokens, model), F32),
            pltpu.VMEM((tokens, model), F32),
            pltpu.VMEM((model, model), F32),
        ],
        compiler_params=pltpu.CompilerParams(vmem_limit_bytes=48 << 20),
        cost_estimate=cost(20e-6 * PEAK_FLOPS, 24e6),
        name="feed_forward",
    )(place, x1, mine, other, dy, gain, wide_w, wide_w, wide_w, down)


def self_output_back_kernel(
    mine_ref, other_ref, wq_ref, x1_ref, gain_ref, dx2_ref, own_o_ref, wo_ref,
    dx1_ref, do_ref, g_out_ref, g_gain_ref,
    sum_ref,
):
    e = pl.program_id(0)

    @pl.when(e == 0)
    def _():
        sum_ref[...] = jnp.zeros_like(sum_ref)
        g_gain_ref[...] = jnp.zeros_like(g_gain_ref)

    dn2 = dot(mine_ref[0], wq_ref[0]) + dot(other_ref[0], wq_ref[1])
    back, g_gain = norm_back(x1_ref[0], gain_ref[...], dn2)
    g_gain_ref[...] += g_gain
    dx1 = dx2_ref[0] + back
    dx1_ref[0] = dx1
    dx1r = dx1.astype(BF16)
    do_ref[0] = dot(wo_ref[...], dx1r, (1, 1)).astype(BF16)
    sum_ref[...] += dot(own_o_ref[0], dx1r)

    @pl.when(e == pl.num_programs(0) - 1)
    def _():
        g_out_ref[...] = sum_ref[...].astype(BF16)


def self_output_back(mine, other, wq, x1, gain, dx2, own_o, wo):
    examples, own, model = x1.shape
    feats = mine.shape[2]
    whole = lambda *shape: pl.BlockSpec(shape, lambda e: (0,) * len(shape))
    per = lambda *shape: pl.BlockSpec((1, *shape), lambda e: (e, 0, 0))
    array = jax.ShapeDtypeStruct
    return pl.pallas_call(
        self_output_back_kernel,
        grid=(examples,),
        in_specs=[
            per(own, feats),
            per(own, feats),
            whole(*wq.shape),
            per(own, model),
            whole(1, model),
            per(own, model),
            per(model, own),
            whole(model, model),
        ],
        out_specs=[per(own, model), per(model, own), whole(model, model), whole(1, model)],
        out_shape=[
            array((examples, own, model), F32),
            array((examples, model, own), BF16),
            array((model, model), BF16),
            array((1, model), F32),
        ],
        scratch_shapes=[pltpu.VMEM((model, model), F32)],
        compiler_params=pltpu.CompilerParams(vmem_limit_bytes=48 << 20),
        cost_estimate=cost(4e-6 * PEAK_FLOPS, 8e6),
        name="self_output_back",
    )(mine, other, wq, x1, gain, dx2, own_o, wo)


def fold_rows(rows, target, columns):
    rest = rows * columns // target
    tile = 16
    if rows % tile or target % tile or rows * target != columns * rest or rows // tile * LANES != rest:
        return (lambda b: b.reshape(*b.shape[:-2], target, rest)), (lambda b: b.reshape(rows, columns))

    def swap(b, down, across):
        b = b.reshape(*b.shape[:-2], down, tile, across, LANES)
        return jnp.swapaxes(b, -4, -2).reshape(*b.shape[:-4], across * tile, down * LANES)

    return (lambda b: swap(b, rows // tile, columns // LANES)), (lambda b: swap(b, target // tile, rest // LANES))


def local(
    dec_input,
    enc_out,
    enc_len,
    cotangent,
    self_query,
    self_key,
    self_value,
    self_output,
    cross_query,
    cross_key,
    cross_value,
    cross_output,
    ffn_gate,
    ffn_up,
    ffn_down,
    self_gain,
    cross_gain,
    ffn_gain,
    bias_table,
):
    place = lax.axis_index("narrow")
    row, core = place // 2, place % 2
    wide = lax.axis_size("wide")
    examples, own, model = dec_input.shape
    length = 4 * own
    heads = model // HD
    own_heads = heads // 4
    memory_rows = enc_out.shape[1]
    share = self_query.shape[0]

    half = lambda w: part_of(w.astype(BF16), core, 2, 1)
    own_qkv = jnp.concatenate(
        [part_of(w.astype(BF16), place, 4, 1) for w in (self_query, self_key, self_value)], 1
    )
    own_qkv = jnp.pad(own_qkv, ((0, 0), (0, -own_qkv.shape[1] % LANES)))
    small = jnp.stack([self_gain, cross_gain, ffn_gain, jnp.pad(bias_table, (0, share - bias_table.shape[0]))], 1)
    small = jnp.pad(small.astype(BF16), ((0, 0), (0, LANES - 4)))
    feats = model // 2
    self_w, small = wide_gather(jnp.concatenate([own_qkv, small], 1), (own_qkv.shape[1], LANES))
    small_rows = small[:, :4].astype(F32).T
    gain_one, gain_two, gain_three = (small_rows[i : i + 1] for i in range(3))
    table = small_rows[3].reshape(wide, share)[:, : bias_table.shape[0]].reshape(BUCKETS, heads)

    both = ("wide", "narrow")
    quarter = lambda w: part_of(w.astype(BF16), place, 4, 0)
    ffn_in = lax.all_gather(
        jnp.concatenate([quarter(cross_output), quarter(ffn_gate), quarter(ffn_up)], 1), both, axis=0, tiled=True
    )
    down_w = lax.all_gather(quarter(ffn_down), both, axis=0, tiled=True)

    enc_other = pair_swap(enc_out)
    starts = (place * memory_rows + np.arange(memory_rows // ROW_BLOCK) * ROW_BLOCK).astype(jnp.int32)
    other_starts = starts + (1 - 2 * core) * memory_rows
    block_starts = jnp.concatenate([starts, other_starts])
    live = jnp.clip(enc_len[:, None] - block_starts[None, :], 0, ROW_BLOCK)

    x_all = narrow_gather(dec_input, 1, row, core)
    hot = jnp.asarray(bucket_table(length))
    distance_bias = jnp.dot(table.T, hot, precision=FULL_ACCURACY)
    vec = jnp.pad(part_of(distance_bias, place, 4, 0), ((0, 8 - own_heads), (0, 0)))
    n1, qkv, self_o, self_lse, self_wt = self_forward(x_all, gain_one, self_w, vec, own_heads)
    across_o = across_swap(self_o)
    pieces = [self_o, pair_swap(self_o), across_o, pair_swap(across_o)]
    memory_w = shared_gather(jnp.concatenate([half(cross_key), half(cross_value)], 1), row, first=(self_o,))
    work = work_list(live)
    keys, values, memory_wt = memory_project(work, enc_out, enc_other, memory_w)
    query_out = after(jnp.concatenate([half(cross_query), half(self_output)], 1), self_o)
    mine_w = shared_gather(query_out, row)
    mine_w = after(mine_w, keys)
    other_w = pair_swap(mine_w)
    me = place.reshape(1).astype(jnp.int32)
    n2, cross_q, x1, own_o, self_out_w, cross_query_wt = self_output_stage(
        me, x_all, pieces, mine_w, other_w, gain_two
    )

    part_o, part_lse = cross_forward(work, cross_q, keys, values)
    came = across_swap(part_of(part_o, 1 - row, 2, 2))
    chip_o, lse = combine(me, part_o, came, part_lse, across_swap(part_lse))
    mine_o, other_o = part_of(chip_o, core, 2, 2), pair_swap(part_of(chip_o, 1 - core, 2, 2))

    tokens = examples * own
    down_rows = ffn_down.shape[0] // 2
    (
        layer_out, dx2, doc_mine, doc_other, inner_mine, inner_other,
        gate_up, gate_up_sent, down, down_sent, grad_co, co_sent, grad_gain_three,
    ) = feed_forward(
        me, x1.reshape(tokens, model), mine_o, other_o, cotangent.reshape(tokens, model), gain_three,
        ffn_in, down_w, down_rows,
    )
    layer_out, dx2 = layer_out.reshape(x1.shape), dx2.reshape(x1.shape)

    rows_of = lambda g: g.reshape(wide, share, -1)
    to_chip = lambda mine, other: jnp.concatenate(in_order(core, mine, pair_swap(other)), 2)
    doc, inner = to_chip(doc_mine, doc_other), to_chip(inner_mine, inner_other)
    doc_came, inner_came = across_swap(doc), across_swap(inner)
    fold, unfold = fold_rows(down_rows, share, model)
    gate_up = plus(gate_up, pair_swap(gate_up_sent))
    early = jnp.concatenate(
        [
            rows_of(plus(grad_co, pair_swap(co_sent))),
            fold(plus(down, pair_swap(down_sent)).reshape(wide, down_rows, model)),
        ],
        2,
    )
    doc_came, inner_came, early, gate_up = lax.optimization_barrier((doc_came, inner_came, early, gate_up))
    early_sum = lax.psum_scatter(
        early.reshape(wide * share, -1), "wide", scatter_dimension=0, tiled=True
    )
    to_all = lambda mine, came: jnp.concatenate(in_order(row, mine, came), 2)
    part_dq, dkv = cross_backward(
        work, cross_q, to_all(doc, doc_came), lse, to_all(inner, inner_came), keys, values
    )

    gate_up_came = across_swap(part_of(gate_up, 1 - row, 2, 1))
    part_dq, dkv, gate_up_came = lax.optimization_barrier((part_dq, dkv, gate_up_came))
    gate_up = wide_scatter_x(rows_of(plus(part_of(gate_up, row, 2, 1), gate_up_came)))

    dq_came = across_swap(part_of(part_dq, 1 - row, 2, 1))
    enc_mine, enc_swapped, grad_memory = memory_backward(live, enc_out, enc_other, dkv, memory_wt)
    enc_came = pair_swap(enc_swapped)
    dq_came, grad_memory, gate_up = lax.optimization_barrier((dq_came, grad_memory, gate_up))
    gate_up_sum = wide_scatter_z(gate_up)
    chip_dq = plus(part_of(part_dq, row, 2, 1), dq_came)
    dq_mine, dq_other = part_of(chip_dq, core, 2, 1), pair_swap(part_of(chip_dq, 1 - core, 2, 1))
    grad_cross_query = jnp.einsum("etd,etf->df", n2, part_dq, preferred_element_type=F32).astype(BF16)
    late = wide_scatter_x(jnp.concatenate([rows_of(grad_cross_query), rows_of(grad_memory)], 2))
    dx1, do, grad_self_output, grad_gain_two = self_output_back(
        dq_mine, dq_other, cross_query_wt, x1, gain_two, dx2, own_o, self_out_w
    )
    enc_grad = plus(enc_mine, enc_came)

    low, high = in_order(row, part_of(do, row, 2, 1), across_swap(part_of(do, 1 - row, 2, 1)))
    column = jnp.stack([low, high], 2)
    low, high = in_order(core, part_of(column, core, 2, 1), pair_swap(part_of(column, 1 - core, 2, 1)))
    do_heads = jnp.stack([low, high], 3).reshape(examples, own_heads * HD, length)
    do_heads, late, enc_grad, gate_up_sum = lax.optimization_barrier((do_heads, late, enc_grad, gate_up_sum))
    part_dn1, grad_self, dvec = self_backward(n1, qkv, do_heads, self_lse, self_wt, vec, own_heads)
    late_sum = wide_scatter_z(late)
    part_dn1, grad_self, late_sum = lax.optimization_barrier((part_dn1, grad_self, late_sum))
    by_core = part_dn1.reshape(examples, 2, 2, own, model)
    column = part_of(by_core, core, 2, 2) + pair_swap(part_of(by_core, 1 - core, 2, 2).astype(BF16)).astype(F32)
    dn1 = part_of(column, row, 2, 1) + across_swap(part_of(column, 1 - row, 2, 1).astype(BF16)).astype(F32)
    grad_in, grad_gain_one = norm_back(
        dec_input.reshape(tokens, model).astype(F32), gain_one, dn1.reshape(tokens, model)
    )
    input_grad = (dx1 + grad_in.reshape(x1.shape)).astype(BF16)

    so = rows_of(plus(part_of(grad_self_output, core, 2, 1), pair_swap(part_of(grad_self_output, 1 - core, 2, 1))))
    so = plus(part_of(so, row, 2, 1), across_swap(part_of(so, 1 - row, 2, 1)))
    self_width = grad_self.shape[1]
    self_halves = grad_self.astype(BF16).reshape(wide, 2, share // 2, self_width)
    last = wide_scatter(jnp.concatenate([self_halves[:, 0], self_halves[:, 1], so], 2))
    low, high = in_order(row, last, across_swap(last))
    last = jnp.stack([low, high])
    low, high = in_order(core, last, pair_swap(last))
    halves = lambda part: jnp.concatenate([part[:, :self_width], part[:, self_width : 2 * self_width]], 0)
    self_sum = [halves(part[y]) for y in range(2) for part in (low, high)]
    q_sum, k_sum, v_sum = (
        jnp.concatenate([part[:, own_heads * HD * i : own_heads * HD * (i + 1)] for part in self_sum], 1)
        for i in range(3)
    )
    so_sum = jnp.concatenate(
        [part[:, :, 2 * self_width :].reshape(share, -1) for part in (low, high)], 1
    )

    early_sum = plus(early_sum, across_swap(early_sum))
    low, high = in_order(core, early_sum, pair_swap(early_sum))
    co_sum = jnp.concatenate([part[:, :feats] for part in (low, high)], 1)
    down_sum = jnp.concatenate([unfold(part[:, feats:]) for part in (low, high)], 0)
    gate_up_sum = jnp.concatenate(in_order(row, gate_up_sum, across_swap(gate_up_sum)), 1)
    gate_sum, up_sum = in_order(core, gate_up_sum, pair_swap(gate_up_sum))
    late_sum = plus(late_sum, across_swap(late_sum))
    low, high = in_order(core, late_sum, pair_swap(late_sum))
    cq_sum, ck_sum, cv_sum = (
        jnp.concatenate([part[:, feats * i : feats * (i + 1)] for part in (low, high)], 1) for i in range(3)
    )

    own_table = jnp.dot(hot, dvec[:own_heads].T, precision=FULL_ACCURACY)
    grad_table = lax.dynamic_update_slice_in_dim(
        jnp.zeros((BUCKETS, heads), F32), own_table, place * own_heads, 1
    )
    small = jnp.concatenate(
        [g.reshape(wide, share) for g in (grad_gain_one, grad_gain_two, grad_gain_three)]
        + [grad_table.reshape(wide, bias_table.shape[0])], 1
    )
    small = small + pair_swap(small)
    small = small + across_swap(small)
    small_sum = wide_scatter(small.reshape(wide, 1, -1)).reshape(-1)
    f = lambda a: a.astype(F32)
    return (
        layer_out,
        input_grad,
        enc_grad,
        *(f(g) for g in (q_sum, k_sum, v_sum, so_sum, cq_sum, ck_sum, cv_sum, co_sum, gate_sum, up_sum, down_sum)),
        small_sum[:share],
        small_sum[share : 2 * share],
        small_sum[2 * share : 3 * share],
        small_sum[3 * share :],
    )


def solution(mesh):
    rows = P("wide", "narrow", None)
    weight, vector = P("wide", None), P("wide")
    return jax.shard_map(
        local,
        mesh=mesh,
        in_specs=(rows, rows, vector, rows, *[weight] * 11, *[vector] * 4),
        out_specs=(rows, rows, rows, *[weight] * 11, *[vector] * 4),
        check_vma=False,
    )
```

```python
import functools
import math

import jax
import jax.numpy as jnp
import numpy as np
from jax import lax
from jax.experimental import pallas as pl
from jax.experimental.pallas import tpu as pltpu
from jax.sharding import PartitionSpec as P

HD = 64
BUCKETS = 32
MAXDIST = 128
NORM_EPS = 1e-06
MASKED = -1e30
LANES = 128
ROW_BLOCK = 512
PEAK_FLOPS = 1.15e15
FULL_ACCURACY = lax.Precision.HIGHEST
F32 = jnp.float32
BF16 = jnp.bfloat16

PAIR = ((0, 1), (1, 0), (2, 3), (3, 2))
ACROSS = ((0, 2), (2, 0), (1, 3), (3, 1))


def bucket_table(length):
    exact = BUCKETS // 2
    hot = np.zeros((BUCKETS, length), np.float32)
    for distance in range(length):
        bucket = distance
        if distance >= exact:
            scaled = math.log(distance / exact) / math.log(MAXDIST / exact) * (BUCKETS - exact)
            bucket = min(exact + math.floor(scaled), BUCKETS - 1)
        hot[bucket, distance] = 1.0
    return hot


def dot(left, right, contract=(1, 0)):
    return lax.dot_general(
        left, right, (((contract[0],), (contract[1],)), ((), ())), preferred_element_type=F32
    )


def root_norm(values, gain):
    return values * lax.rsqrt(jnp.mean(values * values, axis=-1, keepdims=True) + NORM_EPS) * gain


def pair_swap(value):
    return lax.ppermute(value, "narrow", PAIR)


def across_swap(value):
    return lax.ppermute(value, "narrow", ACROSS)


def in_order(flag, mine, other):
    first = flag == 0
    return jnp.where(first, mine, other), jnp.where(first, other, mine)


def narrow_gather(value, axis, row, core):
    low, high = in_order(row, value, across_swap(value))
    column = jnp.stack([low, high], axis)
    low, high = in_order(core, column, pair_swap(column))
    full = jnp.stack([low, high], axis + 1)
    shape = list(value.shape)
    shape[axis] *= 4
    return full.reshape(shape)


def plus(mine, came):
    return (mine.astype(F32) + came.astype(F32)).astype(mine.dtype)


def part_of(value, index, parts, axis):
    size = value.shape[axis] // parts
    return lax.dynamic_slice_in_dim(value, index * size, size, axis)


LINE = 4
BESIDE = tuple((i, i ^ 1) for i in range(2 * LINE))


def along(step):
    return [(2 * z + x, 2 * ((z + step) % LINE) + x) for z in range(LINE) for x in range(2)]


def by_planes():
    return lax.axis_size("wide") == 2 * LINE


def assemble_kernel(widths, order_ref, *refs):
    pieces, outs = refs[: 2 * LINE], refs[2 * LINE :]
    for i, piece in enumerate(pieces):
        at = 0
        for width, out in zip(widths, outs):
            out[order_ref[i]] = piece[:, at : at + width]
            at += width


def after(value, *others):
    return lax.optimization_barrier((value, *others))[0]


def wide_gather(block, widths, first=()):
    rows = block.shape[0]
    if not by_planes():
        full = lax.all_gather(block, "wide", axis=0, tiled=True)
        bounds = np.cumsum([0, *widths])
        return [full[:, a:b] for a, b in zip(bounds[:-1], bounds[1:])]
    z, x = lax.axis_index("wide") // 2, lax.axis_index("wide") % 2
    line = [block] + [lax.ppermute(block, "wide", along(step)) for step in range(1, LINE)]
    line = after(line, *first)
    pieces = line + [lax.ppermute(piece, "wide", BESIDE) for piece in line]
    places = (z - np.arange(LINE)) % LINE * 2
    order = jnp.concatenate([places + x, places + 1 - x]).astype(jnp.int32)
    outs = pl.pallas_call(
        functools.partial(assemble_kernel, widths),
        in_specs=[pl.BlockSpec(memory_space=pltpu.SMEM)] + [pl.BlockSpec(memory_space=pltpu.VMEM)] * len(pieces),
        out_specs=[pl.BlockSpec(memory_space=pltpu.VMEM)] * len(widths),
        out_shape=[jax.ShapeDtypeStruct((2 * LINE, rows, width), block.dtype) for width in widths],
        compiler_params=pltpu.CompilerParams(vmem_limit_bytes=16 << 20),
        name="assemble",
    )(order, *pieces)
    return [out.reshape(2 * LINE * rows, out.shape[2]) for out in outs]


def shared_gather(block, row, first=()):
    rows, width = block.shape
    (full,) = wide_gather(part_of(block, row, 2, 0), (width,), first)
    halves = full.reshape(-1, rows // 2, width)
    return jnp.stack(in_order(row, halves, across_swap(halves)), 1).reshape(-1, width)


def pick(value, index, axis):
    return lax.dynamic_index_in_dim(value, index, axis, keepdims=False)


def x_swap(blocks):
    if not by_planes():
        return (blocks,)
    x = lax.axis_index("wide") % 2
    planes = blocks.reshape(LINE, 2, *blocks.shape[1:])
    return pick(planes, x, 1), lax.ppermute(pick(planes, 1 - x, 1), "wide", BESIDE)


def z_swap(planes):
    if not by_planes():
        shape = planes.shape
        return (
            lax.psum_scatter(
                planes.reshape(shape[0] * shape[1], *shape[2:]), "wide", scatter_dimension=0, tiled=True
            ),
        )
    z = lax.axis_index("wide") // 2
    sent = [pick(planes, (z + step) % LINE, 0) for step in range(1, LINE)]
    return pick(planes, z, 0), *(lax.ppermute(s, "wide", along(i + 1)) for i, s in enumerate(sent))


def total(parts):
    return sum((part.astype(F32) for part in parts[1:]), parts[0].astype(F32)).astype(parts[0].dtype)


def wide_scatter_x(blocks):
    return total(x_swap(blocks))


def wide_scatter_z(planes):
    return total(z_swap(planes))


def wide_scatter(blocks):
    return wide_scatter_z(wide_scatter_x(blocks))


def place_index(place_ref, flip):
    return jnp.bitwise_xor(place_ref[0], flip)


def strip(index, size):
    return pl.ds(pl.multiple_of(index * size, size), size)


def transpose_columns(weight_ref, out_ref):
    for i in range(0, weight_ref.shape[1], LANES):
        out_ref[i : i + LANES, :] = weight_ref[:, i : i + LANES].T


def cost(flops, moved):
    return pl.CostEstimate(flops=int(flops), bytes_accessed=int(moved), transcendentals=0)


def position_bias(vec_ref, bias_ref):
    heads, size, _ = bias_ref.shape
    key = lax.broadcasted_iota(jnp.int32, (size, size), 0)
    query = lax.broadcasted_iota(jnp.int32, (size, size), 1)
    for h in range(heads):
        rows = jnp.broadcast_to(vec_ref[h : h + 1, :], (size, size))
        rolled = pltpu.roll(rows, 0, 1, stride=1, stride_axis=0)
        bias_ref[h] = jnp.where(key <= query, rolled, MASKED)


def self_forward_kernel(
    x_ref, gain_ref, w_ref, vec_ref, qkv_ref, out_ref, lse_ref, wt_ref, bias_ref
):
    heads = bias_ref.shape[0]
    width = heads * HD

    @pl.when(pl.program_id(0) == 0)
    def _():
        transpose_columns(w_ref, wt_ref)
        position_bias(vec_ref, bias_ref)

    normed = root_norm(x_ref[0].astype(F32), gain_ref[...]).astype(BF16)
    qkv = dot(wt_ref[...], normed, (1, 1)).astype(BF16)
    qkv_ref[0] = qkv
    lse_ref[...] = jnp.zeros_like(lse_ref)
    for h in range(heads):
        q, k, v = (qkv[width * part + HD * h : width * part + HD * (h + 1)] for part in range(3))
        s = dot(k, q, (0, 0)) + bias_ref[h]
        peak = jnp.max(s, axis=0, keepdims=True)
        raised = jnp.exp(s - peak)
        total = jnp.sum(raised, axis=0, keepdims=True)
        weight = (raised * (1.0 / total)).astype(BF16)
        out_ref[0, HD * h : HD * (h + 1), :] = dot(v, weight).astype(BF16)
        lse_ref[0, h : h + 1, :] = peak + jnp.log(total)


def self_forward(x, gain, weight, vec, heads):
    examples, length, model = x.shape
    feats = weight.shape[1]
    whole = lambda *shape: pl.BlockSpec(shape, lambda e: (0,) * len(shape))
    per = lambda *shape: pl.BlockSpec((1, *shape), lambda e: (e, 0, 0))
    return pl.pallas_call(
        self_forward_kernel,
        grid=(examples,),
        in_specs=[
            per(length, model),
            whole(1, model),
            whole(*weight.shape),
            whole(*vec.shape),
        ],
        out_specs=[
            per(feats, length),
            per(heads * HD, length),
            per(8, length),
            whole(feats, model),
        ],
        out_shape=[
            jax.ShapeDtypeStruct((examples, feats, length), BF16),
            jax.ShapeDtypeStruct((examples, heads * HD, length), BF16),
            jax.ShapeDtypeStruct((examples, 8, length), F32),
            jax.ShapeDtypeStruct((feats, model), BF16),
        ],
        scratch_shapes=[pltpu.VMEM((heads, length, length), F32)],
        compiler_params=pltpu.CompilerParams(vmem_limit_bytes=48 << 20),
        cost_estimate=cost(9e-6 * PEAK_FLOPS, 8e6),
        name="self_forward",
    )(x, gain, weight, vec)


def self_backward_kernel(
    place_ref, x_ref, gain_ref, qkv_ref, do0_ref, do1_ref, do2_ref, do3_ref, lse_ref, wt_ref, vec_ref,
    dn_ref, gw_ref, dvec_ref, g_gain_ref,
    bias_ref, dsum_ref, dqkv_ref, do_ref, sum_ref,
):
    heads, size, _ = bias_ref.shape
    width = heads * HD
    e = pl.program_id(0)

    @pl.when(e == 0)
    def _():
        position_bias(vec_ref, bias_ref)
        dsum_ref[...] = jnp.zeros_like(dsum_ref)
        sum_ref[...] = jnp.zeros_like(sum_ref)
        dqkv_ref[...] = jnp.zeros_like(dqkv_ref)
        g_gain_ref[...] = jnp.zeros_like(g_gain_ref)

    for flip, piece_ref in enumerate((do0_ref, do1_ref, do2_ref, do3_ref)):
        do_ref[:, strip(place_index(place_ref, flip), piece_ref.shape[2])] = piece_ref[0]
    for h in range(heads):
        q, k, v = (
            qkv_ref[0, width * part + HD * h : width * part + HD * (h + 1), :] for part in range(3)
        )
        do = do_ref[HD * h : HD * (h + 1), :]
        s = dot(k, q, (0, 0)) + bias_ref[h]
        p = jnp.exp(s - lse_ref[0, h : h + 1, :])
        dp = dot(v, do, (0, 0))
        inner = jnp.sum(p * dp, axis=0, keepdims=True)
        ds = p * (dp - inner)
        dsum_ref[h] += ds
        ds = ds.astype(BF16)
        at = lambda part: slice(width * part + HD * h, width * part + HD * (h + 1))
        dqkv_ref[:, at(0)] = dot(k, ds).T.astype(BF16)
        dqkv_ref[:, at(1)] = dot(ds, q, (1, 1)).astype(BF16)
        dqkv_ref[:, at(2)] = dot(p.astype(BF16), do, (1, 1)).astype(BF16)
    dqkv = dqkv_ref[...]
    dn = dot(dqkv, wt_ref[...])
    dn_ref[0] = dn.astype(BF16)
    x = x_ref[0].astype(F32)
    scaled = x * lax.rsqrt(jnp.mean(x * x, axis=-1, keepdims=True) + NORM_EPS)
    g_gain_ref[...] += jnp.sum(dn * scaled, axis=0, keepdims=True)
    sum_ref[...] += dot((scaled * gain_ref[...]).astype(BF16), dqkv, (0, 0))

    @pl.when(e == pl.num_programs(0) - 1)
    def _():
        gw_ref[...] = sum_ref[...].astype(BF16)
        dvec_ref[...] = jnp.zeros_like(dvec_ref)
        for h in range(heads):
            back, count = dsum_ref[h], size
            while count > 8:
                count //= 2
                back = back[:count] + pltpu.roll(back[count:], size - count, 1)
            total = back[:1]
            for r in range(1, count):
                total = total + pltpu.roll(back[r : r + 1], size - r, 1)
            dvec_ref[h : h + 1, :] = total


def self_backward(place, x, gain, qkv, do, lse, wt, vec, heads):
    examples, length, model = x.shape
    feats = wt.shape[0]
    whole = lambda *shape: pl.BlockSpec(shape, lambda e: (0,) * len(shape))
    per = lambda *shape: pl.BlockSpec((1, *shape), lambda e: (e, 0, 0))
    return pl.pallas_call(
        self_backward_kernel,
        grid=(examples,),
        in_specs=[
            pl.BlockSpec(memory_space=pltpu.SMEM),
            per(length, model),
            whole(1, model),
            per(feats, length),
            *[per(heads * HD, length // 4)] * 4,
            per(8, length),
            whole(*wt.shape),
            whole(*vec.shape),
        ],
        out_specs=[per(length, model), whole(model, feats), whole(8, length), whole(1, model)],
        out_shape=[
            jax.ShapeDtypeStruct((examples, length, model), BF16),
            jax.ShapeDtypeStruct((model, feats), BF16),
            jax.ShapeDtypeStruct((8, length), F32),
            jax.ShapeDtypeStruct((1, model), F32),
        ],
        scratch_shapes=[
            pltpu.VMEM((heads, length, length), F32),
            pltpu.VMEM((heads, length, length), F32),
            pltpu.VMEM((length, feats), BF16),
            pltpu.VMEM((heads * HD, length), BF16),
            pltpu.VMEM((model, feats), F32),
        ],
        compiler_params=pltpu.CompilerParams(vmem_limit_bytes=48 << 20),
        cost_estimate=cost(16e-6 * PEAK_FLOPS, 12e6),
        name="self_backward",
    )(place, x, gain, qkv, *do, lse, wt, vec)


def work_list(live):
    examples, blocks = live.shape
    flat = live.reshape(-1)
    index = jnp.arange(flat.shape[0], dtype=jnp.int32)
    block = index % blocks
    visit = (flat > 0) | (block == 0)
    before = jnp.sum(jnp.where(visit[None, :] & (index[None, :] < index[:, None]), 1, 0), axis=1)
    ends = visit & ~jnp.any(
        visit[None, :] & (index[None, :] > index[:, None]) & (index[None, :] // blocks == index[:, None] // blocks), axis=1
    )
    chosen = (before[None, :] == index[:, None]) & visit[None, :]
    take = lambda values: jnp.sum(jnp.where(chosen, values[None, :], 0), axis=1)
    final = jnp.max(jnp.where(visit, index, 0))
    found = jnp.any(chosen, axis=1)
    at = jnp.where(found, take(index), final)
    rows = [at // blocks, at % blocks, take(flat), found & (at % blocks == 0), take(ends.astype(jnp.int32))]
    return jnp.stack([r.astype(jnp.int32) for r in rows])


def memory_project_kernel(work_ref, own_ref, other_ref, w_ref, k_ref, v_ref, wt_ref):
    i = pl.program_id(0)
    block, live = work_ref[1, i], work_ref[2, i]
    half = wt_ref.shape[0] // 2
    own_blocks = 2

    @pl.when(i == 0)
    def _():
        transpose_columns(w_ref, wt_ref)

    def project(rows):
        both = dot(wt_ref[...], rows, (1, 1)).astype(BF16)
        k_ref[0] = both[:half]
        v_ref[0] = both[half:]

    @pl.when((live > 0) & (block < own_blocks))
    def _():
        project(own_ref[0])

    @pl.when((live > 0) & (block >= own_blocks))
    def _():
        project(other_ref[0])


def memory_project(work, own, other, weight):
    examples, rows, model = own.shape
    half = rows // ROW_BLOCK
    feats = weight.shape[1] // 2
    row_spec = lambda first: pl.BlockSpec(
        (1, ROW_BLOCK, model), lambda i, work: (work[0, i], jnp.clip(work[1, i] - first, 0, half - 1), 0)
    )
    out_spec = pl.BlockSpec((1, feats, ROW_BLOCK), lambda i, work: (work[0, i], 0, work[1, i]))
    out = jax.ShapeDtypeStruct((examples, feats, 2 * rows), BF16)
    w_spec = lambda *shape: pl.BlockSpec(shape, lambda i, work: (0, 0))
    return pl.pallas_call(
        memory_project_kernel,
        grid_spec=pltpu.PrefetchScalarGridSpec(
            num_scalar_prefetch=1,
            grid=(work.shape[1],),
            in_specs=[row_spec(0), row_spec(half), w_spec(*weight.shape)],
            out_specs=[out_spec, out_spec, w_spec(2 * feats, model)],
        ),
        out_shape=[out, out, jax.ShapeDtypeStruct((2 * feats, model), BF16)],
        compiler_params=pltpu.CompilerParams(vmem_limit_bytes=48 << 20),
        cost_estimate=cost(12e-6 * PEAK_FLOPS, 12e6),
        name="memory_project",
    )(work, own, other, weight)


def cross_forward_kernel(work_ref, q_ref, k_ref, v_ref, o_ref, lse_ref, peak_ref, total_ref, acc_ref):
    i = pl.program_id(0)
    heads = acc_ref.shape[0] // HD
    live = work_ref[2, i]

    @pl.when(work_ref[3, i] == 1)
    def _():
        peak_ref[...] = jnp.full_like(peak_ref, MASKED)
        total_ref[...] = jnp.zeros_like(total_ref)
        acc_ref[...] = jnp.zeros_like(acc_ref)

    def block(partial):
        for h in range(heads):
            at = slice(HD * h, HD * (h + 1))
            s = dot(k_ref[0, at, :], q_ref[0, at, :], (0, 0))
            if partial:
                s = jnp.where(lax.broadcasted_iota(jnp.int32, s.shape, 0) < live, s, MASKED)
            before = peak_ref[h : h + 1, :]
            peak = jnp.maximum(before, jnp.max(s, axis=0, keepdims=True))
            p = jnp.exp(s - peak)
            shrink = jnp.exp(before - peak)
            peak_ref[h : h + 1, :] = peak
            total_ref[h : h + 1, :] = total_ref[h : h + 1, :] * shrink + jnp.sum(p, axis=0, keepdims=True)
            acc_ref[at, :] = acc_ref[at, :] * shrink + dot(v_ref[0, at, :], p.astype(BF16))

    @pl.when(live == ROW_BLOCK)
    def _():
        block(False)

    @pl.when((live > 0) & (live < ROW_BLOCK))
    def _():
        block(True)

    @pl.when(work_ref[4, i] == 1)
    def _():
        total = total_ref[...]
        some = total > 0
        inverse = jnp.where(some, 1.0 / jnp.where(some, total, 1.0), 0.0)
        lse_ref[0] = jnp.where(some, peak_ref[...] + jnp.log(jnp.where(some, total, 1.0)), MASKED)
        for h in range(heads):
            at = slice(HD * h, HD * (h + 1))
            o_ref[0, at, :] = (acc_ref[at, :] * inverse[h : h + 1, :]).astype(o_ref.dtype)


def cross_forward(work, q, k, v):
    examples, feats, length = q.shape
    q_spec = pl.BlockSpec((1, feats, length), lambda i, work: (work[0, i], 0, 0))
    k_spec = pl.BlockSpec((1, feats, ROW_BLOCK), lambda i, work: (work[0, i], 0, work[1, i]))
    l_spec = pl.BlockSpec((1, 8, length), lambda i, work: (work[0, i], 0, 0))
    return pl.pallas_call(
        cross_forward_kernel,
        grid_spec=pltpu.PrefetchScalarGridSpec(
            num_scalar_prefetch=1,
            grid=(work.shape[1],),
            in_specs=[q_spec, k_spec, k_spec],
            out_specs=[q_spec, l_spec],
            scratch_shapes=[
                pltpu.VMEM((8, length), F32),
                pltpu.VMEM((8, length), F32),
                pltpu.VMEM((feats, length), F32),
            ],
        ),
        out_shape=[
            jax.ShapeDtypeStruct((examples, feats, length), BF16),
            jax.ShapeDtypeStruct((examples, 8, length), F32),
        ],
        compiler_params=pltpu.CompilerParams(vmem_limit_bytes=48 << 20),
        cost_estimate=cost(30e-6 * PEAK_FLOPS, 16e6),
        name="cross_forward",
    )(work, q, k, v)


def cross_backward_kernel(
    work_ref, place_ref, q_ref, do0_ref, do1_ref, do2_ref, do3_ref, lse_ref, in0_ref, in1_ref, in2_ref, in3_ref,
    k_ref, v_ref, dq_ref, dkv_ref, acc_ref, do_ref, inner_ref,
):
    i = pl.program_id(0)
    feats = acc_ref.shape[0]
    heads = feats // HD
    live = work_ref[2, i]

    @pl.when(work_ref[3, i] == 1)
    def _():
        acc_ref[...] = jnp.zeros_like(acc_ref)
        for pieces, full_ref in (
            ((do0_ref, do1_ref, do2_ref, do3_ref), do_ref),
            ((in0_ref, in1_ref, in2_ref, in3_ref), inner_ref),
        ):
            for flip, piece_ref in enumerate(pieces):
                full_ref[:, strip(place_index(place_ref, flip), piece_ref.shape[2])] = piece_ref[0]

    def block(partial):
        for h in range(heads):
            at = slice(HD * h, HD * (h + 1))
            q, do, k, v = q_ref[0, at, :], do_ref[at, :], k_ref[0, at, :], v_ref[0, at, :]
            s = dot(k, q, (0, 0))
            p = jnp.exp(s - lse_ref[0, h : h + 1, :])
            if partial:
                p = jnp.where(lax.broadcasted_iota(jnp.int32, s.shape, 0) < live, p, 0.0)
            dp = dot(v, do, (0, 0))
            ds = (p * (dp - inner_ref[h : h + 1, :])).astype(BF16)
            acc_ref[at, :] += dot(k, ds)
            dkv_ref[0, :, at] = dot(ds, q, (1, 1)).astype(BF16)
            dkv_ref[0, :, feats + HD * h : feats + HD * (h + 1)] = dot(p.astype(BF16), do, (1, 1)).astype(BF16)

    @pl.when(live == ROW_BLOCK)
    def _():
        block(False)

    @pl.when((live > 0) & (live < ROW_BLOCK))
    def _():
        block(True)

    @pl.when(work_ref[4, i] == 1)
    def _():
        dq_ref[0] = acc_ref[...].T.astype(BF16)


def cross_backward(work, place, q, do, lse, inner, k, v):
    examples, feats, length = q.shape
    rows = k.shape[2]
    of_example = lambda *shape: pl.BlockSpec((1, *shape), lambda i, work, place: (work[0, i], 0, 0))
    k_spec = pl.BlockSpec((1, feats, ROW_BLOCK), lambda i, work, place: (work[0, i], 0, work[1, i]))
    d_spec = pl.BlockSpec((1, ROW_BLOCK, 2 * feats), lambda i, work, place: (work[0, i], work[1, i], 0))
    return pl.pallas_call(
        cross_backward_kernel,
        grid_spec=pltpu.PrefetchScalarGridSpec(
            num_scalar_prefetch=2,
            grid=(work.shape[1],),
            in_specs=[
                of_example(feats, length),
                *[of_example(feats, length // 4)] * 4,
                of_example(8, length),
                *[of_example(8, length // 4)] * 4,
                k_spec,
                k_spec,
            ],
            out_specs=[of_example(length, feats), d_spec],
            scratch_shapes=[
                pltpu.VMEM((feats, length), F32),
                pltpu.VMEM((feats, length), BF16),
                pltpu.VMEM((8, length), F32),
            ],
        ),
        out_shape=[
            jax.ShapeDtypeStruct((examples, length, feats), BF16),
            jax.ShapeDtypeStruct((examples, rows, 2 * feats), BF16),
        ],
        compiler_params=pltpu.CompilerParams(vmem_limit_bytes=48 << 20),
        cost_estimate=cost(45e-6 * PEAK_FLOPS, 24e6),
        name="cross_backward",
    )(work, place, q, *do, lse, *inner, k, v)


def memory_backward_kernel(
    live_ref, own_ref, other_ref, dkv_ref, wt_ref, out_ref, out_other_ref, g_ref, sum_ref
):
    e, j = pl.program_id(0), pl.program_id(1)
    own_blocks = pl.num_programs(1) // 2

    @pl.when((e == 0) & (j == 0))
    def _():
        sum_ref[...] = jnp.zeros_like(sum_ref)

    for mine, rows_ref, to_ref in ((j < own_blocks, own_ref, out_ref), (j >= own_blocks, other_ref, out_other_ref)):

        @pl.when(mine & (live_ref[e, j] > 0))
        def _():
            dkv = dkv_ref[0]
            sum_ref[...] += dot(rows_ref[0], dkv, (0, 0))
            to_ref[0] = dot(dkv, wt_ref[...]).astype(BF16)

        @pl.when(mine & (live_ref[e, j] == 0))
        def _():
            to_ref[0] = jnp.zeros_like(to_ref[0])

    @pl.when((e == pl.num_programs(0) - 1) & (j == pl.num_programs(1) - 1))
    def _():
        g_ref[...] = sum_ref[...].astype(BF16)


def memory_backward(live, own, other, dkv, wt):
    examples, count, model = own.shape
    width = dkv.shape[2]
    half = count // ROW_BLOCK
    row_spec = lambda first: pl.BlockSpec(
        (1, ROW_BLOCK, model), lambda e, j, live: (e, jnp.clip(j - first, 0, half - 1), 0)
    )
    d_spec = pl.BlockSpec((1, ROW_BLOCK, width), lambda e, j, live: (e, j, 0))
    w_spec = pl.BlockSpec(wt.shape, lambda e, j, live: (0, 0))
    return pl.pallas_call(
        memory_backward_kernel,
        grid_spec=pltpu.PrefetchScalarGridSpec(
            num_scalar_prefetch=1,
            grid=(examples, 2 * half),
            in_specs=[row_spec(0), row_spec(half), d_spec, w_spec],
            out_specs=[row_spec(0), row_spec(half), pl.BlockSpec((model, width), lambda e, j, live: (0, 0))],
            scratch_shapes=[pltpu.VMEM((model, width), F32)],
        ),
        out_shape=[
            jax.ShapeDtypeStruct(own.shape, BF16),
            jax.ShapeDtypeStruct(own.shape, BF16),
            jax.ShapeDtypeStruct((model, width), BF16),
        ],
        compiler_params=pltpu.CompilerParams(vmem_limit_bytes=48 << 20),
        cost_estimate=cost(18e-6 * PEAK_FLOPS, 30e6),
        name="memory_backward",
    )(live, own, other, dkv, wt)


def self_output_kernel(
    place_ref, x_ref, o0_ref, o1_ref, o2_ref, o3_ref, mine_ref, other_ref, gain_ref,
    n2_ref, q_ref, x1_ref, own_o_ref, wo_ref, wq_ref,
    rows_ref,
):
    core = jnp.bitwise_and(place_ref[0], 1)
    feats = wq_ref.shape[1]
    width = o0_ref.shape[1]
    own = x1_ref.shape[1]

    @pl.when(pl.program_id(0) == 0)
    def _():
        for i, from_ref in ((core, mine_ref), (1 - core, other_ref)):
            wo_ref[:, strip(i, feats)] = from_ref[:, feats:]
        for i, from_ref in enumerate((mine_ref, other_ref)):
            for at in range(0, feats, LANES):
                wq_ref[i, at : at + LANES, :] = from_ref[:, at : at + LANES].T

    x1 = x_ref[0].astype(F32)
    for flip, o_ref in enumerate((o0_ref, o1_ref, o2_ref, o3_ref)):
        heads = strip(place_index(place_ref, flip), width)
        x1 += dot(o_ref[0], wo_ref[heads, :], (0, 0))
        own_o_ref[0, heads, :] = o_ref[0, :, strip(place_ref[0], own)]
    n2 = root_norm(x1, gain_ref[...]).astype(BF16)
    n2_ref[0] = n2
    q_ref[0] = dot(wq_ref[0], n2, (1, 1)).astype(BF16)
    rows_ref[...] = x1
    x1_ref[0] = rows_ref[strip(place_ref[0], own), :]


def self_output_stage(place, x, pieces, mine, other, gain):
    examples, length, model = x.shape
    own, feats, width = length // 4, model // 2, pieces[0].shape[1]
    whole = lambda *shape: pl.BlockSpec(shape, lambda e: (0,) * len(shape))
    per = lambda *shape: pl.BlockSpec((1, *shape), lambda e: (e, 0, 0))
    array = jax.ShapeDtypeStruct
    return pl.pallas_call(
        self_output_kernel,
        grid=(examples,),
        in_specs=[pl.BlockSpec(memory_space=pltpu.SMEM), per(length, model)]
        + [per(width, length)] * 4
        + [whole(*mine.shape), whole(*other.shape), whole(1, model)],
        out_specs=[
            per(length, model),
            per(feats, length),
            per(own, model),
            per(model, own),
            whole(model, model),
            whole(2, feats, model),
        ],
        out_shape=[
            array((examples, length, model), BF16),
            array((examples, feats, length), BF16),
            array((examples, own, model), F32),
            array((examples, model, own), BF16),
            array((model, model), BF16),
            array((2, feats, model), BF16),
        ],
        scratch_shapes=[pltpu.VMEM((length, model), F32)],
        compiler_params=pltpu.CompilerParams(vmem_limit_bytes=48 << 20),
        cost_estimate=cost(6e-6 * PEAK_FLOPS, 10e6),
        name="self_output_stage",
    )(place, x, *pieces, mine, other, gain)


def combine_kernel(place_ref, o_ref, came_ref, lse_ref, other_lse_ref, chip_ref, total_ref):
    row = lax.shift_right_logical(place_ref[0], 1)
    here = strip(row, came_ref.shape[2])
    one, two = lse_ref[0], other_lse_ref[0]
    peak = jnp.maximum(one, two)
    total_ref[0] = peak + jnp.log(jnp.exp(one - peak) + jnp.exp(two - peak))
    own_weight = jnp.exp(lse_ref[0, :, here] - total_ref[0, :, here])
    other_weight = jnp.exp(other_lse_ref[0, :, here] - total_ref[0, :, here])
    for h in range(o_ref.shape[1] // HD):
        at = slice(HD * h, HD * (h + 1))
        one = o_ref[0, at, here].astype(F32) * own_weight[h : h + 1, :]
        chip_ref[0, at, :] = (one + came_ref[0, at, :].astype(F32) * other_weight[h : h + 1, :]).astype(BF16)


def combine(place, o, came, lse, other_lse):
    examples, feats, length = o.shape
    per = lambda *shape: pl.BlockSpec((1, *shape), lambda e: (e, 0, 0))
    return pl.pallas_call(
        combine_kernel,
        grid=(examples,),
        in_specs=[
            pl.BlockSpec(memory_space=pltpu.SMEM),
            per(feats, length),
            per(feats, length // 2),
            per(8, length),
            per(8, length),
        ],
        out_specs=[per(feats, length // 2), per(8, length)],
        out_shape=[
            jax.ShapeDtypeStruct((examples, feats, length // 2), BF16),
            jax.ShapeDtypeStruct((examples, 8, length), F32),
        ],
        compiler_params=pltpu.CompilerParams(vmem_limit_bytes=24 << 20),
        cost_estimate=cost(2e-6 * PEAK_FLOPS, 3e6),
        name="combine",
    )(place, o, came, lse, other_lse)


def norm_back(values, gain, grad):
    scale = lax.rsqrt(jnp.mean(values * values, axis=-1, keepdims=True) + NORM_EPS)
    pulled = grad * gain
    inner = jnp.mean(values * pulled, axis=-1, keepdims=True)
    back = scale * pulled - values * (scale * scale * scale * inner)
    return back, jnp.sum(grad * values * scale, axis=0, keepdims=True)


def feed_forward_kernel(
    place_ref, x1_ref, mine_ref, other_ref, dy_ref, gain_ref, wo_ref, gate_ref, up_ref, down_ref,
    out_ref, dx2_ref, doc_mine_ref, doc_other_ref, inner_mine_ref, inner_other_ref,
    g_ref, g_sent_ref, g_down_ref, g_down_sent_ref, g_out_ref, g_out_sent_ref, g_gain_ref,
    x2_ref, n3_ref, sum_ref, dn3_ref, g_full_ref, *, piece,
):
    i = pl.program_id(0)
    core = jnp.bitwise_and(place_ref[0], 1)
    examples, feats, own = mine_ref.shape

    def deal(low, high, keep_ref, sent_ref):
        keep_ref[...] = jnp.where(core == 0, low, high).astype(BF16)
        sent_ref[...] = jnp.where(core == 0, high, low).astype(BF16)
    sides = ((core, mine_ref, doc_mine_ref, inner_mine_ref), (1 - core, other_ref, doc_other_ref, inner_other_ref))

    @pl.when(i == 0)
    def _():
        for e in range(examples):
            x2 = x1_ref[own * e : own * (e + 1), :]
            for side, o_ref, *_ in sides:
                x2 += dot(o_ref[e], wo_ref[strip(side, feats), :], (0, 0))
            x2_ref[own * e : own * (e + 1), :] = x2
        n3_ref[...] = root_norm(x2_ref[...], gain_ref[...]).astype(BF16)
        sum_ref[...] = jnp.zeros_like(sum_ref)
        dn3_ref[...] = jnp.zeros_like(dn3_ref)

    n3, dy = n3_ref[...], dy_ref[...]
    a, u = dot(n3, gate_ref[...]), dot(n3, up_ref[...])
    dh = dot(dy, down_ref[...], (1, 1))
    root = math.sqrt(2 / math.pi)
    bent = jnp.tanh(root * (a + 0.044715 * (a * a * a)))
    rise = 0.5 * (1.0 + bent)
    gelu = a * rise
    slope = rise + 0.5 * a * (1.0 - bent * bent) * (root * (1.0 + 3 * 0.044715 * (a * a)))
    hidden = (gelu * u).astype(BF16)
    da = (dh * u * slope).astype(BF16)
    du = (dh * gelu).astype(BF16)
    sum_ref[...] += dot(hidden, down_ref[...])
    g_down = dot(hidden, dy, (0, 0))
    pieces = g_down.reshape(g_down.shape[0] // (2 * piece), 2, piece, g_down.shape[1])
    deal(*(pieces[:, side].reshape(g_down_ref.shape) for side in range(2)), g_down_ref, g_down_sent_ref)
    deal(dot(n3, da, (0, 0)), dot(n3, du, (0, 0)), g_ref, g_sent_ref)
    dn3_ref[...] += dot(da, gate_ref[...], (1, 1)) + dot(du, up_ref[...], (1, 1))

    @pl.when(i == pl.num_programs(0) - 1)
    def _():
        x2 = x2_ref[...]
        out_ref[...] = (x2 + sum_ref[...]).astype(BF16)
        back, g_gain = norm_back(x2, gain_ref[...], dn3_ref[...])
        g_gain_ref[...] = g_gain
        dx2 = dy_ref[...].astype(F32) + back
        dx2_ref[...] = dx2
        n3_ref[...] = dx2.astype(BF16)
        for side, o_ref, doc_ref, inner_ref in sides:
            heads = strip(side, feats)
            total = jnp.zeros((feats, wo_ref.shape[1]), F32)
            inner_ref[...] = jnp.zeros_like(inner_ref)
            for e in range(examples):
                dx2r = n3_ref[own * e : own * (e + 1), :]
                total += dot(o_ref[e], dx2r)
                doc = dot(wo_ref[heads, :], dx2r, (1, 1)).astype(BF16)
                doc_ref[e] = doc
                product = doc.astype(F32) * o_ref[e].astype(F32)
                for h in range(feats // HD):
                    inner_ref[e, h : h + 1, :] = jnp.sum(product[HD * h : HD * (h + 1)], axis=0, keepdims=True)
            g_full_ref[heads, :] = total
        deal(g_full_ref[:, :feats], g_full_ref[:, feats:], g_out_ref, g_out_sent_ref)


def feed_forward(place, x1, mine, other, dy, gain, wide_w, down, piece):
    tokens, model = x1.shape
    examples, feats, own = mine.shape
    hidden = down.shape[0]
    part = 256
    whole = lambda *shape: pl.BlockSpec(shape, lambda i: (0,) * len(shape))
    first = model // part
    array = jax.ShapeDtypeStruct
    return pl.pallas_call(
        functools.partial(feed_forward_kernel, piece=piece),
        grid=(hidden // part,),
        in_specs=[
            pl.BlockSpec(memory_space=pltpu.SMEM),
            whole(tokens, model),
            whole(*mine.shape),
            whole(*other.shape),
            whole(tokens, model),
            whole(1, model),
            whole(model, model),
            pl.BlockSpec((model, part), lambda i: (0, first + i)),
            pl.BlockSpec((model, part), lambda i: (0, first + hidden // part + i)),
            pl.BlockSpec((part, model), lambda i: (i, 0)),
        ],
        out_specs=[
            whole(tokens, model),
            whole(tokens, model),
            whole(*mine.shape),
            whole(*mine.shape),
            whole(examples, 8, own),
            whole(examples, 8, own),
            *[pl.BlockSpec((model, part), lambda i: (0, i))] * 2,
            *[pl.BlockSpec((part // 2, model), lambda i: (i, 0))] * 2,
            *[whole(model, feats)] * 2,
            whole(1, model),
        ],
        out_shape=[
            array((tokens, model), BF16),
            array((tokens, model), F32),
            array(mine.shape, BF16),
            array(mine.shape, BF16),
            array((examples, 8, own), F32),
            array((examples, 8, own), F32),
            *[array((model, hidden), BF16)] * 2,
            *[array((hidden // 2, model), BF16)] * 2,
            *[array((model, feats), BF16)] * 2,
            array((1, model), F32),
        ],
        scratch_shapes=[
            pltpu.VMEM((tokens, model), F32),
            pltpu.VMEM((tokens, model), BF16),
            pltpu.VMEM((tokens, model), F32),
            pltpu.VMEM((tokens, model), F32),
            pltpu.VMEM((model, model), F32),
        ],
        compiler_params=pltpu.CompilerParams(vmem_limit_bytes=48 << 20),
        cost_estimate=cost(20e-6 * PEAK_FLOPS, 24e6),
        name="feed_forward",
    )(place, x1, mine, other, dy, gain, wide_w, wide_w, wide_w, down)


def self_output_back_kernel(
    place_ref, mine_ref, other_ref, wq_ref, x1_ref, gain_ref, dx2_ref, own_o_ref, wo_ref,
    dx1_ref, do_mine_ref, do_pair_ref, do_across_ref, g_keep_ref, g_sent_ref, g_gain_ref,
    sum_ref, do_ref,
):
    e = pl.program_id(0)
    core, row = jnp.bitwise_and(place_ref[0], 1), lax.shift_right_logical(place_ref[0], 1)
    width, feats = do_mine_ref.shape[1], do_across_ref.shape[1]

    @pl.when(e == 0)
    def _():
        sum_ref[...] = jnp.zeros_like(sum_ref)
        g_gain_ref[...] = jnp.zeros_like(g_gain_ref)

    dn2 = dot(mine_ref[0], wq_ref[0]) + dot(other_ref[0], wq_ref[1])
    back, g_gain = norm_back(x1_ref[0], gain_ref[...], dn2)
    g_gain_ref[...] += g_gain
    dx1 = dx2_ref[0] + back
    dx1_ref[0] = dx1
    dx1r = dx1.astype(BF16)
    do_ref[...] = dot(wo_ref[...], dx1r, (1, 1)).astype(BF16)
    do_mine_ref[0] = do_ref[strip(place_ref[0], width), :]
    do_pair_ref[0] = do_ref[strip(place_index(place_ref, 1), width), :]
    do_across_ref[0] = do_ref[strip(1 - row, feats), :]
    sum_ref[...] += dot(own_o_ref[0], dx1r)

    @pl.when(e == pl.num_programs(0) - 1)
    def _():
        g_keep_ref[...] = sum_ref[:, strip(core, feats)].astype(BF16)
        g_sent_ref[...] = sum_ref[:, strip(1 - core, feats)].astype(BF16)


def self_output_back(place, mine, other, wq, x1, gain, dx2, own_o, wo):
    examples, own, model = x1.shape
    feats = mine.shape[2]
    whole = lambda *shape: pl.BlockSpec(shape, lambda e: (0,) * len(shape))
    per = lambda *shape: pl.BlockSpec((1, *shape), lambda e: (e, 0, 0))
    array = jax.ShapeDtypeStruct
    return pl.pallas_call(
        self_output_back_kernel,
        grid=(examples,),
        in_specs=[
            pl.BlockSpec(memory_space=pltpu.SMEM),
            per(own, feats),
            per(own, feats),
            whole(*wq.shape),
            per(own, model),
            whole(1, model),
            per(own, model),
            per(model, own),
            whole(model, model),
        ],
        out_specs=[
            per(own, model),
            *[per(model // 4, own)] * 2,
            per(feats, own),
            *[whole(model, feats)] * 2,
            whole(1, model),
        ],
        out_shape=[
            array((examples, own, model), F32),
            *[array((examples, model // 4, own), BF16)] * 2,
            array((examples, feats, own), BF16),
            *[array((model, feats), BF16)] * 2,
            array((1, model), F32),
        ],
        scratch_shapes=[pltpu.VMEM((model, model), F32), pltpu.VMEM((model, own), BF16)],
        compiler_params=pltpu.CompilerParams(vmem_limit_bytes=48 << 20),
        cost_estimate=cost(4e-6 * PEAK_FLOPS, 8e6),
        name="self_output_back",
    )(place, mine, other, wq, x1, gain, dx2, own_o, wo)


def fold_rows(rows, target, columns):
    rest = rows * columns // target
    tile = 16
    if rows % tile or rows // tile * LANES != rest or columns // LANES * tile != target:
        return (lambda b: b.reshape(*b.shape[:-2], target, rest)), (lambda b: b.reshape(rows, columns))

    def swap(b, down, across):
        b = b.reshape(*b.shape[:-2], down, tile, across, LANES)
        return jnp.swapaxes(b, -4, -2).reshape(*b.shape[:-4], across * tile, down * LANES)

    return (lambda b: swap(b, rows // tile, columns // LANES)), (lambda b: swap(b, target // tile, rest // LANES))


def local(
    dec_input,
    enc_out,
    enc_len,
    cotangent,
    self_query,
    self_key,
    self_value,
    self_output,
    cross_query,
    cross_key,
    cross_value,
    cross_output,
    ffn_gate,
    ffn_up,
    ffn_down,
    self_gain,
    cross_gain,
    ffn_gain,
    bias_table,
):
    place = lax.axis_index("narrow")
    row, core = place // 2, place % 2
    wide = lax.axis_size("wide")
    examples, own, model = dec_input.shape
    length = 4 * own
    heads = model // HD
    own_heads = heads // 4
    memory_rows = enc_out.shape[1]
    share = self_query.shape[0]

    half = lambda w: part_of(w.astype(BF16), core, 2, 1)
    own_qkv = jnp.concatenate(
        [part_of(w.astype(BF16), place, 4, 1) for w in (self_query, self_key, self_value)], 1
    )
    own_qkv = jnp.pad(own_qkv, ((0, 0), (0, -own_qkv.shape[1] % LANES)))
    small = jnp.stack([self_gain, cross_gain, ffn_gain, jnp.pad(bias_table, (0, share - bias_table.shape[0]))], 1)
    small = jnp.pad(small.astype(BF16), ((0, 0), (0, LANES - 4)))
    feats = model // 2
    self_w, small = wide_gather(jnp.concatenate([own_qkv, small], 1), (own_qkv.shape[1], LANES))
    small_rows = small[:, :4].astype(F32).T
    gain_one, gain_two, gain_three = (small_rows[i : i + 1] for i in range(3))
    table = small_rows[3].reshape(wide, share)[:, : bias_table.shape[0]].reshape(BUCKETS, heads)

    both = ("wide", "narrow")
    quarter = lambda w: part_of(w.astype(BF16), place, 4, 0)
    ffn_in = lax.all_gather(
        jnp.concatenate([quarter(cross_output), quarter(ffn_gate), quarter(ffn_up)], 1), both, axis=0, tiled=True
    )
    down_w = lax.all_gather(quarter(ffn_down), both, axis=0, tiled=True)

    enc_other = pair_swap(enc_out)
    starts = (place * memory_rows + np.arange(memory_rows // ROW_BLOCK) * ROW_BLOCK).astype(jnp.int32)
    other_starts = starts + (1 - 2 * core) * memory_rows
    block_starts = jnp.concatenate([starts, other_starts])
    live = jnp.clip(enc_len[:, None] - block_starts[None, :], 0, ROW_BLOCK)

    x_all = narrow_gather(dec_input, 1, row, core)
    hot = jnp.asarray(bucket_table(length))
    distance_bias = jnp.dot(table.T, hot, precision=FULL_ACCURACY)
    vec = jnp.pad(part_of(distance_bias, place, 4, 0), ((0, 8 - own_heads), (0, 0)))
    qkv, self_o, self_lse, self_wt = self_forward(x_all, gain_one, self_w, vec, own_heads)
    across_o = across_swap(self_o)
    pieces = [self_o, pair_swap(self_o), across_o, pair_swap(across_o)]
    memory_w = shared_gather(jnp.concatenate([half(cross_key), half(cross_value)], 1), row, first=(self_o,))
    work = work_list(live)
    keys, values, memory_wt = memory_project(work, enc_out, enc_other, memory_w)
    query_out = after(jnp.concatenate([half(cross_query), half(self_output)], 1), self_o)
    mine_w = shared_gather(query_out, row)
    mine_w = after(mine_w, keys)
    other_w = pair_swap(mine_w)
    me = place.reshape(1).astype(jnp.int32)
    n2, cross_q, x1, own_o, self_out_w, cross_query_wt = self_output_stage(
        me, x_all, pieces, mine_w, other_w, gain_two
    )

    part_o, part_lse = cross_forward(work, cross_q, keys, values)
    came = across_swap(part_of(part_o, 1 - row, 2, 2))
    chip_o, lse = combine(me, part_o, came, part_lse, across_swap(part_lse))
    mine_o, other_o = part_of(chip_o, core, 2, 2), pair_swap(part_of(chip_o, 1 - core, 2, 2))

    tokens = examples * own
    down_rows = ffn_down.shape[0] // 2
    (
        layer_out, dx2, doc_mine, doc_other, inner_mine, inner_other,
        gate_up, gate_up_sent, down, down_sent, grad_co, co_sent, grad_gain_three,
    ) = feed_forward(
        me, x1.reshape(tokens, model), mine_o, other_o, cotangent.reshape(tokens, model), gain_three,
        ffn_in, down_w, down_rows,
    )
    layer_out, dx2 = layer_out.reshape(x1.shape), dx2.reshape(x1.shape)

    rows_of = lambda g: g.reshape(wide, share, -1)

    def from_all(mine, other):
        pair = pair_swap(other)
        return [mine, pair, across_swap(mine), across_swap(pair)]

    doc, inner = from_all(doc_mine, doc_other), from_all(inner_mine, inner_other)
    ffn = gate_up, pair_swap(gate_up_sent)
    by_y = lambda y: [part_of(g, y, 2, 1).astype(F32) for g in ffn]
    ffn_sent = sum(by_y(1 - row)).astype(BF16)
    down = plus(down, pair_swap(down_sent)).reshape(wide, down_rows, model)
    co = plus(grad_co, pair_swap(co_sent))
    doc, inner, ffn_sent, down, co = lax.optimization_barrier((doc, inner, ffn_sent, down, co))
    ffn_came, down = across_swap(ffn_sent), wide_scatter_x(down)
    part_dq, dkv = cross_backward(work, me, cross_q, doc, lse, inner, keys, values)
    part_dq, dkv, ffn_came, down = lax.optimization_barrier((part_dq, dkv, ffn_came, down))
    ffn = wide_scatter_x(rows_of(sum(by_y(row), ffn_came.astype(F32)).astype(BF16)))

    dq_came = across_swap(part_of(part_dq, 1 - row, 2, 1))
    enc_mine, enc_swapped, grad_memory = memory_backward(live, enc_out, enc_other, dkv, memory_wt)
    enc_came = pair_swap(enc_swapped)
    dq_came, grad_memory, ffn = lax.optimization_barrier((dq_came, grad_memory, ffn))
    down_came = across_swap(part_of(down, 1 - row, 2, 1))
    ffn_sum = wide_scatter_z(ffn)
    chip_dq = plus(part_of(part_dq, row, 2, 1), dq_came)
    dq_mine, dq_other = part_of(chip_dq, core, 2, 1), pair_swap(part_of(chip_dq, 1 - core, 2, 1))
    grad_cross_query = jnp.einsum("etd,etf->df", n2, part_dq, preferred_element_type=F32).astype(BF16)
    late = x_swap(jnp.concatenate([rows_of(g) for g in (grad_cross_query, grad_memory, co)], 2))
    dx1, do_mine, do_pair, do_across, grad_so, so_sent, grad_gain_two = self_output_back(
        me, dq_mine, dq_other, cross_query_wt, x1, gain_two, dx2, own_o, self_out_w
    )
    do_across, do_pair, down_came = lax.optimization_barrier((do_across, do_pair, down_came))

    do_came = across_swap(do_across)
    do = [do_mine, pair_swap(do_pair), part_of(do_came, core, 2, 1), pair_swap(part_of(do_came, 1 - core, 2, 1))]
    so = rows_of(plus(grad_so, pair_swap(so_sent)))
    down = plus(part_of(down, row, 2, 1), down_came)
    do, ffn_sum, so, late, down = lax.optimization_barrier((do, ffn_sum, so, late, down))
    fold, unfold = fold_rows(down.shape[1], share, model)
    late = z_swap(jnp.concatenate([total(late), fold(down)], 2))
    so_came = across_swap(part_of(so, 1 - row, 2, 1))
    part_dn1, grad_self, dvec, grad_gain_one = self_backward(
        me, x_all, gain_one, qkv, do, self_lse, self_wt, vec, own_heads
    )
    part_dn1, grad_self, so_came, late = lax.optimization_barrier((part_dn1, grad_self, so_came, late))

    own_table = jnp.dot(hot, dvec[:own_heads].T, precision=FULL_ACCURACY)
    grad_table = lax.dynamic_update_slice_in_dim(
        jnp.zeros((BUCKETS, heads), F32), own_table, place * own_heads, 1
    )
    small = [g.reshape(wide, -1) for g in (grad_gain_one, grad_gain_two, grad_gain_three, grad_table)]
    small = jnp.concatenate(small, 1).astype(BF16)
    small_count = small.shape[1]
    small = jnp.pad(small, ((0, 0), (0, share // 2 * LANES - small_count))).reshape(wide, -1, LANES)
    so = plus(part_of(so, row, 2, 1), so_came)
    self_width = grad_self.shape[1]
    self_halves = grad_self.reshape(wide, 2, share // 2, self_width)
    last = x_swap(jnp.concatenate([self_halves[:, 0], self_halves[:, 1], so, small], 2))
    by_core = part_dn1.reshape(examples, 2, 2, own, model)
    column = plus(part_of(by_core, core, 2, 2).astype(F32), pair_swap(part_of(by_core, 1 - core, 2, 2)))
    dn1_sent = part_of(column, 1 - row, 2, 1).astype(BF16)
    enc_grad = plus(enc_mine, enc_came)
    sums = jnp.concatenate([ffn_sum, total(late)], 1)
    last, dn1_sent, enc_grad, sums = lax.optimization_barrier((last, dn1_sent, enc_grad, sums))
    last, dn1_came, sums_came = z_swap(total(last)), across_swap(dn1_sent), across_swap(sums)
    last, dn1_came, sums_came = lax.optimization_barrier((last, dn1_came, sums_came))
    last_sum = total(last)
    last_came = across_swap(last_sum)
    dn1 = plus(part_of(column, row, 2, 1), dn1_came)
    grad_in, _ = norm_back(
        dec_input.reshape(tokens, model).astype(F32), gain_one, dn1.reshape(tokens, model)
    )
    input_grad = (dx1 + grad_in.reshape(x1.shape)).astype(BF16)

    bounds = np.cumsum([0, ffn_sum.shape[1], 4 * feats])
    low, high = in_order(row, sums, sums_came)
    sums = jnp.concatenate(
        [
            low[:, : bounds[1]],
            high[:, : bounds[1]],
            plus(sums[:, bounds[1] : bounds[2]], sums_came[:, bounds[1] : bounds[2]]),
            low[:, bounds[2] :],
            high[:, bounds[2] :],
        ],
        1,
    )
    parts = in_order(core, sums, pair_swap(sums))
    gate_sum, up_sum = (part[:, : 2 * bounds[1]] for part in parts)
    cq_sum, ck_sum, cv_sum, co_sum = (
        jnp.concatenate([part[:, 2 * bounds[1] + feats * i : 2 * bounds[1] + feats * (i + 1)] for part in parts], 1)
        for i in range(4)
    )
    down_sum = [jnp.split(part[:, 2 * bounds[1] + 4 * feats :], 2, 1) for part in parts]
    down_sum = jnp.concatenate([unfold(half) for part in down_sum for half in part], 0)

    last = jnp.stack(in_order(row, last_sum, last_came))
    low, high = in_order(core, last, pair_swap(last))
    halves = lambda part: jnp.concatenate([part[:, :self_width], part[:, self_width : 2 * self_width]], 0)
    self_sum = [halves(part[y]) for y in range(2) for part in (low, high)]
    q_sum, k_sum, v_sum = (
        jnp.concatenate([part[:, own_heads * HD * i : own_heads * HD * (i + 1)] for part in self_sum], 1)
        for i in range(3)
    )
    so_sum = jnp.concatenate(
        [part[:, :, 2 * self_width : 2 * self_width + feats].reshape(share, -1) for part in (low, high)], 1
    )
    small_sum = sum(part[y, :, 2 * self_width + feats :].astype(F32) for part in (low, high) for y in range(2))
    small_sum = small_sum.reshape(-1)[:small_count]
    f = lambda a: a.astype(F32)
    return (
        layer_out,
        input_grad,
        enc_grad,
        *(f(g) for g in (q_sum, k_sum, v_sum, so_sum, cq_sum, ck_sum, cv_sum, co_sum, gate_sum, up_sum, down_sum)),
        small_sum[:share],
        small_sum[share : 2 * share],
        small_sum[2 * share : 3 * share],
        small_sum[3 * share :],
    )


def solution(mesh):
    rows = P("wide", "narrow", None)
    weight, vector = P("wide", None), P("wide")
    return jax.shard_map(
        local,
        mesh=mesh,
        in_specs=(rows, rows, vector, rows, *[weight] * 11, *[vector] * 4),
        out_specs=(rows, rows, rows, *[weight] * 11, *[vector] * 4),
        check_vma=False,
    )
```

```python
import functools
import math

import jax
import jax.numpy as jnp
import numpy as np
from jax import lax
from jax.experimental import pallas as pl
from jax.experimental.pallas import tpu as pltpu
from jax.sharding import PartitionSpec as P

HD = 64
BUCKETS = 32
MAXDIST = 128
NORM_EPS = 1e-06
MASKED = -1e30
LANES = 128
ROW_BLOCK = 512
PEAK_FLOPS = 1.15e15
FULL_ACCURACY = lax.Precision.HIGHEST
F32 = jnp.float32
BF16 = jnp.bfloat16

PAIR = ((0, 1), (1, 0), (2, 3), (3, 2))
ACROSS = ((0, 2), (2, 0), (1, 3), (3, 1))


def bucket_table(length):
    exact = BUCKETS // 2
    hot = np.zeros((BUCKETS, length), np.float32)
    for distance in range(length):
        bucket = distance
        if distance >= exact:
            scaled = math.log(distance / exact) / math.log(MAXDIST / exact) * (BUCKETS - exact)
            bucket = min(exact + math.floor(scaled), BUCKETS - 1)
        hot[bucket, distance] = 1.0
    return hot


def dot(left, right, contract=(1, 0)):
    return lax.dot_general(
        left, right, (((contract[0],), (contract[1],)), ((), ())), preferred_element_type=F32
    )


def root_norm(values, gain):
    return values * lax.rsqrt(jnp.mean(values * values, axis=-1, keepdims=True) + NORM_EPS) * gain


def pair_swap(value):
    return lax.ppermute(value, "narrow", PAIR)


def across_swap(value):
    return lax.ppermute(value, "narrow", ACROSS)


def in_order(flag, mine, other):
    first = flag == 0
    return jnp.where(first, mine, other), jnp.where(first, other, mine)


def narrow_gather(value, axis, row, core):
    low, high = in_order(row, value, across_swap(value))
    column = jnp.stack([low, high], axis)
    low, high = in_order(core, column, pair_swap(column))
    full = jnp.stack([low, high], axis + 1)
    shape = list(value.shape)
    shape[axis] *= 4
    return full.reshape(shape)


def plus(mine, came):
    return (mine.astype(F32) + came.astype(F32)).astype(mine.dtype)


def part_of(value, index, parts, axis):
    size = value.shape[axis] // parts
    return lax.dynamic_slice_in_dim(value, index * size, size, axis)


LINE = 4
BESIDE = tuple((i, i ^ 1) for i in range(2 * LINE))


def along(step):
    return [(2 * z + x, 2 * ((z + step) % LINE) + x) for z in range(LINE) for x in range(2)]


def by_planes():
    return lax.axis_size("wide") == 2 * LINE


def assemble_kernel(widths, order_ref, *refs):
    pieces, outs = refs[: 2 * LINE], refs[2 * LINE :]
    for i, piece in enumerate(pieces):
        at = 0
        for width, out in zip(widths, outs):
            out[order_ref[i]] = piece[:, at : at + width]
            at += width


def after(value, *others):
    return lax.optimization_barrier((value, *others))[0]


def wide_gather(block, widths, first=()):
    rows = block.shape[0]
    if not by_planes():
        full = lax.all_gather(block, "wide", axis=0, tiled=True)
        bounds = np.cumsum([0, *widths])
        return [full[:, a:b] for a, b in zip(bounds[:-1], bounds[1:])]
    z, x = lax.axis_index("wide") // 2, lax.axis_index("wide") % 2
    line = [block] + [lax.ppermute(block, "wide", along(step)) for step in range(1, LINE)]
    line = after(line, *first)
    pieces = line + [lax.ppermute(piece, "wide", BESIDE) for piece in line]
    places = (z - np.arange(LINE)) % LINE * 2
    order = jnp.concatenate([places + x, places + 1 - x]).astype(jnp.int32)
    outs = pl.pallas_call(
        functools.partial(assemble_kernel, widths),
        in_specs=[pl.BlockSpec(memory_space=pltpu.SMEM)] + [pl.BlockSpec(memory_space=pltpu.VMEM)] * len(pieces),
        out_specs=[pl.BlockSpec(memory_space=pltpu.VMEM)] * len(widths),
        out_shape=[jax.ShapeDtypeStruct((2 * LINE, rows, width), block.dtype) for width in widths],
        compiler_params=pltpu.CompilerParams(vmem_limit_bytes=16 << 20),
        name="assemble",
    )(order, *pieces)
    return [out.reshape(2 * LINE * rows, out.shape[2]) for out in outs]


def shared_gather(block, row, first=()):
    rows, width = block.shape
    (full,) = wide_gather(part_of(block, row, 2, 0), (width,), first)
    halves = full.reshape(-1, rows // 2, width)
    return jnp.stack(in_order(row, halves, across_swap(halves)), 1).reshape(-1, width)


def pick(value, index, axis):
    return lax.dynamic_index_in_dim(value, index, axis, keepdims=False)


def x_swap(blocks):
    if not by_planes():
        return (blocks,)
    x = lax.axis_index("wide") % 2
    planes = blocks.reshape(LINE, 2, *blocks.shape[1:])
    return pick(planes, x, 1), lax.ppermute(pick(planes, 1 - x, 1), "wide", BESIDE)


def z_swap(planes):
    if not by_planes():
        shape = planes.shape
        return (
            lax.psum_scatter(
                planes.reshape(shape[0] * shape[1], *shape[2:]), "wide", scatter_dimension=0, tiled=True
            ),
        )
    z = lax.axis_index("wide") // 2
    sent = [pick(planes, (z + step) % LINE, 0) for step in range(1, LINE)]
    return pick(planes, z, 0), *(lax.ppermute(s, "wide", along(i + 1)) for i, s in enumerate(sent))


def total(parts):
    return sum((part.astype(F32) for part in parts[1:]), parts[0].astype(F32)).astype(parts[0].dtype)


def wide_scatter_x(blocks):
    return total(x_swap(blocks))


def wide_scatter_z(planes):
    return total(z_swap(planes))


def wide_scatter(blocks):
    return wide_scatter_z(wide_scatter_x(blocks))


def place_index(place_ref, flip):
    return jnp.bitwise_xor(place_ref[0], flip)


def strip(index, size):
    return pl.ds(pl.multiple_of(index * size, size), size)


def transpose_columns(weight_ref, out_ref):
    for i in range(0, weight_ref.shape[1], LANES):
        out_ref[i : i + LANES, :] = weight_ref[:, i : i + LANES].T


def cost(flops, moved):
    return pl.CostEstimate(flops=int(flops), bytes_accessed=int(moved), transcendentals=0)


def position_bias(vec_ref, bias_ref):
    heads, size, _ = bias_ref.shape
    key = lax.broadcasted_iota(jnp.int32, (size, size), 0)
    query = lax.broadcasted_iota(jnp.int32, (size, size), 1)
    for h in range(heads):
        rows = jnp.broadcast_to(vec_ref[h : h + 1, :], (size, size))
        rolled = pltpu.roll(rows, 0, 1, stride=1, stride_axis=0)
        bias_ref[h] = jnp.where(key <= query, rolled, MASKED)


def self_forward_kernel(
    x_ref, gain_ref, w_ref, vec_ref, qkv_ref, out_ref, lse_ref, wt_ref, bias_ref
):
    heads = bias_ref.shape[0]
    width = heads * HD

    @pl.when(pl.program_id(0) == 0)
    def _():
        transpose_columns(w_ref, wt_ref)
        position_bias(vec_ref, bias_ref)

    normed = root_norm(x_ref[0].astype(F32), gain_ref[...]).astype(BF16)
    qkv = dot(wt_ref[...], normed, (1, 1)).astype(BF16)
    qkv_ref[0] = qkv
    lse_ref[...] = jnp.zeros_like(lse_ref)
    piece = lambda part, h: qkv[width * part + HD * h : width * part + HD * (h + 1)]
    following = dot(piece(1, 0), piece(0, 0), (0, 0))
    for h in range(heads):
        s = following + bias_ref[h]
        if h + 1 < heads:
            following = dot(piece(1, h + 1), piece(0, h + 1), (0, 0))
        peak = jnp.max(s, axis=0, keepdims=True)
        raised = jnp.exp(s - peak)
        total = jnp.sum(raised, axis=0, keepdims=True)
        weight = (raised * (1.0 / total)).astype(BF16)
        out_ref[0, HD * h : HD * (h + 1), :] = dot(piece(2, h), weight).astype(BF16)
        lse_ref[0, h : h + 1, :] = peak + jnp.log(total)


def self_forward(x, gain, weight, vec, heads):
    examples, length, model = x.shape
    feats = weight.shape[1]
    whole = lambda *shape: pl.BlockSpec(shape, lambda e: (0,) * len(shape))
    per = lambda *shape: pl.BlockSpec((1, *shape), lambda e: (e, 0, 0))
    return pl.pallas_call(
        self_forward_kernel,
        grid=(examples,),
        in_specs=[
            per(length, model),
            whole(1, model),
            whole(*weight.shape),
            whole(*vec.shape),
        ],
        out_specs=[
            per(feats, length),
            per(heads * HD, length),
            per(8, length),
            whole(feats, model),
        ],
        out_shape=[
            jax.ShapeDtypeStruct((examples, feats, length), BF16),
            jax.ShapeDtypeStruct((examples, heads * HD, length), BF16),
            jax.ShapeDtypeStruct((examples, 8, length), F32),
            jax.ShapeDtypeStruct((feats, model), BF16),
        ],
        scratch_shapes=[pltpu.VMEM((heads, length, length), F32)],
        compiler_params=pltpu.CompilerParams(vmem_limit_bytes=48 << 20),
        cost_estimate=cost(9e-6 * PEAK_FLOPS, 8e6),
        name="self_forward",
    )(x, gain, weight, vec)


def self_backward_kernel(
    place_ref, x_ref, gain_ref, qkv_ref, do0_ref, do1_ref, do2_ref, do3_ref, lse_ref, wt_ref, vec_ref,
    dn_ref, gw_ref, dvec_ref, g_gain_ref,
    bias_ref, dsum_ref, dqkv_ref, do_ref, sum_ref,
):
    heads, size, _ = bias_ref.shape
    width = heads * HD
    e = pl.program_id(0)

    @pl.when(e == 0)
    def _():
        position_bias(vec_ref, bias_ref)
        dsum_ref[...] = jnp.zeros_like(dsum_ref)
        sum_ref[...] = jnp.zeros_like(sum_ref)
        dqkv_ref[...] = jnp.zeros_like(dqkv_ref)
        g_gain_ref[...] = jnp.zeros_like(g_gain_ref)

    for flip, piece_ref in enumerate((do0_ref, do1_ref, do2_ref, do3_ref)):
        do_ref[:, strip(place_index(place_ref, flip), piece_ref.shape[2])] = piece_ref[0]
    piece = lambda part, h: qkv_ref[0, width * part + HD * h : width * part + HD * (h + 1), :]
    out = lambda h: do_ref[HD * h : HD * (h + 1), :]
    products = lambda h: (dot(piece(1, h), piece(0, h), (0, 0)), dot(piece(2, h), out(h), (0, 0)))
    following = products(0)
    for h in range(heads):
        s, dp = following
        if h + 1 < heads:
            following = products(h + 1)
        p = jnp.exp(s + bias_ref[h] - lse_ref[0, h : h + 1, :])
        inner = jnp.sum(p * dp, axis=0, keepdims=True)
        ds = p * (dp - inner)
        dsum_ref[h] += ds
        ds = ds.astype(BF16)
        at = lambda part: slice(width * part + HD * h, width * part + HD * (h + 1))
        dqkv_ref[:, at(0)] = dot(piece(1, h), ds).T.astype(BF16)
        dqkv_ref[:, at(1)] = dot(ds, piece(0, h), (1, 1)).astype(BF16)
        dqkv_ref[:, at(2)] = dot(p.astype(BF16), out(h), (1, 1)).astype(BF16)
    dqkv = dqkv_ref[...]
    dn = dot(dqkv, wt_ref[...])
    dn_ref[0] = dn.astype(BF16)
    x = x_ref[0].astype(F32)
    scaled = x * lax.rsqrt(jnp.mean(x * x, axis=-1, keepdims=True) + NORM_EPS)
    g_gain_ref[...] += jnp.sum(dn * scaled, axis=0, keepdims=True)
    sum_ref[...] += dot((scaled * gain_ref[...]).astype(BF16), dqkv, (0, 0))

    @pl.when(e == pl.num_programs(0) - 1)
    def _():
        gw_ref[...] = sum_ref[...].astype(BF16)
        dvec_ref[...] = jnp.zeros_like(dvec_ref)
        for h in range(heads):
            back, count = dsum_ref[h], size
            while count > 8:
                count //= 2
                back = back[:count] + pltpu.roll(back[count:], size - count, 1)
            total = back[:1]
            for r in range(1, count):
                total = total + pltpu.roll(back[r : r + 1], size - r, 1)
            dvec_ref[h : h + 1, :] = total


def self_backward(place, x, gain, qkv, do, lse, wt, vec, heads):
    examples, length, model = x.shape
    feats = wt.shape[0]
    whole = lambda *shape: pl.BlockSpec(shape, lambda e: (0,) * len(shape))
    per = lambda *shape: pl.BlockSpec((1, *shape), lambda e: (e, 0, 0))
    return pl.pallas_call(
        self_backward_kernel,
        grid=(examples,),
        in_specs=[
            pl.BlockSpec(memory_space=pltpu.SMEM),
            per(length, model),
            whole(1, model),
            per(feats, length),
            *[per(heads * HD, length // 4)] * 4,
            per(8, length),
            whole(*wt.shape),
            whole(*vec.shape),
        ],
        out_specs=[per(length, model), whole(model, feats), whole(8, length), whole(1, model)],
        out_shape=[
            jax.ShapeDtypeStruct((examples, length, model), BF16),
            jax.ShapeDtypeStruct((model, feats), BF16),
            jax.ShapeDtypeStruct((8, length), F32),
            jax.ShapeDtypeStruct((1, model), F32),
        ],
        scratch_shapes=[
            pltpu.VMEM((heads, length, length), F32),
            pltpu.VMEM((heads, length, length), F32),
            pltpu.VMEM((length, feats), BF16),
            pltpu.VMEM((heads * HD, length), BF16),
            pltpu.VMEM((model, feats), F32),
        ],
        compiler_params=pltpu.CompilerParams(vmem_limit_bytes=48 << 20),
        cost_estimate=cost(16e-6 * PEAK_FLOPS, 12e6),
        name="self_backward",
    )(place, x, gain, qkv, *do, lse, wt, vec)


def work_list(live):
    examples, blocks = live.shape
    flat = live.reshape(-1)
    index = jnp.arange(flat.shape[0], dtype=jnp.int32)
    block = index % blocks
    visit = (flat > 0) | (block == 0)
    before = jnp.sum(jnp.where(visit[None, :] & (index[None, :] < index[:, None]), 1, 0), axis=1)
    ends = visit & ~jnp.any(
        visit[None, :] & (index[None, :] > index[:, None]) & (index[None, :] // blocks == index[:, None] // blocks), axis=1
    )
    chosen = (before[None, :] == index[:, None]) & visit[None, :]
    take = lambda values: jnp.sum(jnp.where(chosen, values[None, :], 0), axis=1)
    final = jnp.max(jnp.where(visit, index, 0))
    found = jnp.any(chosen, axis=1)
    at = jnp.where(found, take(index), final)
    rows = [at // blocks, at % blocks, take(flat), found & (at % blocks == 0), take(ends.astype(jnp.int32))]
    return jnp.stack([r.astype(jnp.int32) for r in rows])


def memory_project_kernel(work_ref, own_ref, other_ref, w_ref, k_ref, v_ref, wt_ref):
    i = pl.program_id(0)
    block, live = work_ref[1, i], work_ref[2, i]
    half = wt_ref.shape[0] // 2
    own_blocks = 2

    @pl.when(i == 0)
    def _():
        transpose_columns(w_ref, wt_ref)

    def project(rows):
        both = dot(wt_ref[...], rows, (1, 1)).astype(BF16)
        k_ref[0] = both[:half]
        v_ref[0] = both[half:]

    @pl.when((live > 0) & (block < own_blocks))
    def _():
        project(own_ref[0])

    @pl.when((live > 0) & (block >= own_blocks))
    def _():
        project(other_ref[0])


def memory_project(work, own, other, weight):
    examples, rows, model = own.shape
    half = rows // ROW_BLOCK
    feats = weight.shape[1] // 2
    row_spec = lambda first: pl.BlockSpec(
        (1, ROW_BLOCK, model), lambda i, work: (work[0, i], jnp.clip(work[1, i] - first, 0, half - 1), 0)
    )
    out_spec = pl.BlockSpec((1, feats, ROW_BLOCK), lambda i, work: (work[0, i], 0, work[1, i]))
    out = jax.ShapeDtypeStruct((examples, feats, 2 * rows), BF16)
    w_spec = lambda *shape: pl.BlockSpec(shape, lambda i, work: (0, 0))
    return pl.pallas_call(
        memory_project_kernel,
        grid_spec=pltpu.PrefetchScalarGridSpec(
            num_scalar_prefetch=1,
            grid=(work.shape[1],),
            in_specs=[row_spec(0), row_spec(half), w_spec(*weight.shape)],
            out_specs=[out_spec, out_spec, w_spec(2 * feats, model)],
        ),
        out_shape=[out, out, jax.ShapeDtypeStruct((2 * feats, model), BF16)],
        compiler_params=pltpu.CompilerParams(vmem_limit_bytes=48 << 20),
        cost_estimate=cost(12e-6 * PEAK_FLOPS, 12e6),
        name="memory_project",
    )(work, own, other, weight)


def cross_forward_kernel(work_ref, q_ref, k_ref, v_ref, o_ref, lse_ref, peak_ref, total_ref, acc_ref):
    i = pl.program_id(0)
    heads = acc_ref.shape[0] // HD
    live = work_ref[2, i]

    @pl.when(work_ref[3, i] == 1)
    def _():
        peak_ref[...] = jnp.full_like(peak_ref, MASKED)
        total_ref[...] = jnp.zeros_like(total_ref)
        acc_ref[...] = jnp.zeros_like(acc_ref)

    def scores(h):
        at = slice(HD * h, HD * (h + 1))
        return dot(k_ref[0, at, :], q_ref[0, at, :], (0, 0))

    def block(partial):
        following = scores(0)
        for h in range(heads):
            at = slice(HD * h, HD * (h + 1))
            s = following
            if h + 1 < heads:
                following = scores(h + 1)
            if partial:
                s = jnp.where(lax.broadcasted_iota(jnp.int32, s.shape, 0) < live, s, MASKED)
            before = peak_ref[h : h + 1, :]
            peak = jnp.maximum(before, jnp.max(s, axis=0, keepdims=True))
            p = jnp.exp(s - peak)
            shrink = jnp.exp(before - peak)
            peak_ref[h : h + 1, :] = peak
            total_ref[h : h + 1, :] = total_ref[h : h + 1, :] * shrink + jnp.sum(p, axis=0, keepdims=True)
            acc_ref[at, :] = acc_ref[at, :] * shrink + dot(v_ref[0, at, :], p.astype(BF16))

    @pl.when(live == ROW_BLOCK)
    def _():
        block(False)

    @pl.when((live > 0) & (live < ROW_BLOCK))
    def _():
        block(True)

    @pl.when(work_ref[4, i] == 1)
    def _():
        total = total_ref[...]
        some = total > 0
        inverse = jnp.where(some, 1.0 / jnp.where(some, total, 1.0), 0.0)
        lse_ref[0] = jnp.where(some, peak_ref[...] + jnp.log(jnp.where(some, total, 1.0)), MASKED)
        for h in range(heads):
            at = slice(HD * h, HD * (h + 1))
            o_ref[0, at, :] = (acc_ref[at, :] * inverse[h : h + 1, :]).astype(o_ref.dtype)


def cross_forward(work, q, k, v):
    examples, feats, length = q.shape
    q_spec = pl.BlockSpec((1, feats, length), lambda i, work: (work[0, i], 0, 0))
    k_spec = pl.BlockSpec((1, feats, ROW_BLOCK), lambda i, work: (work[0, i], 0, work[1, i]))
    l_spec = pl.BlockSpec((1, 8, length), lambda i, work: (work[0, i], 0, 0))
    return pl.pallas_call(
        cross_forward_kernel,
        grid_spec=pltpu.PrefetchScalarGridSpec(
            num_scalar_prefetch=1,
            grid=(work.shape[1],),
            in_specs=[q_spec, k_spec, k_spec],
            out_specs=[q_spec, l_spec],
            scratch_shapes=[
                pltpu.VMEM((8, length), F32),
                pltpu.VMEM((8, length), F32),
                pltpu.VMEM((feats, length), F32),
            ],
        ),
        out_shape=[
            jax.ShapeDtypeStruct((examples, feats, length), BF16),
            jax.ShapeDtypeStruct((examples, 8, length), F32),
        ],
        compiler_params=pltpu.CompilerParams(vmem_limit_bytes=48 << 20),
        cost_estimate=cost(30e-6 * PEAK_FLOPS, 16e6),
        name="cross_forward",
    )(work, q, k, v)


def cross_backward_kernel(
    work_ref, place_ref, q_ref, do0_ref, do1_ref, do2_ref, do3_ref, lse_ref, in0_ref, in1_ref, in2_ref, in3_ref,
    k_ref, v_ref, dq_ref, dkv_ref, acc_ref, do_ref, inner_ref,
):
    i = pl.program_id(0)
    feats = acc_ref.shape[0]
    heads = feats // HD
    live = work_ref[2, i]

    @pl.when(work_ref[3, i] == 1)
    def _():
        acc_ref[...] = jnp.zeros_like(acc_ref)
        for pieces, full_ref in (
            ((do0_ref, do1_ref, do2_ref, do3_ref), do_ref),
            ((in0_ref, in1_ref, in2_ref, in3_ref), inner_ref),
        ):
            for flip, piece_ref in enumerate(pieces):
                full_ref[:, strip(place_index(place_ref, flip), piece_ref.shape[2])] = piece_ref[0]

    def products(h):
        at = slice(HD * h, HD * (h + 1))
        return dot(k_ref[0, at, :], q_ref[0, at, :], (0, 0)), dot(v_ref[0, at, :], do_ref[at, :], (0, 0))

    def block(partial):
        following = products(0)
        for h in range(heads):
            at = slice(HD * h, HD * (h + 1))
            s, dp = following
            if h + 1 < heads:
                following = products(h + 1)
            p = jnp.exp(s - lse_ref[0, h : h + 1, :])
            if partial:
                p = jnp.where(lax.broadcasted_iota(jnp.int32, s.shape, 0) < live, p, 0.0)
            ds = (p * (dp - inner_ref[h : h + 1, :])).astype(BF16)
            acc_ref[at, :] += dot(k_ref[0, at, :], ds)
            dkv_ref[0, :, at] = dot(ds, q_ref[0, at, :], (1, 1)).astype(BF16)
            dkv_ref[0, :, feats + HD * h : feats + HD * (h + 1)] = dot(p.astype(BF16), do_ref[at, :], (1, 1)).astype(BF16)

    @pl.when(live == ROW_BLOCK)
    def _():
        block(False)

    @pl.when((live > 0) & (live < ROW_BLOCK))
    def _():
        block(True)

    @pl.when(work_ref[4, i] == 1)
    def _():
        dq_ref[0] = acc_ref[...].T.astype(BF16)


def cross_backward(work, place, q, do, lse, inner, k, v):
    examples, feats, length = q.shape
    rows = k.shape[2]
    of_example = lambda *shape: pl.BlockSpec((1, *shape), lambda i, work, place: (work[0, i], 0, 0))
    k_spec = pl.BlockSpec((1, feats, ROW_BLOCK), lambda i, work, place: (work[0, i], 0, work[1, i]))
    d_spec = pl.BlockSpec((1, ROW_BLOCK, 2 * feats), lambda i, work, place: (work[0, i], work[1, i], 0))
    return pl.pallas_call(
        cross_backward_kernel,
        grid_spec=pltpu.PrefetchScalarGridSpec(
            num_scalar_prefetch=2,
            grid=(work.shape[1],),
            in_specs=[
                of_example(feats, length),
                *[of_example(feats, length // 4)] * 4,
                of_example(8, length),
                *[of_example(8, length // 4)] * 4,
                k_spec,
                k_spec,
            ],
            out_specs=[of_example(length, feats), d_spec],
            scratch_shapes=[
                pltpu.VMEM((feats, length), F32),
                pltpu.VMEM((feats, length), BF16),
                pltpu.VMEM((8, length), F32),
            ],
        ),
        out_shape=[
            jax.ShapeDtypeStruct((examples, length, feats), BF16),
            jax.ShapeDtypeStruct((examples, rows, 2 * feats), BF16),
        ],
        compiler_params=pltpu.CompilerParams(vmem_limit_bytes=48 << 20),
        cost_estimate=cost(45e-6 * PEAK_FLOPS, 24e6),
        name="cross_backward",
    )(work, place, q, *do, lse, *inner, k, v)


def memory_backward_kernel(
    live_ref, own_ref, other_ref, dkv_ref, wt_ref, out_ref, out_other_ref, g_ref, sum_ref
):
    e, j = pl.program_id(0), pl.program_id(1)
    own_blocks = pl.num_programs(1) // 2

    @pl.when((e == 0) & (j == 0))
    def _():
        sum_ref[...] = jnp.zeros_like(sum_ref)

    for mine, rows_ref, to_ref in ((j < own_blocks, own_ref, out_ref), (j >= own_blocks, other_ref, out_other_ref)):

        @pl.when(mine & (live_ref[e, j] > 0))
        def _():
            dkv = dkv_ref[0]
            sum_ref[...] += dot(rows_ref[0], dkv, (0, 0))
            to_ref[0] = dot(dkv, wt_ref[...]).astype(BF16)

        @pl.when(mine & (live_ref[e, j] == 0))
        def _():
            to_ref[0] = jnp.zeros_like(to_ref[0])

    @pl.when((e == pl.num_programs(0) - 1) & (j == pl.num_programs(1) - 1))
    def _():
        g_ref[...] = sum_ref[...].astype(BF16)


def memory_backward(live, own, other, dkv, wt):
    examples, count, model = own.shape
    width = dkv.shape[2]
    half = count // ROW_BLOCK
    row_spec = lambda first: pl.BlockSpec(
        (1, ROW_BLOCK, model), lambda e, j, live: (e, jnp.clip(j - first, 0, half - 1), 0)
    )
    d_spec = pl.BlockSpec((1, ROW_BLOCK, width), lambda e, j, live: (e, j, 0))
    w_spec = pl.BlockSpec(wt.shape, lambda e, j, live: (0, 0))
    return pl.pallas_call(
        memory_backward_kernel,
        grid_spec=pltpu.PrefetchScalarGridSpec(
            num_scalar_prefetch=1,
            grid=(examples, 2 * half),
            in_specs=[row_spec(0), row_spec(half), d_spec, w_spec],
            out_specs=[row_spec(0), row_spec(half), pl.BlockSpec((model, width), lambda e, j, live: (0, 0))],
            scratch_shapes=[pltpu.VMEM((model, width), F32)],
        ),
        out_shape=[
            jax.ShapeDtypeStruct(own.shape, BF16),
            jax.ShapeDtypeStruct(own.shape, BF16),
            jax.ShapeDtypeStruct((model, width), BF16),
        ],
        compiler_params=pltpu.CompilerParams(vmem_limit_bytes=48 << 20),
        cost_estimate=cost(18e-6 * PEAK_FLOPS, 30e6),
        name="memory_backward",
    )(live, own, other, dkv, wt)


def self_output_kernel(
    place_ref, x_ref, o0_ref, o1_ref, o2_ref, o3_ref, mine_ref, other_ref, gain_ref,
    n2_ref, q_ref, x1_ref, own_o_ref, wo_ref, wq_ref,
    rows_ref,
):
    core = jnp.bitwise_and(place_ref[0], 1)
    feats = wq_ref.shape[1]
    width = o0_ref.shape[1]
    own = x1_ref.shape[1]

    @pl.when(pl.program_id(0) == 0)
    def _():
        for i, from_ref in ((core, mine_ref), (1 - core, other_ref)):
            wo_ref[:, strip(i, feats)] = from_ref[:, feats:]
        for i, from_ref in enumerate((mine_ref, other_ref)):
            for at in range(0, feats, LANES):
                wq_ref[i, at : at + LANES, :] = from_ref[:, at : at + LANES].T

    x1 = x_ref[0].astype(F32)
    for flip, o_ref in enumerate((o0_ref, o1_ref, o2_ref, o3_ref)):
        heads = strip(place_index(place_ref, flip), width)
        x1 += dot(o_ref[0], wo_ref[heads, :], (0, 0))
        own_o_ref[0, heads, :] = o_ref[0, :, strip(place_ref[0], own)]
    n2 = root_norm(x1, gain_ref[...]).astype(BF16)
    n2_ref[0] = n2
    q_ref[0] = dot(wq_ref[0], n2, (1, 1)).astype(BF16)
    rows_ref[...] = x1
    x1_ref[0] = rows_ref[strip(place_ref[0], own), :]


def self_output_stage(place, x, pieces, mine, other, gain):
    examples, length, model = x.shape
    own, feats, width = length // 4, model // 2, pieces[0].shape[1]
    whole = lambda *shape: pl.BlockSpec(shape, lambda e: (0,) * len(shape))
    per = lambda *shape: pl.BlockSpec((1, *shape), lambda e: (e, 0, 0))
    array = jax.ShapeDtypeStruct
    return pl.pallas_call(
        self_output_kernel,
        grid=(examples,),
        in_specs=[pl.BlockSpec(memory_space=pltpu.SMEM), per(length, model)]
        + [per(width, length)] * 4
        + [whole(*mine.shape), whole(*other.shape), whole(1, model)],
        out_specs=[
            per(length, model),
            per(feats, length),
            per(own, model),
            per(model, own),
            whole(model, model),
            whole(2, feats, model),
        ],
        out_shape=[
            array((examples, length, model), BF16),
            array((examples, feats, length), BF16),
            array((examples, own, model), F32),
            array((examples, model, own), BF16),
            array((model, model), BF16),
            array((2, feats, model), BF16),
        ],
        scratch_shapes=[pltpu.VMEM((length, model), F32)],
        compiler_params=pltpu.CompilerParams(vmem_limit_bytes=48 << 20),
        cost_estimate=cost(6e-6 * PEAK_FLOPS, 10e6),
        name="self_output_stage",
    )(place, x, *pieces, mine, other, gain)


def combine_kernel(place_ref, o_ref, came_ref, lse_ref, other_lse_ref, chip_ref, total_ref):
    row = lax.shift_right_logical(place_ref[0], 1)
    here = strip(row, came_ref.shape[2])
    one, two = lse_ref[0], other_lse_ref[0]
    peak = jnp.maximum(one, two)
    total_ref[0] = peak + jnp.log(jnp.exp(one - peak) + jnp.exp(two - peak))
    own_weight = jnp.exp(lse_ref[0, :, here] - total_ref[0, :, here])
    other_weight = jnp.exp(other_lse_ref[0, :, here] - total_ref[0, :, here])
    for h in range(o_ref.shape[1] // HD):
        at = slice(HD * h, HD * (h + 1))
        one = o_ref[0, at, here].astype(F32) * own_weight[h : h + 1, :]
        chip_ref[0, at, :] = (one + came_ref[0, at, :].astype(F32) * other_weight[h : h + 1, :]).astype(BF16)


def combine(place, o, came, lse, other_lse):
    examples, feats, length = o.shape
    per = lambda *shape: pl.BlockSpec((1, *shape), lambda e: (e, 0, 0))
    return pl.pallas_call(
        combine_kernel,
        grid=(examples,),
        in_specs=[
            pl.BlockSpec(memory_space=pltpu.SMEM),
            per(feats, length),
            per(feats, length // 2),
            per(8, length),
            per(8, length),
        ],
        out_specs=[per(feats, length // 2), per(8, length)],
        out_shape=[
            jax.ShapeDtypeStruct((examples, feats, length // 2), BF16),
            jax.ShapeDtypeStruct((examples, 8, length), F32),
        ],
        compiler_params=pltpu.CompilerParams(vmem_limit_bytes=24 << 20),
        cost_estimate=cost(2e-6 * PEAK_FLOPS, 3e6),
        name="combine",
    )(place, o, came, lse, other_lse)


def norm_back(values, gain, grad):
    scale = lax.rsqrt(jnp.mean(values * values, axis=-1, keepdims=True) + NORM_EPS)
    pulled = grad * gain
    inner = jnp.mean(values * pulled, axis=-1, keepdims=True)
    back = scale * pulled - values * (scale * scale * scale * inner)
    return back, jnp.sum(grad * values * scale, axis=0, keepdims=True)


def feed_forward_kernel(
    place_ref, x1_ref, mine_ref, other_ref, dy_ref, gain_ref, wo_ref, gate_ref, up_ref, down_ref,
    out_ref, dx2_ref, doc_mine_ref, doc_other_ref, inner_mine_ref, inner_other_ref,
    g_ref, g_sent_ref, g_down_ref, g_down_sent_ref, g_out_ref, g_out_sent_ref, g_gain_ref,
    x2_ref, n3_ref, sum_ref, dn3_ref, g_full_ref, *, piece,
):
    i = pl.program_id(0)
    core = jnp.bitwise_and(place_ref[0], 1)
    examples, feats, own = mine_ref.shape

    def deal(low, high, keep_ref, sent_ref):
        keep_ref[...] = jnp.where(core == 0, low, high).astype(BF16)
        sent_ref[...] = jnp.where(core == 0, high, low).astype(BF16)
    sides = ((core, mine_ref, doc_mine_ref, inner_mine_ref), (1 - core, other_ref, doc_other_ref, inner_other_ref))

    @pl.when(i == 0)
    def _():
        for e in range(examples):
            x2 = x1_ref[own * e : own * (e + 1), :]
            for side, o_ref, *_ in sides:
                x2 += dot(o_ref[e], wo_ref[strip(side, feats), :], (0, 0))
            x2_ref[own * e : own * (e + 1), :] = x2
        n3_ref[...] = root_norm(x2_ref[...], gain_ref[...]).astype(BF16)
        sum_ref[...] = jnp.zeros_like(sum_ref)
        dn3_ref[...] = jnp.zeros_like(dn3_ref)

    n3, dy = n3_ref[...], dy_ref[...]
    a, u = dot(n3, gate_ref[...]), dot(n3, up_ref[...])
    dh = dot(dy, down_ref[...], (1, 1))
    root = math.sqrt(2 / math.pi)
    bent = jnp.tanh(root * (a + 0.044715 * (a * a * a)))
    rise = 0.5 * (1.0 + bent)
    gelu = a * rise
    slope = rise + 0.5 * a * (1.0 - bent * bent) * (root * (1.0 + 3 * 0.044715 * (a * a)))
    hidden = (gelu * u).astype(BF16)
    da = (dh * u * slope).astype(BF16)
    du = (dh * gelu).astype(BF16)
    sum_ref[...] += dot(hidden, down_ref[...])
    g_down = dot(hidden, dy, (0, 0))
    pieces = g_down.reshape(g_down.shape[0] // (2 * piece), 2, piece, g_down.shape[1])
    deal(*(pieces[:, side].reshape(g_down_ref.shape) for side in range(2)), g_down_ref, g_down_sent_ref)
    deal(dot(n3, da, (0, 0)), dot(n3, du, (0, 0)), g_ref, g_sent_ref)
    dn3_ref[...] += dot(da, gate_ref[...], (1, 1)) + dot(du, up_ref[...], (1, 1))

    @pl.when(i == pl.num_programs(0) - 1)
    def _():
        x2 = x2_ref[...]
        out_ref[...] = (x2 + sum_ref[...]).astype(BF16)
        back, g_gain = norm_back(x2, gain_ref[...], dn3_ref[...])
        g_gain_ref[...] = g_gain
        dx2 = dy_ref[...].astype(F32) + back
        dx2_ref[...] = dx2
        n3_ref[...] = dx2.astype(BF16)
        for side, o_ref, doc_ref, inner_ref in sides:
            heads = strip(side, feats)
            total = jnp.zeros((feats, wo_ref.shape[1]), F32)
            inner_ref[...] = jnp.zeros_like(inner_ref)
            for e in range(examples):
                dx2r = n3_ref[own * e : own * (e + 1), :]
                total += dot(o_ref[e], dx2r)
                doc = dot(wo_ref[heads, :], dx2r, (1, 1)).astype(BF16)
                doc_ref[e] = doc
                product = doc.astype(F32) * o_ref[e].astype(F32)
                for h in range(feats // HD):
                    inner_ref[e, h : h + 1, :] = jnp.sum(product[HD * h : HD * (h + 1)], axis=0, keepdims=True)
            g_full_ref[heads, :] = total
        deal(g_full_ref[:, :feats], g_full_ref[:, feats:], g_out_ref, g_out_sent_ref)


def feed_forward(place, x1, mine, other, dy, gain, wide_w, down, piece):
    tokens, model = x1.shape
    examples, feats, own = mine.shape
    hidden = down.shape[0]
    part = 256
    whole = lambda *shape: pl.BlockSpec(shape, lambda i: (0,) * len(shape))
    first = model // part
    array = jax.ShapeDtypeStruct
    return pl.pallas_call(
        functools.partial(feed_forward_kernel, piece=piece),
        grid=(hidden // part,),
        in_specs=[
            pl.BlockSpec(memory_space=pltpu.SMEM),
            whole(tokens, model),
            whole(*mine.shape),
            whole(*other.shape),
            whole(tokens, model),
            whole(1, model),
            whole(model, model),
            pl.BlockSpec((model, part), lambda i: (0, first + i)),
            pl.BlockSpec((model, part), lambda i: (0, first + hidden // part + i)),
            pl.BlockSpec((part, model), lambda i: (i, 0)),
        ],
        out_specs=[
            whole(tokens, model),
            whole(tokens, model),
            whole(*mine.shape),
            whole(*mine.shape),
            whole(examples, 8, own),
            whole(examples, 8, own),
            *[pl.BlockSpec((model, part), lambda i: (0, i))] * 2,
            *[pl.BlockSpec((part // 2, model), lambda i: (i, 0))] * 2,
            *[whole(model, feats)] * 2,
            whole(1, model),
        ],
        out_shape=[
            array((tokens, model), BF16),
            array((tokens, model), F32),
            array(mine.shape, BF16),
            array(mine.shape, BF16),
            array((examples, 8, own), F32),
            array((examples, 8, own), F32),
            *[array((model, hidden), BF16)] * 2,
            *[array((hidden // 2, model), BF16)] * 2,
            *[array((model, feats), BF16)] * 2,
            array((1, model), F32),
        ],
        scratch_shapes=[
            pltpu.VMEM((tokens, model), F32),
            pltpu.VMEM((tokens, model), BF16),
            pltpu.VMEM((tokens, model), F32),
            pltpu.VMEM((tokens, model), F32),
            pltpu.VMEM((model, model), F32),
        ],
        compiler_params=pltpu.CompilerParams(vmem_limit_bytes=48 << 20),
        cost_estimate=cost(20e-6 * PEAK_FLOPS, 24e6),
        name="feed_forward",
    )(place, x1, mine, other, dy, gain, wide_w, wide_w, wide_w, down)


def self_output_back_kernel(
    place_ref, mine_ref, other_ref, wq_ref, x1_ref, gain_ref, dx2_ref, own_o_ref, wo_ref,
    dx1_ref, do_mine_ref, do_pair_ref, do_across_ref, g_keep_ref, g_sent_ref, g_gain_ref,
    sum_ref, do_ref,
):
    e = pl.program_id(0)
    core, row = jnp.bitwise_and(place_ref[0], 1), lax.shift_right_logical(place_ref[0], 1)
    width, feats = do_mine_ref.shape[1], do_across_ref.shape[1]

    @pl.when(e == 0)
    def _():
        sum_ref[...] = jnp.zeros_like(sum_ref)
        g_gain_ref[...] = jnp.zeros_like(g_gain_ref)

    dn2 = dot(mine_ref[0], wq_ref[0]) + dot(other_ref[0], wq_ref[1])
    back, g_gain = norm_back(x1_ref[0], gain_ref[...], dn2)
    g_gain_ref[...] += g_gain
    dx1 = dx2_ref[0] + back
    dx1_ref[0] = dx1
    dx1r = dx1.astype(BF16)
    do_ref[...] = dot(wo_ref[...], dx1r, (1, 1)).astype(BF16)
    do_mine_ref[0] = do_ref[strip(place_ref[0], width), :]
    do_pair_ref[0] = do_ref[strip(place_index(place_ref, 1), width), :]
    do_across_ref[0] = do_ref[strip(1 - row, feats), :]
    sum_ref[...] += dot(own_o_ref[0], dx1r)

    @pl.when(e == pl.num_programs(0) - 1)
    def _():
        g_keep_ref[...] = sum_ref[:, strip(core, feats)].astype(BF16)
        g_sent_ref[...] = sum_ref[:, strip(1 - core, feats)].astype(BF16)


def self_output_back(place, mine, other, wq, x1, gain, dx2, own_o, wo):
    examples, own, model = x1.shape
    feats = mine.shape[2]
    whole = lambda *shape: pl.BlockSpec(shape, lambda e: (0,) * len(shape))
    per = lambda *shape: pl.BlockSpec((1, *shape), lambda e: (e, 0, 0))
    array = jax.ShapeDtypeStruct
    return pl.pallas_call(
        self_output_back_kernel,
        grid=(examples,),
        in_specs=[
            pl.BlockSpec(memory_space=pltpu.SMEM),
            per(own, feats),
            per(own, feats),
            whole(*wq.shape),
            per(own, model),
            whole(1, model),
            per(own, model),
            per(model, own),
            whole(model, model),
        ],
        out_specs=[
            per(own, model),
            *[per(model // 4, own)] * 2,
            per(feats, own),
            *[whole(model, feats)] * 2,
            whole(1, model),
        ],
        out_shape=[
            array((examples, own, model), F32),
            *[array((examples, model // 4, own), BF16)] * 2,
            array((examples, feats, own), BF16),
            *[array((model, feats), BF16)] * 2,
            array((1, model), F32),
        ],
        scratch_shapes=[pltpu.VMEM((model, model), F32), pltpu.VMEM((model, own), BF16)],
        compiler_params=pltpu.CompilerParams(vmem_limit_bytes=48 << 20),
        cost_estimate=cost(4e-6 * PEAK_FLOPS, 8e6),
        name="self_output_back",
    )(place, mine, other, wq, x1, gain, dx2, own_o, wo)


def fold_rows(rows, target, columns):
    rest = rows * columns // target
    tile = 16
    if rows % tile or rows // tile * LANES != rest or columns // LANES * tile != target:
        return (lambda b: b.reshape(*b.shape[:-2], target, rest)), (lambda b: b.reshape(rows, columns))

    def swap(b, down, across):
        b = b.reshape(*b.shape[:-2], down, tile, across, LANES)
        return jnp.swapaxes(b, -4, -2).reshape(*b.shape[:-4], across * tile, down * LANES)

    return (lambda b: swap(b, rows // tile, columns // LANES)), (lambda b: swap(b, target // tile, rest // LANES))


def local(
    dec_input,
    enc_out,
    enc_len,
    cotangent,
    self_query,
    self_key,
    self_value,
    self_output,
    cross_query,
    cross_key,
    cross_value,
    cross_output,
    ffn_gate,
    ffn_up,
    ffn_down,
    self_gain,
    cross_gain,
    ffn_gain,
    bias_table,
):
    place = lax.axis_index("narrow")
    row, core = place // 2, place % 2
    wide = lax.axis_size("wide")
    examples, own, model = dec_input.shape
    length = 4 * own
    heads = model // HD
    own_heads = heads // 4
    memory_rows = enc_out.shape[1]
    share = self_query.shape[0]

    half = lambda w: part_of(w.astype(BF16), core, 2, 1)
    own_qkv = jnp.concatenate(
        [part_of(w.astype(BF16), place, 4, 1) for w in (self_query, self_key, self_value)], 1
    )
    own_qkv = jnp.pad(own_qkv, ((0, 0), (0, -own_qkv.shape[1] % LANES)))
    small = jnp.stack([self_gain, cross_gain, ffn_gain, jnp.pad(bias_table, (0, share - bias_table.shape[0]))], 1)
    small = jnp.pad(small.astype(BF16), ((0, 0), (0, LANES - 4)))
    feats = model // 2
    self_w, small = wide_gather(jnp.concatenate([own_qkv, small], 1), (own_qkv.shape[1], LANES))
    small_rows = small[:, :4].astype(F32).T
    gain_one, gain_two, gain_three = (small_rows[i : i + 1] for i in range(3))
    table = small_rows[3].reshape(wide, share)[:, : bias_table.shape[0]].reshape(BUCKETS, heads)

    both = ("wide", "narrow")
    quarter = lambda w: part_of(w.astype(BF16), place, 4, 0)
    ffn_in = lax.all_gather(
        jnp.concatenate([quarter(cross_output), quarter(ffn_gate), quarter(ffn_up)], 1), both, axis=0, tiled=True
    )
    down_w = lax.all_gather(quarter(ffn_down), both, axis=0, tiled=True)

    enc_other = pair_swap(enc_out)
    starts = (place * memory_rows + np.arange(memory_rows // ROW_BLOCK) * ROW_BLOCK).astype(jnp.int32)
    other_starts = starts + (1 - 2 * core) * memory_rows
    block_starts = jnp.concatenate([starts, other_starts])
    live = jnp.clip(enc_len[:, None] - block_starts[None, :], 0, ROW_BLOCK)

    x_all = narrow_gather(dec_input, 1, row, core)
    hot = jnp.asarray(bucket_table(length))
    distance_bias = jnp.dot(table.T, hot, precision=FULL_ACCURACY)
    vec = jnp.pad(part_of(distance_bias, place, 4, 0), ((0, 8 - own_heads), (0, 0)))
    qkv, self_o, self_lse, self_wt = self_forward(x_all, gain_one, self_w, vec, own_heads)
    across_o = across_swap(self_o)
    pieces = [self_o, pair_swap(self_o), across_o, pair_swap(across_o)]
    memory_w = shared_gather(jnp.concatenate([half(cross_key), half(cross_value)], 1), row, first=(self_o,))
    work = work_list(live)
    keys, values, memory_wt = memory_project(work, enc_out, enc_other, memory_w)
    query_out = after(jnp.concatenate([half(cross_query), half(self_output)], 1), self_o)
    (mine_w,) = wide_gather(query_out, (query_out.shape[1],))
    mine_w = after(mine_w, keys)
    other_w = pair_swap(mine_w)
    me = place.reshape(1).astype(jnp.int32)
    n2, cross_q, x1, own_o, self_out_w, cross_query_wt = self_output_stage(
        me, x_all, pieces, mine_w, other_w, gain_two
    )

    part_o, part_lse = cross_forward(work, cross_q, keys, values)
    came = across_swap(part_of(part_o, 1 - row, 2, 2))
    chip_o, lse = combine(me, part_o, came, part_lse, across_swap(part_lse))
    mine_o, other_o = part_of(chip_o, core, 2, 2), pair_swap(part_of(chip_o, 1 - core, 2, 2))

    tokens = examples * own
    down_rows = ffn_down.shape[0] // 2
    (
        layer_out, dx2, doc_mine, doc_other, inner_mine, inner_other,
        gate_up, gate_up_sent, down, down_sent, grad_co, co_sent, grad_gain_three,
    ) = feed_forward(
        me, x1.reshape(tokens, model), mine_o, other_o, cotangent.reshape(tokens, model), gain_three,
        ffn_in, down_w, down_rows,
    )
    layer_out, dx2 = layer_out.reshape(x1.shape), dx2.reshape(x1.shape)

    rows_of = lambda g: g.reshape(wide, share, -1)

    def from_all(mine, other):
        pair = pair_swap(other)
        return [mine, pair, across_swap(mine), across_swap(pair)]

    doc, inner = from_all(doc_mine, doc_other), from_all(inner_mine, inner_other)
    ffn = gate_up, pair_swap(gate_up_sent)
    by_y = lambda y: [part_of(g, y, 2, 1).astype(F32) for g in ffn]
    ffn_sent = sum(by_y(1 - row)).astype(BF16)
    down = plus(down, pair_swap(down_sent)).reshape(wide, down_rows, model)
    co = plus(grad_co, pair_swap(co_sent))
    doc, inner, ffn_sent, down, co = lax.optimization_barrier((doc, inner, ffn_sent, down, co))
    ffn_came, down = across_swap(ffn_sent), wide_scatter_x(down)
    part_dq, dkv = cross_backward(work, me, cross_q, doc, lse, inner, keys, values)
    part_dq, dkv, ffn_came, down = lax.optimization_barrier((part_dq, dkv, ffn_came, down))
    ffn = wide_scatter_x(rows_of(sum(by_y(row), ffn_came.astype(F32)).astype(BF16)))

    dq_came = across_swap(part_of(part_dq, 1 - row, 2, 1))
    enc_mine, enc_swapped, grad_memory = memory_backward(live, enc_out, enc_other, dkv, memory_wt)
    enc_came = pair_swap(enc_swapped)
    dq_came, grad_memory, ffn = lax.optimization_barrier((dq_came, grad_memory, ffn))
    down_came = across_swap(part_of(down, 1 - row, 2, 1))
    chip_dq = plus(part_of(part_dq, row, 2, 1), dq_came)
    dq_mine, dq_other = part_of(chip_dq, core, 2, 1), pair_swap(part_of(chip_dq, 1 - core, 2, 1))
    grad_cross_query = jnp.einsum("etd,etf->df", n2, part_dq, preferred_element_type=F32).astype(BF16)
    late = x_swap(jnp.concatenate([rows_of(g) for g in (grad_cross_query, grad_memory, co)], 2))
    dx1, do_mine, do_pair, do_across, grad_so, so_sent, grad_gain_two = self_output_back(
        me, dq_mine, dq_other, cross_query_wt, x1, gain_two, dx2, own_o, self_out_w
    )

    ffn = z_swap(after(ffn, do_across))

    do_came = across_swap(do_across)
    do = [do_mine, pair_swap(do_pair), part_of(do_came, core, 2, 1), pair_swap(part_of(do_came, 1 - core, 2, 1))]
    so = rows_of(plus(grad_so, pair_swap(so_sent)))
    down = plus(part_of(down, row, 2, 1), down_came)
    do, so, late, down = lax.optimization_barrier((do, so, late, down))
    fold, unfold = fold_rows(down.shape[1], share, model)
    late = z_swap(jnp.concatenate([total(late), fold(down)], 2))
    so_came = across_swap(part_of(so, 1 - row, 2, 1))
    part_dn1, grad_self, dvec, grad_gain_one = self_backward(
        me, x_all, gain_one, qkv, do, self_lse, self_wt, vec, own_heads
    )
    part_dn1, grad_self, so_came, ffn, *early = lax.optimization_barrier((part_dn1, grad_self, so_came, ffn, *late[:-1]))
    late, ffn_sum = (*early, *late[-1:]), total(ffn)

    own_table = jnp.dot(hot, dvec[:own_heads].T, precision=FULL_ACCURACY)
    grad_table = lax.dynamic_update_slice_in_dim(
        jnp.zeros((BUCKETS, heads), F32), own_table, place * own_heads, 1
    )
    small = [g.reshape(wide, -1) for g in (grad_gain_one, grad_gain_two, grad_gain_three, grad_table)]
    small = jnp.concatenate(small, 1).astype(BF16)
    small_count = small.shape[1]
    small = jnp.pad(small, ((0, 0), (0, share // 2 * LANES - small_count))).reshape(wide, -1, LANES)
    so = plus(part_of(so, row, 2, 1), so_came)
    self_width = grad_self.shape[1]
    self_halves = grad_self.reshape(wide, 2, share // 2, self_width)
    last = x_swap(jnp.concatenate([self_halves[:, 0], self_halves[:, 1], so, small], 2))
    by_core = part_dn1.reshape(examples, 2, 2, own, model)
    column = plus(part_of(by_core, core, 2, 2).astype(F32), pair_swap(part_of(by_core, 1 - core, 2, 2)))
    dn1_sent = part_of(column, 1 - row, 2, 1).astype(BF16)
    enc_grad = plus(enc_mine, enc_came)
    sums = jnp.concatenate([ffn_sum, total(late)], 1)
    dn1_came, sums_came = across_swap(dn1_sent), across_swap(sums)
    last, dn1_sent, enc_grad, sums = lax.optimization_barrier((last, dn1_sent, enc_grad, sums))
    last = z_swap(total(last))
    last, dn1_came, sums_came = lax.optimization_barrier((last, dn1_came, sums_came))
    last_sum = total(last)
    last_came = across_swap(last_sum)
    dn1 = plus(part_of(column, row, 2, 1), dn1_came)
    grad_in, _ = norm_back(
        dec_input.reshape(tokens, model).astype(F32), gain_one, dn1.reshape(tokens, model)
    )
    input_grad = (dx1 + grad_in.reshape(x1.shape)).astype(BF16)

    bounds = np.cumsum([0, ffn_sum.shape[1], 4 * feats])
    low, high = in_order(row, sums, sums_came)
    sums = jnp.concatenate(
        [
            low[:, : bounds[1]],
            high[:, : bounds[1]],
            plus(sums[:, bounds[1] : bounds[2]], sums_came[:, bounds[1] : bounds[2]]),
            low[:, bounds[2] :],
            high[:, bounds[2] :],
        ],
        1,
    )
    parts = in_order(core, sums, pair_swap(sums))
    gate_sum, up_sum = (part[:, : 2 * bounds[1]] for part in parts)
    cq_sum, ck_sum, cv_sum, co_sum = (
        jnp.concatenate([part[:, 2 * bounds[1] + feats * i : 2 * bounds[1] + feats * (i + 1)] for part in parts], 1)
        for i in range(4)
    )
    down_sum = [jnp.split(part[:, 2 * bounds[1] + 4 * feats :], 2, 1) for part in parts]
    down_sum = jnp.concatenate([unfold(half) for part in down_sum for half in part], 0)

    last = jnp.stack(in_order(row, last_sum, last_came))
    low, high = in_order(core, last, pair_swap(last))
    halves = lambda part: jnp.concatenate([part[:, :self_width], part[:, self_width : 2 * self_width]], 0)
    self_sum = [halves(part[y]) for y in range(2) for part in (low, high)]
    q_sum, k_sum, v_sum = (
        jnp.concatenate([part[:, own_heads * HD * i : own_heads * HD * (i + 1)] for part in self_sum], 1)
        for i in range(3)
    )
    so_sum = jnp.concatenate(
        [part[:, :, 2 * self_width : 2 * self_width + feats].reshape(share, -1) for part in (low, high)], 1
    )
    small_sum = sum(part[y, :, 2 * self_width + feats :].astype(F32) for part in (low, high) for y in range(2))
    small_sum = small_sum.reshape(-1)[:small_count]
    f = lambda a: a.astype(F32)
    return (
        layer_out,
        input_grad,
        enc_grad,
        *(f(g) for g in (q_sum, k_sum, v_sum, so_sum, cq_sum, ck_sum, cv_sum, co_sum, gate_sum, up_sum, down_sum)),
        small_sum[:share],
        small_sum[share : 2 * share],
        small_sum[2 * share : 3 * share],
        small_sum[3 * share :],
    )


def solution(mesh):
    rows = P("wide", "narrow", None)
    weight, vector = P("wide", None), P("wide")
    return jax.shard_map(
        local,
        mesh=mesh,
        in_specs=(rows, rows, vector, rows, *[weight] * 11, *[vector] * 4),
        out_specs=(rows, rows, rows, *[weight] * 11, *[vector] * 4),
        check_vma=False,
    )
```

```python
import functools
import math

import jax
import jax.numpy as jnp
import numpy as np
from jax import lax
from jax.experimental import pallas as pl
from jax.experimental.pallas import tpu as pltpu
from jax.sharding import PartitionSpec as P

HD = 64
BUCKETS = 32
MAXDIST = 128
NORM_EPS = 1e-06
MASKED = -1e30
LANES = 128
ROW_BLOCK = 512
PEAK_FLOPS = 1.15e15
FULL_ACCURACY = lax.Precision.HIGHEST
F32 = jnp.float32
BF16 = jnp.bfloat16

PAIR = ((0, 1), (1, 0), (2, 3), (3, 2))
ACROSS = ((0, 2), (2, 0), (1, 3), (3, 1))


def bucket_table(length):
    exact = BUCKETS // 2
    hot = np.zeros((BUCKETS, length), np.float32)
    for distance in range(length):
        bucket = distance
        if distance >= exact:
            scaled = math.log(distance / exact) / math.log(MAXDIST / exact) * (BUCKETS - exact)
            bucket = min(exact + math.floor(scaled), BUCKETS - 1)
        hot[bucket, distance] = 1.0
    return hot


def dot(left, right, contract=(1, 0)):
    return lax.dot_general(
        left, right, (((contract[0],), (contract[1],)), ((), ())), preferred_element_type=F32
    )


def root_norm(values, gain):
    return values * lax.rsqrt(jnp.mean(values * values, axis=-1, keepdims=True) + NORM_EPS) * gain


def pair_swap(value):
    return lax.ppermute(value, "narrow", PAIR)


def across_swap(value):
    return lax.ppermute(value, "narrow", ACROSS)


def in_order(flag, mine, other):
    first = flag == 0
    return jnp.where(first, mine, other), jnp.where(first, other, mine)


def narrow_gather(value, axis, row, core):
    low, high = in_order(row, value, across_swap(value))
    column = jnp.stack([low, high], axis)
    low, high = in_order(core, column, pair_swap(column))
    full = jnp.stack([low, high], axis + 1)
    shape = list(value.shape)
    shape[axis] *= 4
    return full.reshape(shape)


def plus(mine, came):
    return (mine.astype(F32) + came.astype(F32)).astype(mine.dtype)


def part_of(value, index, parts, axis):
    size = value.shape[axis] // parts
    return lax.dynamic_slice_in_dim(value, index * size, size, axis)


LINE = 4
BESIDE = tuple((i, i ^ 1) for i in range(2 * LINE))


def along(step):
    return [(2 * z + x, 2 * ((z + step) % LINE) + x) for z in range(LINE) for x in range(2)]


def by_planes():
    return lax.axis_size("wide") == 2 * LINE


def assemble_kernel(widths, order_ref, *refs):
    pieces, outs = refs[: 2 * LINE], refs[2 * LINE :]
    for i, piece in enumerate(pieces):
        at = 0
        for width, out in zip(widths, outs):
            out[order_ref[i]] = piece[:, at : at + width]
            at += width


def after(value, *others):
    return lax.optimization_barrier((value, *others))[0]


def wide_gather(block, widths, first=()):
    rows = block.shape[0]
    if not by_planes():
        full = lax.all_gather(block, "wide", axis=0, tiled=True)
        bounds = np.cumsum([0, *widths])
        return [full[:, a:b] for a, b in zip(bounds[:-1], bounds[1:])]
    z, x = lax.axis_index("wide") // 2, lax.axis_index("wide") % 2
    line = [block] + [lax.ppermute(block, "wide", along(step)) for step in range(1, LINE)]
    line = after(line, *first)
    pieces = line + [lax.ppermute(piece, "wide", BESIDE) for piece in line]
    places = (z - np.arange(LINE)) % LINE * 2
    order = jnp.concatenate([places + x, places + 1 - x]).astype(jnp.int32)
    outs = pl.pallas_call(
        functools.partial(assemble_kernel, widths),
        in_specs=[pl.BlockSpec(memory_space=pltpu.SMEM)] + [pl.BlockSpec(memory_space=pltpu.VMEM)] * len(pieces),
        out_specs=[pl.BlockSpec(memory_space=pltpu.VMEM)] * len(widths),
        out_shape=[jax.ShapeDtypeStruct((2 * LINE, rows, width), block.dtype) for width in widths],
        compiler_params=pltpu.CompilerParams(vmem_limit_bytes=16 << 20),
        name="assemble",
    )(order, *pieces)
    return [out.reshape(2 * LINE * rows, out.shape[2]) for out in outs]


def shared_gather(block, row, first=()):
    rows, width = block.shape
    (full,) = wide_gather(part_of(block, row, 2, 0), (width,), first)
    halves = full.reshape(-1, rows // 2, width)
    return jnp.stack(in_order(row, halves, across_swap(halves)), 1).reshape(-1, width)


def pick(value, index, axis):
    return lax.dynamic_index_in_dim(value, index, axis, keepdims=False)


def x_swap(blocks):
    if not by_planes():
        return (blocks,)
    x = lax.axis_index("wide") % 2
    planes = blocks.reshape(LINE, 2, *blocks.shape[1:])
    return pick(planes, x, 1), lax.ppermute(pick(planes, 1 - x, 1), "wide", BESIDE)


def z_swap(planes):
    if not by_planes():
        shape = planes.shape
        return (
            lax.psum_scatter(
                planes.reshape(shape[0] * shape[1], *shape[2:]), "wide", scatter_dimension=0, tiled=True
            ),
        )
    z = lax.axis_index("wide") // 2
    sent = [pick(planes, (z + step) % LINE, 0) for step in range(1, LINE)]
    return pick(planes, z, 0), *(lax.ppermute(s, "wide", along(i + 1)) for i, s in enumerate(sent))


def total(parts):
    return sum((part.astype(F32) for part in parts[1:]), parts[0].astype(F32)).astype(parts[0].dtype)


def wide_scatter_x(blocks):
    return total(x_swap(blocks))


def wide_scatter_z(planes):
    return total(z_swap(planes))


def wide_scatter(blocks):
    return wide_scatter_z(wide_scatter_x(blocks))


def place_index(place_ref, flip):
    return jnp.bitwise_xor(place_ref[0], flip)


def strip(index, size):
    return pl.ds(pl.multiple_of(index * size, size), size)


def transpose_columns(weight_ref, out_ref):
    for i in range(0, weight_ref.shape[1], LANES):
        out_ref[i : i + LANES, :] = weight_ref[:, i : i + LANES].T


def cost(flops, moved):
    return pl.CostEstimate(flops=int(flops), bytes_accessed=int(moved), transcendentals=0)


def position_bias(vec_ref, bias_ref):
    heads, size, _ = bias_ref.shape
    key = lax.broadcasted_iota(jnp.int32, (size, size), 0)
    query = lax.broadcasted_iota(jnp.int32, (size, size), 1)
    for h in range(heads):
        rows = jnp.broadcast_to(vec_ref[h : h + 1, :], (size, size))
        rolled = pltpu.roll(rows, 0, 1, stride=1, stride_axis=0)
        bias_ref[h] = jnp.where(key <= query, rolled, MASKED)


def self_forward_kernel(
    x_ref, gain_ref, w_ref, vec_ref, qkv_ref, out_ref, lse_ref, wt_ref, bias_ref
):
    heads = bias_ref.shape[0]
    width = heads * HD

    @pl.when(pl.program_id(0) == 0)
    def _():
        transpose_columns(w_ref, wt_ref)
        position_bias(vec_ref, bias_ref)

    normed = root_norm(x_ref[0].astype(F32), gain_ref[...]).astype(BF16)
    qkv = dot(wt_ref[...], normed, (1, 1)).astype(BF16)
    qkv_ref[0] = qkv
    lse_ref[...] = jnp.zeros_like(lse_ref)
    piece = lambda part, h: qkv[width * part + HD * h : width * part + HD * (h + 1)]
    following = dot(piece(1, 0), piece(0, 0), (0, 0))
    for h in range(heads):
        s = following + bias_ref[h]
        if h + 1 < heads:
            following = dot(piece(1, h + 1), piece(0, h + 1), (0, 0))
        peak = jnp.max(s, axis=0, keepdims=True)
        raised = jnp.exp(s - peak)
        total = jnp.sum(raised, axis=0, keepdims=True)
        weight = (raised * (1.0 / total)).astype(BF16)
        out_ref[0, HD * h : HD * (h + 1), :] = dot(piece(2, h), weight).astype(BF16)
        lse_ref[0, h : h + 1, :] = peak + jnp.log(total)


def self_forward(x, gain, weight, vec, heads):
    examples, length, model = x.shape
    feats = weight.shape[1]
    whole = lambda *shape: pl.BlockSpec(shape, lambda e: (0,) * len(shape))
    per = lambda *shape: pl.BlockSpec((1, *shape), lambda e: (e, 0, 0))
    return pl.pallas_call(
        self_forward_kernel,
        grid=(examples,),
        in_specs=[
            per(length, model),
            whole(1, model),
            whole(*weight.shape),
            whole(*vec.shape),
        ],
        out_specs=[
            per(feats, length),
            per(heads * HD, length),
            per(8, length),
            whole(feats, model),
        ],
        out_shape=[
            jax.ShapeDtypeStruct((examples, feats, length), BF16),
            jax.ShapeDtypeStruct((examples, heads * HD, length), BF16),
            jax.ShapeDtypeStruct((examples, 8, length), F32),
            jax.ShapeDtypeStruct((feats, model), BF16),
        ],
        scratch_shapes=[pltpu.VMEM((heads, length, length), F32)],
        compiler_params=pltpu.CompilerParams(vmem_limit_bytes=48 << 20),
        cost_estimate=cost(9e-6 * PEAK_FLOPS, 8e6),
        name="self_forward",
    )(x, gain, weight, vec)


def self_backward_kernel(
    place_ref, x_ref, gain_ref, qkv_ref, do0_ref, do1_ref, do2_ref, do3_ref, lse_ref, wt_ref, vec_ref,
    dn_ref, gw_ref, dvec_ref, g_gain_ref,
    bias_ref, dsum_ref, dqkv_ref, do_ref, sum_ref,
):
    heads, size, _ = bias_ref.shape
    width = heads * HD
    e = pl.program_id(0)

    @pl.when(e == 0)
    def _():
        position_bias(vec_ref, bias_ref)
        dsum_ref[...] = jnp.zeros_like(dsum_ref)
        sum_ref[...] = jnp.zeros_like(sum_ref)
        dqkv_ref[...] = jnp.zeros_like(dqkv_ref)
        g_gain_ref[...] = jnp.zeros_like(g_gain_ref)

    for flip, piece_ref in enumerate((do0_ref, do1_ref, do2_ref, do3_ref)):
        do_ref[:, strip(place_index(place_ref, flip), piece_ref.shape[2])] = piece_ref[0]
    piece = lambda part, h: qkv_ref[0, width * part + HD * h : width * part + HD * (h + 1), :]
    out = lambda h: do_ref[HD * h : HD * (h + 1), :]
    products = lambda h: (dot(piece(1, h), piece(0, h), (0, 0)), dot(piece(2, h), out(h), (0, 0)))
    following = products(0)
    for h in range(heads):
        s, dp = following
        if h + 1 < heads:
            following = products(h + 1)
        p = jnp.exp(s + bias_ref[h] - lse_ref[0, h : h + 1, :])
        inner = jnp.sum(p * dp, axis=0, keepdims=True)
        ds = p * (dp - inner)
        dsum_ref[h] += ds
        ds = ds.astype(BF16)
        at = lambda part: slice(width * part + HD * h, width * part + HD * (h + 1))
        dqkv_ref[:, at(0)] = dot(piece(1, h), ds).T.astype(BF16)
        dqkv_ref[:, at(1)] = dot(ds, piece(0, h), (1, 1)).astype(BF16)
        dqkv_ref[:, at(2)] = dot(p.astype(BF16), out(h), (1, 1)).astype(BF16)
    dqkv = dqkv_ref[...]
    dn = dot(dqkv, wt_ref[...])
    dn_ref[0] = dn.astype(BF16)
    x = x_ref[0].astype(F32)
    scaled = x * lax.rsqrt(jnp.mean(x * x, axis=-1, keepdims=True) + NORM_EPS)
    g_gain_ref[...] += jnp.sum(dn * scaled, axis=0, keepdims=True)
    sum_ref[...] += dot((scaled * gain_ref[...]).astype(BF16), dqkv, (0, 0))

    @pl.when(e == pl.num_programs(0) - 1)
    def _():
        gw_ref[...] = sum_ref[...].astype(BF16)
        dvec_ref[...] = jnp.zeros_like(dvec_ref)
        for h in range(heads):
            back, count = dsum_ref[h], size
            while count > 8:
                count //= 2
                back = back[:count] + pltpu.roll(back[count:], size - count, 1)
            total = back[:1]
            for r in range(1, count):
                total = total + pltpu.roll(back[r : r + 1], size - r, 1)
            dvec_ref[h : h + 1, :] = total


def self_backward(place, x, gain, qkv, do, lse, wt, vec, heads):
    examples, length, model = x.shape
    feats = wt.shape[0]
    whole = lambda *shape: pl.BlockSpec(shape, lambda e: (0,) * len(shape))
    per = lambda *shape: pl.BlockSpec((1, *shape), lambda e: (e, 0, 0))
    return pl.pallas_call(
        self_backward_kernel,
        grid=(examples,),
        in_specs=[
            pl.BlockSpec(memory_space=pltpu.SMEM),
            per(length, model),
            whole(1, model),
            per(feats, length),
            *[per(heads * HD, length // 4)] * 4,
            per(8, length),
            whole(*wt.shape),
            whole(*vec.shape),
        ],
        out_specs=[per(length, model), whole(model, feats), whole(8, length), whole(1, model)],
        out_shape=[
            jax.ShapeDtypeStruct((examples, length, model), BF16),
            jax.ShapeDtypeStruct((model, feats), BF16),
            jax.ShapeDtypeStruct((8, length), F32),
            jax.ShapeDtypeStruct((1, model), F32),
        ],
        scratch_shapes=[
            pltpu.VMEM((heads, length, length), F32),
            pltpu.VMEM((heads, length, length), F32),
            pltpu.VMEM((length, feats), BF16),
            pltpu.VMEM((heads * HD, length), BF16),
            pltpu.VMEM((model, feats), F32),
        ],
        compiler_params=pltpu.CompilerParams(vmem_limit_bytes=48 << 20),
        cost_estimate=cost(16e-6 * PEAK_FLOPS, 12e6),
        name="self_backward",
    )(place, x, gain, qkv, *do, lse, wt, vec)


def work_list(live):
    examples, blocks = live.shape
    flat = live.reshape(-1)
    index = jnp.arange(flat.shape[0], dtype=jnp.int32)
    block = index % blocks
    visit = (flat > 0) | (block == 0)
    before = jnp.sum(jnp.where(visit[None, :] & (index[None, :] < index[:, None]), 1, 0), axis=1)
    ends = visit & ~jnp.any(
        visit[None, :] & (index[None, :] > index[:, None]) & (index[None, :] // blocks == index[:, None] // blocks), axis=1
    )
    chosen = (before[None, :] == index[:, None]) & visit[None, :]
    take = lambda values: jnp.sum(jnp.where(chosen, values[None, :], 0), axis=1)
    final = jnp.max(jnp.where(visit, index, 0))
    found = jnp.any(chosen, axis=1)
    at = jnp.where(found, take(index), final)
    rows = [at // blocks, at % blocks, take(flat), found & (at % blocks == 0), take(ends.astype(jnp.int32))]
    return jnp.stack([r.astype(jnp.int32) for r in rows])


def memory_project_kernel(work_ref, own_ref, other_ref, w_ref, k_ref, v_ref, wt_ref):
    i = pl.program_id(0)
    block, live = work_ref[1, i], work_ref[2, i]
    half = wt_ref.shape[0] // 2
    own_blocks = 2

    @pl.when(i == 0)
    def _():
        transpose_columns(w_ref, wt_ref)

    def project(rows):
        both = dot(wt_ref[...], rows, (1, 1)).astype(BF16)
        k_ref[0] = both[:half]
        v_ref[0] = both[half:]

    @pl.when((live > 0) & (block < own_blocks))
    def _():
        project(own_ref[0])

    @pl.when((live > 0) & (block >= own_blocks))
    def _():
        project(other_ref[0])


def memory_project(work, own, other, weight):
    examples, rows, model = own.shape
    half = rows // ROW_BLOCK
    feats = weight.shape[1] // 2
    row_spec = lambda first: pl.BlockSpec(
        (1, ROW_BLOCK, model), lambda i, work: (work[0, i], jnp.clip(work[1, i] - first, 0, half - 1), 0)
    )
    out_spec = pl.BlockSpec((1, feats, ROW_BLOCK), lambda i, work: (work[0, i], 0, work[1, i]))
    out = jax.ShapeDtypeStruct((examples, feats, 2 * rows), BF16)
    w_spec = lambda *shape: pl.BlockSpec(shape, lambda i, work: (0, 0))
    return pl.pallas_call(
        memory_project_kernel,
        grid_spec=pltpu.PrefetchScalarGridSpec(
            num_scalar_prefetch=1,
            grid=(work.shape[1],),
            in_specs=[row_spec(0), row_spec(half), w_spec(*weight.shape)],
            out_specs=[out_spec, out_spec, w_spec(2 * feats, model)],
        ),
        out_shape=[out, out, jax.ShapeDtypeStruct((2 * feats, model), BF16)],
        compiler_params=pltpu.CompilerParams(vmem_limit_bytes=48 << 20),
        cost_estimate=cost(12e-6 * PEAK_FLOPS, 12e6),
        name="memory_project",
    )(work, own, other, weight)


def cross_forward_kernel(work_ref, q_ref, k_ref, v_ref, o_ref, lse_ref, peak_ref, total_ref, acc_ref):
    i = pl.program_id(0)
    heads = acc_ref.shape[0] // HD
    live = work_ref[2, i]

    @pl.when(work_ref[3, i] == 1)
    def _():
        peak_ref[...] = jnp.full_like(peak_ref, MASKED)
        total_ref[...] = jnp.zeros_like(total_ref)
        acc_ref[...] = jnp.zeros_like(acc_ref)

    def scores(h):
        at = slice(HD * h, HD * (h + 1))
        return dot(k_ref[0, at, :], q_ref[0, at, :], (0, 0))

    def block(partial):
        following = scores(0)
        for h in range(heads):
            at = slice(HD * h, HD * (h + 1))
            s = following
            if h + 1 < heads:
                following = scores(h + 1)
            if partial:
                s = jnp.where(lax.broadcasted_iota(jnp.int32, s.shape, 0) < live, s, MASKED)
            before = peak_ref[h : h + 1, :]
            peak = jnp.maximum(before, jnp.max(s, axis=0, keepdims=True))
            p = jnp.exp(s - peak)
            shrink = jnp.exp(before - peak)
            peak_ref[h : h + 1, :] = peak
            total_ref[h : h + 1, :] = total_ref[h : h + 1, :] * shrink + jnp.sum(p, axis=0, keepdims=True)
            acc_ref[at, :] = acc_ref[at, :] * shrink + dot(v_ref[0, at, :], p.astype(BF16))

    @pl.when(live == ROW_BLOCK)
    def _():
        block(False)

    @pl.when((live > 0) & (live < ROW_BLOCK))
    def _():
        block(True)

    @pl.when(work_ref[4, i] == 1)
    def _():
        total = total_ref[...]
        some = total > 0
        inverse = jnp.where(some, 1.0 / jnp.where(some, total, 1.0), 0.0)
        lse_ref[0] = jnp.where(some, peak_ref[...] + jnp.log(jnp.where(some, total, 1.0)), MASKED)
        for h in range(heads):
            at = slice(HD * h, HD * (h + 1))
            o_ref[0, at, :] = (acc_ref[at, :] * inverse[h : h + 1, :]).astype(o_ref.dtype)


def cross_forward(work, q, k, v):
    examples, feats, length = q.shape
    q_spec = pl.BlockSpec((1, feats, length), lambda i, work: (work[0, i], 0, 0))
    k_spec = pl.BlockSpec((1, feats, ROW_BLOCK), lambda i, work: (work[0, i], 0, work[1, i]))
    l_spec = pl.BlockSpec((1, 8, length), lambda i, work: (work[0, i], 0, 0))
    return pl.pallas_call(
        cross_forward_kernel,
        grid_spec=pltpu.PrefetchScalarGridSpec(
            num_scalar_prefetch=1,
            grid=(work.shape[1],),
            in_specs=[q_spec, k_spec, k_spec],
            out_specs=[q_spec, l_spec],
            scratch_shapes=[
                pltpu.VMEM((8, length), F32),
                pltpu.VMEM((8, length), F32),
                pltpu.VMEM((feats, length), F32),
            ],
        ),
        out_shape=[
            jax.ShapeDtypeStruct((examples, feats, length), BF16),
            jax.ShapeDtypeStruct((examples, 8, length), F32),
        ],
        compiler_params=pltpu.CompilerParams(vmem_limit_bytes=48 << 20),
        cost_estimate=cost(30e-6 * PEAK_FLOPS, 16e6),
        name="cross_forward",
    )(work, q, k, v)


def cross_backward_kernel(
    work_ref, place_ref, q_ref, do0_ref, do1_ref, do2_ref, do3_ref, lse_ref, in0_ref, in1_ref, in2_ref, in3_ref,
    k_ref, v_ref, dq_ref, dkv_ref, acc_ref, do_ref, inner_ref,
):
    i = pl.program_id(0)
    feats = acc_ref.shape[0]
    heads = feats // HD
    live = work_ref[2, i]

    @pl.when(work_ref[3, i] == 1)
    def _():
        acc_ref[...] = jnp.zeros_like(acc_ref)
        for pieces, full_ref in (
            ((do0_ref, do1_ref, do2_ref, do3_ref), do_ref),
            ((in0_ref, in1_ref, in2_ref, in3_ref), inner_ref),
        ):
            for flip, piece_ref in enumerate(pieces):
                full_ref[:, strip(place_index(place_ref, flip), piece_ref.shape[2])] = piece_ref[0]

    def products(h):
        at = slice(HD * h, HD * (h + 1))
        return dot(k_ref[0, at, :], q_ref[0, at, :], (0, 0)), dot(v_ref[0, at, :], do_ref[at, :], (0, 0))

    def block(partial):
        following = products(0)
        for h in range(heads):
            at = slice(HD * h, HD * (h + 1))
            s, dp = following
            if h + 1 < heads:
                following = products(h + 1)
            p = jnp.exp(s - lse_ref[0, h : h + 1, :])
            if partial:
                p = jnp.where(lax.broadcasted_iota(jnp.int32, s.shape, 0) < live, p, 0.0)
            ds = (p * (dp - inner_ref[h : h + 1, :])).astype(BF16)
            acc_ref[at, :] += dot(k_ref[0, at, :], ds)
            dkv_ref[0, :, at] = dot(ds, q_ref[0, at, :], (1, 1)).astype(BF16)
            dkv_ref[0, :, feats + HD * h : feats + HD * (h + 1)] = dot(p.astype(BF16), do_ref[at, :], (1, 1)).astype(BF16)

    @pl.when(live == ROW_BLOCK)
    def _():
        block(False)

    @pl.when((live > 0) & (live < ROW_BLOCK))
    def _():
        block(True)

    @pl.when(work_ref[4, i] == 1)
    def _():
        dq_ref[0] = acc_ref[...].T.astype(BF16)


def cross_backward(work, place, q, do, lse, inner, k, v):
    examples, feats, length = q.shape
    rows = k.shape[2]
    of_example = lambda *shape: pl.BlockSpec((1, *shape), lambda i, work, place: (work[0, i], 0, 0))
    k_spec = pl.BlockSpec((1, feats, ROW_BLOCK), lambda i, work, place: (work[0, i], 0, work[1, i]))
    d_spec = pl.BlockSpec((1, ROW_BLOCK, 2 * feats), lambda i, work, place: (work[0, i], work[1, i], 0))
    return pl.pallas_call(
        cross_backward_kernel,
        grid_spec=pltpu.PrefetchScalarGridSpec(
            num_scalar_prefetch=2,
            grid=(work.shape[1],),
            in_specs=[
                of_example(feats, length),
                *[of_example(feats, length // 4)] * 4,
                of_example(8, length),
                *[of_example(8, length // 4)] * 4,
                k_spec,
                k_spec,
            ],
            out_specs=[of_example(length, feats), d_spec],
            scratch_shapes=[
                pltpu.VMEM((feats, length), F32),
                pltpu.VMEM((feats, length), BF16),
                pltpu.VMEM((8, length), F32),
            ],
        ),
        out_shape=[
            jax.ShapeDtypeStruct((examples, length, feats), BF16),
            jax.ShapeDtypeStruct((examples, rows, 2 * feats), BF16),
        ],
        compiler_params=pltpu.CompilerParams(vmem_limit_bytes=48 << 20),
        cost_estimate=cost(45e-6 * PEAK_FLOPS, 24e6),
        name="cross_backward",
    )(work, place, q, *do, lse, *inner, k, v)


def memory_backward_kernel(
    live_ref, own_ref, other_ref, dkv_ref, wt_ref, out_ref, out_other_ref, g_ref, sum_ref
):
    e, j = pl.program_id(0), pl.program_id(1)
    own_blocks = pl.num_programs(1) // 2

    @pl.when((e == 0) & (j == 0))
    def _():
        sum_ref[...] = jnp.zeros_like(sum_ref)

    for mine, rows_ref, to_ref in ((j < own_blocks, own_ref, out_ref), (j >= own_blocks, other_ref, out_other_ref)):

        @pl.when(mine & (live_ref[e, j] > 0))
        def _():
            dkv = dkv_ref[0]
            sum_ref[...] += dot(rows_ref[0], dkv, (0, 0))
            to_ref[0] = dot(dkv, wt_ref[...]).astype(BF16)

        @pl.when(mine & (live_ref[e, j] == 0))
        def _():
            to_ref[0] = jnp.zeros_like(to_ref[0])

    @pl.when((e == pl.num_programs(0) - 1) & (j == pl.num_programs(1) - 1))
    def _():
        g_ref[...] = sum_ref[...].astype(BF16)


def memory_backward(live, own, other, dkv, wt):
    examples, count, model = own.shape
    width = dkv.shape[2]
    half = count // ROW_BLOCK
    row_spec = lambda first: pl.BlockSpec(
        (1, ROW_BLOCK, model), lambda e, j, live: (e, jnp.clip(j - first, 0, half - 1), 0)
    )
    d_spec = pl.BlockSpec((1, ROW_BLOCK, width), lambda e, j, live: (e, j, 0))
    w_spec = pl.BlockSpec(wt.shape, lambda e, j, live: (0, 0))
    return pl.pallas_call(
        memory_backward_kernel,
        grid_spec=pltpu.PrefetchScalarGridSpec(
            num_scalar_prefetch=1,
            grid=(examples, 2 * half),
            in_specs=[row_spec(0), row_spec(half), d_spec, w_spec],
            out_specs=[row_spec(0), row_spec(half), pl.BlockSpec((model, width), lambda e, j, live: (0, 0))],
            scratch_shapes=[pltpu.VMEM((model, width), F32)],
        ),
        out_shape=[
            jax.ShapeDtypeStruct(own.shape, BF16),
            jax.ShapeDtypeStruct(own.shape, BF16),
            jax.ShapeDtypeStruct((model, width), BF16),
        ],
        compiler_params=pltpu.CompilerParams(vmem_limit_bytes=48 << 20),
        cost_estimate=cost(18e-6 * PEAK_FLOPS, 30e6),
        name="memory_backward",
    )(live, own, other, dkv, wt)


def self_output_kernel(
    place_ref, x_ref, o0_ref, o1_ref, o2_ref, o3_ref, mine_ref, other_ref, gain_ref,
    n2_ref, q_ref, x1_ref, own_o_ref, wo_ref, wq_ref,
    rows_ref,
):
    core = jnp.bitwise_and(place_ref[0], 1)
    feats = wq_ref.shape[1]
    width = o0_ref.shape[1]
    own = x1_ref.shape[1]

    @pl.when(pl.program_id(0) == 0)
    def _():
        for i, from_ref in ((core, mine_ref), (1 - core, other_ref)):
            wo_ref[:, strip(i, feats)] = from_ref[:, feats:]
        for i, from_ref in enumerate((mine_ref, other_ref)):
            for at in range(0, feats, LANES):
                wq_ref[i, at : at + LANES, :] = from_ref[:, at : at + LANES].T

    x1 = x_ref[0].astype(F32)
    for flip, o_ref in enumerate((o0_ref, o1_ref, o2_ref, o3_ref)):
        heads = strip(place_index(place_ref, flip), width)
        x1 += dot(o_ref[0], wo_ref[heads, :], (0, 0))
        own_o_ref[0, heads, :] = o_ref[0, :, strip(place_ref[0], own)]
    n2 = root_norm(x1, gain_ref[...]).astype(BF16)
    n2_ref[0] = n2
    q_ref[0] = dot(wq_ref[0], n2, (1, 1)).astype(BF16)
    rows_ref[...] = x1
    x1_ref[0] = rows_ref[strip(place_ref[0], own), :]


def self_output_stage(place, x, pieces, mine, other, gain):
    examples, length, model = x.shape
    own, feats, width = length // 4, model // 2, pieces[0].shape[1]
    whole = lambda *shape: pl.BlockSpec(shape, lambda e: (0,) * len(shape))
    per = lambda *shape: pl.BlockSpec((1, *shape), lambda e: (e, 0, 0))
    array = jax.ShapeDtypeStruct
    return pl.pallas_call(
        self_output_kernel,
        grid=(examples,),
        in_specs=[pl.BlockSpec(memory_space=pltpu.SMEM), per(length, model)]
        + [per(width, length)] * 4
        + [whole(*mine.shape), whole(*other.shape), whole(1, model)],
        out_specs=[
            per(length, model),
            per(feats, length),
            per(own, model),
            per(model, own),
            whole(model, model),
            whole(2, feats, model),
        ],
        out_shape=[
            array((examples, length, model), BF16),
            array((examples, feats, length), BF16),
            array((examples, own, model), F32),
            array((examples, model, own), BF16),
            array((model, model), BF16),
            array((2, feats, model), BF16),
        ],
        scratch_shapes=[pltpu.VMEM((length, model), F32)],
        compiler_params=pltpu.CompilerParams(vmem_limit_bytes=48 << 20),
        cost_estimate=cost(6e-6 * PEAK_FLOPS, 10e6),
        name="self_output_stage",
    )(place, x, *pieces, mine, other, gain)


def combine_kernel(place_ref, o_ref, came_ref, lse_ref, other_lse_ref, chip_ref, total_ref):
    row = lax.shift_right_logical(place_ref[0], 1)
    here = strip(row, came_ref.shape[2])
    one, two = lse_ref[0], other_lse_ref[0]
    peak = jnp.maximum(one, two)
    total_ref[0] = peak + jnp.log(jnp.exp(one - peak) + jnp.exp(two - peak))
    own_weight = jnp.exp(lse_ref[0, :, here] - total_ref[0, :, here])
    other_weight = jnp.exp(other_lse_ref[0, :, here] - total_ref[0, :, here])
    for h in range(o_ref.shape[1] // HD):
        at = slice(HD * h, HD * (h + 1))
        one = o_ref[0, at, here].astype(F32) * own_weight[h : h + 1, :]
        chip_ref[0, at, :] = (one + came_ref[0, at, :].astype(F32) * other_weight[h : h + 1, :]).astype(BF16)


def combine(place, o, came, lse, other_lse):
    examples, feats, length = o.shape
    per = lambda *shape: pl.BlockSpec((1, *shape), lambda e: (e, 0, 0))
    return pl.pallas_call(
        combine_kernel,
        grid=(examples,),
        in_specs=[
            pl.BlockSpec(memory_space=pltpu.SMEM),
            per(feats, length),
            per(feats, length // 2),
            per(8, length),
            per(8, length),
        ],
        out_specs=[per(feats, length // 2), per(8, length)],
        out_shape=[
            jax.ShapeDtypeStruct((examples, feats, length // 2), BF16),
            jax.ShapeDtypeStruct((examples, 8, length), F32),
        ],
        compiler_params=pltpu.CompilerParams(vmem_limit_bytes=24 << 20),
        cost_estimate=cost(2e-6 * PEAK_FLOPS, 3e6),
        name="combine",
    )(place, o, came, lse, other_lse)


def norm_back(values, gain, grad):
    scale = lax.rsqrt(jnp.mean(values * values, axis=-1, keepdims=True) + NORM_EPS)
    pulled = grad * gain
    inner = jnp.mean(values * pulled, axis=-1, keepdims=True)
    back = scale * pulled - values * (scale * scale * scale * inner)
    return back, jnp.sum(grad * values * scale, axis=0, keepdims=True)


def feed_forward_kernel(
    place_ref, x1_ref, mine_ref, other_ref, dy_ref, gain_ref, wo_ref, gate_ref, up_ref, down_ref,
    out_ref, dx2_ref, doc_mine_ref, doc_other_ref, inner_mine_ref, inner_other_ref,
    g_ref, g_sent_ref, g_down_ref, g_down_sent_ref, g_out_ref, g_out_sent_ref, g_gain_ref,
    x2_ref, n3_ref, sum_ref, dn3_ref, g_full_ref, *, piece,
):
    i = pl.program_id(0)
    core = jnp.bitwise_and(place_ref[0], 1)
    examples, feats, own = mine_ref.shape

    def deal(low, high, keep_ref, sent_ref):
        keep_ref[...] = jnp.where(core == 0, low, high).astype(BF16)
        sent_ref[...] = jnp.where(core == 0, high, low).astype(BF16)
    sides = ((core, mine_ref, doc_mine_ref, inner_mine_ref), (1 - core, other_ref, doc_other_ref, inner_other_ref))

    @pl.when(i == 0)
    def _():
        for e in range(examples):
            x2 = x1_ref[own * e : own * (e + 1), :]
            for side, o_ref, *_ in sides:
                x2 += dot(o_ref[e], wo_ref[strip(side, feats), :], (0, 0))
            x2_ref[own * e : own * (e + 1), :] = x2
        n3_ref[...] = root_norm(x2_ref[...], gain_ref[...]).astype(BF16)
        sum_ref[...] = jnp.zeros_like(sum_ref)
        dn3_ref[...] = jnp.zeros_like(dn3_ref)

    n3, dy = n3_ref[...], dy_ref[...]
    a, u = dot(n3, gate_ref[...]), dot(n3, up_ref[...])
    dh = dot(dy, down_ref[...], (1, 1))
    root = math.sqrt(2 / math.pi)
    bent = jnp.tanh(root * (a + 0.044715 * (a * a * a)))
    rise = 0.5 * (1.0 + bent)
    gelu = a * rise
    slope = rise + 0.5 * a * (1.0 - bent * bent) * (root * (1.0 + 3 * 0.044715 * (a * a)))
    hidden = (gelu * u).astype(BF16)
    da = (dh * u * slope).astype(BF16)
    du = (dh * gelu).astype(BF16)
    sum_ref[...] += dot(hidden, down_ref[...])
    g_down = dot(hidden, dy, (0, 0))
    pieces = g_down.reshape(g_down.shape[0] // (2 * piece), 2, piece, g_down.shape[1])
    deal(*(pieces[:, side].reshape(g_down_ref.shape) for side in range(2)), g_down_ref, g_down_sent_ref)
    deal(dot(n3, da, (0, 0)), dot(n3, du, (0, 0)), g_ref, g_sent_ref)
    dn3_ref[...] += dot(da, gate_ref[...], (1, 1)) + dot(du, up_ref[...], (1, 1))

    @pl.when(i == pl.num_programs(0) - 1)
    def _():
        x2 = x2_ref[...]
        out_ref[...] = (x2 + sum_ref[...]).astype(BF16)
        back, g_gain = norm_back(x2, gain_ref[...], dn3_ref[...])
        g_gain_ref[...] = g_gain
        dx2 = dy_ref[...].astype(F32) + back
        dx2_ref[...] = dx2
        n3_ref[...] = dx2.astype(BF16)
        for side, o_ref, doc_ref, inner_ref in sides:
            heads = strip(side, feats)
            total = jnp.zeros((feats, wo_ref.shape[1]), F32)
            inner_ref[...] = jnp.zeros_like(inner_ref)
            for e in range(examples):
                dx2r = n3_ref[own * e : own * (e + 1), :]
                total += dot(o_ref[e], dx2r)
                doc = dot(wo_ref[heads, :], dx2r, (1, 1)).astype(BF16)
                doc_ref[e] = doc
                product = doc.astype(F32) * o_ref[e].astype(F32)
                for h in range(feats // HD):
                    inner_ref[e, h : h + 1, :] = jnp.sum(product[HD * h : HD * (h + 1)], axis=0, keepdims=True)
            g_full_ref[heads, :] = total
        deal(g_full_ref[:, :feats], g_full_ref[:, feats:], g_out_ref, g_out_sent_ref)


def feed_forward(place, x1, mine, other, dy, gain, wide_w, down, piece):
    tokens, model = x1.shape
    examples, feats, own = mine.shape
    hidden = down.shape[0]
    part = 256
    whole = lambda *shape: pl.BlockSpec(shape, lambda i: (0,) * len(shape))
    first = model // part
    array = jax.ShapeDtypeStruct
    return pl.pallas_call(
        functools.partial(feed_forward_kernel, piece=piece),
        grid=(hidden // part,),
        in_specs=[
            pl.BlockSpec(memory_space=pltpu.SMEM),
            whole(tokens, model),
            whole(*mine.shape),
            whole(*other.shape),
            whole(tokens, model),
            whole(1, model),
            whole(model, model),
            pl.BlockSpec((model, part), lambda i: (0, first + i)),
            pl.BlockSpec((model, part), lambda i: (0, first + hidden // part + i)),
            pl.BlockSpec((part, model), lambda i: (i, 0)),
        ],
        out_specs=[
            whole(tokens, model),
            whole(tokens, model),
            whole(*mine.shape),
            whole(*mine.shape),
            whole(examples, 8, own),
            whole(examples, 8, own),
            *[pl.BlockSpec((model, part), lambda i: (0, i))] * 2,
            *[pl.BlockSpec((part // 2, model), lambda i: (i, 0))] * 2,
            *[whole(model, feats)] * 2,
            whole(1, model),
        ],
        out_shape=[
            array((tokens, model), BF16),
            array((tokens, model), F32),
            array(mine.shape, BF16),
            array(mine.shape, BF16),
            array((examples, 8, own), F32),
            array((examples, 8, own), F32),
            *[array((model, hidden), BF16)] * 2,
            *[array((hidden // 2, model), BF16)] * 2,
            *[array((model, feats), BF16)] * 2,
            array((1, model), F32),
        ],
        scratch_shapes=[
            pltpu.VMEM((tokens, model), F32),
            pltpu.VMEM((tokens, model), BF16),
            pltpu.VMEM((tokens, model), F32),
            pltpu.VMEM((tokens, model), F32),
            pltpu.VMEM((model, model), F32),
        ],
        compiler_params=pltpu.CompilerParams(vmem_limit_bytes=48 << 20),
        cost_estimate=cost(20e-6 * PEAK_FLOPS, 24e6),
        name="feed_forward",
    )(place, x1, mine, other, dy, gain, wide_w, wide_w, wide_w, down)


def self_output_back_kernel(
    place_ref, mine_ref, other_ref, wq_ref, x1_ref, gain_ref, dx2_ref, own_o_ref, wo_ref,
    dx1_ref, do_mine_ref, do_pair_ref, do_across_ref, g_keep_ref, g_sent_ref, g_gain_ref,
    sum_ref, do_ref,
):
    e = pl.program_id(0)
    core, row = jnp.bitwise_and(place_ref[0], 1), lax.shift_right_logical(place_ref[0], 1)
    width, feats = do_mine_ref.shape[1], do_across_ref.shape[1]

    @pl.when(e == 0)
    def _():
        sum_ref[...] = jnp.zeros_like(sum_ref)
        g_gain_ref[...] = jnp.zeros_like(g_gain_ref)

    dn2 = dot(mine_ref[0], wq_ref[0]) + dot(other_ref[0], wq_ref[1])
    back, g_gain = norm_back(x1_ref[0], gain_ref[...], dn2)
    g_gain_ref[...] += g_gain
    dx1 = dx2_ref[0] + back
    dx1_ref[0] = dx1
    dx1r = dx1.astype(BF16)
    do_ref[...] = dot(wo_ref[...], dx1r, (1, 1)).astype(BF16)
    do_mine_ref[0] = do_ref[strip(place_ref[0], width), :]
    do_pair_ref[0] = do_ref[strip(place_index(place_ref, 1), width), :]
    do_across_ref[0] = do_ref[strip(1 - row, feats), :]
    sum_ref[...] += dot(own_o_ref[0], dx1r)

    @pl.when(e == pl.num_programs(0) - 1)
    def _():
        g_keep_ref[...] = sum_ref[:, strip(core, feats)].astype(BF16)
        g_sent_ref[...] = sum_ref[:, strip(1 - core, feats)].astype(BF16)


def self_output_back(place, mine, other, wq, x1, gain, dx2, own_o, wo):
    examples, own, model = x1.shape
    feats = mine.shape[2]
    whole = lambda *shape: pl.BlockSpec(shape, lambda e: (0,) * len(shape))
    per = lambda *shape: pl.BlockSpec((1, *shape), lambda e: (e, 0, 0))
    array = jax.ShapeDtypeStruct
    return pl.pallas_call(
        self_output_back_kernel,
        grid=(examples,),
        in_specs=[
            pl.BlockSpec(memory_space=pltpu.SMEM),
            per(own, feats),
            per(own, feats),
            whole(*wq.shape),
            per(own, model),
            whole(1, model),
            per(own, model),
            per(model, own),
            whole(model, model),
        ],
        out_specs=[
            per(own, model),
            *[per(model // 4, own)] * 2,
            per(feats, own),
            *[whole(model, feats)] * 2,
            whole(1, model),
        ],
        out_shape=[
            array((examples, own, model), F32),
            *[array((examples, model // 4, own), BF16)] * 2,
            array((examples, feats, own), BF16),
            *[array((model, feats), BF16)] * 2,
            array((1, model), F32),
        ],
        scratch_shapes=[pltpu.VMEM((model, model), F32), pltpu.VMEM((model, own), BF16)],
        compiler_params=pltpu.CompilerParams(vmem_limit_bytes=48 << 20),
        cost_estimate=cost(4e-6 * PEAK_FLOPS, 8e6),
        name="self_output_back",
    )(place, mine, other, wq, x1, gain, dx2, own_o, wo)


def fold_rows(rows, target, columns):
    rest = rows * columns // target
    tile = 16
    if rows % tile or rows // tile * LANES != rest or columns // LANES * tile != target:
        return (lambda b: b.reshape(*b.shape[:-2], target, rest)), (lambda b: b.reshape(rows, columns))

    def swap(b, down, across):
        b = b.reshape(*b.shape[:-2], down, tile, across, LANES)
        return jnp.swapaxes(b, -4, -2).reshape(*b.shape[:-4], across * tile, down * LANES)

    return (lambda b: swap(b, rows // tile, columns // LANES)), (lambda b: swap(b, target // tile, rest // LANES))


def local(
    dec_input,
    enc_out,
    enc_len,
    cotangent,
    self_query,
    self_key,
    self_value,
    self_output,
    cross_query,
    cross_key,
    cross_value,
    cross_output,
    ffn_gate,
    ffn_up,
    ffn_down,
    self_gain,
    cross_gain,
    ffn_gain,
    bias_table,
):
    place = lax.axis_index("narrow")
    row, core = place // 2, place % 2
    wide = lax.axis_size("wide")
    examples, own, model = dec_input.shape
    length = 4 * own
    heads = model // HD
    own_heads = heads // 4
    memory_rows = enc_out.shape[1]
    share = self_query.shape[0]

    half = lambda w: part_of(w.astype(BF16), core, 2, 1)
    own_qkv = jnp.concatenate(
        [part_of(w.astype(BF16), place, 4, 1) for w in (self_query, self_key, self_value)], 1
    )
    own_qkv = jnp.pad(own_qkv, ((0, 0), (0, -own_qkv.shape[1] % LANES)))
    small = jnp.stack([self_gain, cross_gain, ffn_gain, jnp.pad(bias_table, (0, share - bias_table.shape[0]))], 1)
    small = jnp.pad(small.astype(BF16), ((0, 0), (0, LANES - 4)))
    feats = model // 2
    self_w, small = wide_gather(jnp.concatenate([own_qkv, small], 1), (own_qkv.shape[1], LANES))
    small_rows = small[:, :4].astype(F32).T
    gain_one, gain_two, gain_three = (small_rows[i : i + 1] for i in range(3))
    table = small_rows[3].reshape(wide, share)[:, : bias_table.shape[0]].reshape(BUCKETS, heads)

    both = ("wide", "narrow")
    quarter = lambda w: part_of(w.astype(BF16), place, 4, 0)
    ffn_in = lax.all_gather(
        jnp.concatenate([quarter(cross_output), quarter(ffn_gate), quarter(ffn_up)], 1), both, axis=0, tiled=True
    )
    down_w = lax.all_gather(quarter(ffn_down), both, axis=0, tiled=True)

    enc_other = pair_swap(enc_out)
    starts = (place * memory_rows + np.arange(memory_rows // ROW_BLOCK) * ROW_BLOCK).astype(jnp.int32)
    other_starts = starts + (1 - 2 * core) * memory_rows
    block_starts = jnp.concatenate([starts, other_starts])
    live = jnp.clip(enc_len[:, None] - block_starts[None, :], 0, ROW_BLOCK)

    x_all = narrow_gather(dec_input, 1, row, core)
    hot = jnp.asarray(bucket_table(length))
    distance_bias = jnp.dot(table.T, hot, precision=FULL_ACCURACY)
    vec = jnp.pad(part_of(distance_bias, place, 4, 0), ((0, 8 - own_heads), (0, 0)))
    qkv, self_o, self_lse, self_wt = self_forward(x_all, gain_one, self_w, vec, own_heads)
    across_o = across_swap(self_o)
    pieces = [self_o, pair_swap(self_o), across_o, pair_swap(across_o)]
    memory_w = shared_gather(jnp.concatenate([half(cross_key), half(cross_value)], 1), row, first=(self_o,))
    work = work_list(live)
    keys, values, memory_wt = memory_project(work, enc_out, enc_other, memory_w)
    query_out = after(jnp.concatenate([half(cross_query), half(self_output)], 1), self_o)
    (mine_w,) = wide_gather(query_out, (query_out.shape[1],))
    mine_w = after(mine_w, keys)
    other_w = pair_swap(mine_w)
    me = place.reshape(1).astype(jnp.int32)
    n2, cross_q, x1, own_o, self_out_w, cross_query_wt = self_output_stage(
        me, x_all, pieces, mine_w, other_w, gain_two
    )

    part_o, part_lse = cross_forward(work, cross_q, keys, values)
    came = across_swap(part_of(part_o, 1 - row, 2, 2))
    chip_o, lse = combine(me, part_o, came, part_lse, across_swap(part_lse))
    mine_o, other_o = part_of(chip_o, core, 2, 2), pair_swap(part_of(chip_o, 1 - core, 2, 2))

    tokens = examples * own
    down_rows = ffn_down.shape[0] // 2
    (
        layer_out, dx2, doc_mine, doc_other, inner_mine, inner_other,
        gate_up, gate_up_sent, down, down_sent, grad_co, co_sent, grad_gain_three,
    ) = feed_forward(
        me, x1.reshape(tokens, model), mine_o, other_o, cotangent.reshape(tokens, model), gain_three,
        ffn_in, down_w, down_rows,
    )
    layer_out, dx2 = layer_out.reshape(x1.shape), dx2.reshape(x1.shape)

    rows_of = lambda g: g.reshape(wide, share, -1)

    def from_all(mine, other):
        pair = pair_swap(other)
        return [mine, pair, across_swap(mine), across_swap(pair)]

    doc, inner = from_all(doc_mine, doc_other), from_all(inner_mine, inner_other)
    ffn = gate_up, pair_swap(gate_up_sent)
    by_y = lambda y: [part_of(g, y, 2, 1).astype(F32) for g in ffn]
    ffn_sent = sum(by_y(1 - row)).astype(BF16)
    down = plus(down, pair_swap(down_sent)).reshape(wide, down_rows, model)
    co = plus(grad_co, pair_swap(co_sent))
    doc, inner, ffn_sent, down, co = lax.optimization_barrier((doc, inner, ffn_sent, down, co))
    ffn_came, down = across_swap(ffn_sent), wide_scatter_x(down)
    part_dq, dkv = cross_backward(work, me, cross_q, doc, lse, inner, keys, values)
    part_dq, dkv, ffn_came, down = lax.optimization_barrier((part_dq, dkv, ffn_came, down))
    ffn = wide_scatter_x(rows_of(sum(by_y(row), ffn_came.astype(F32)).astype(BF16)))

    dq_came = across_swap(part_of(part_dq, 1 - row, 2, 1))
    enc_mine, enc_swapped, grad_memory = memory_backward(live, enc_out, enc_other, dkv, memory_wt)
    enc_came = pair_swap(enc_swapped)
    dq_came, grad_memory, ffn = lax.optimization_barrier((dq_came, grad_memory, ffn))
    down_came = across_swap(part_of(down, 1 - row, 2, 1))
    chip_dq = plus(part_of(part_dq, row, 2, 1), dq_came)
    dq_mine, dq_other = part_of(chip_dq, core, 2, 1), pair_swap(part_of(chip_dq, 1 - core, 2, 1))
    grad_cross_query = jnp.einsum("etd,etf->df", n2, part_dq, preferred_element_type=F32).astype(BF16)
    late = x_swap(jnp.concatenate([rows_of(g) for g in (grad_cross_query, grad_memory, co)], 2))
    dx1, do_mine, do_pair, do_across, grad_so, so_sent, grad_gain_two = self_output_back(
        me, dq_mine, dq_other, cross_query_wt, x1, gain_two, dx2, own_o, self_out_w
    )

    ffn = z_swap(after(ffn, do_across))

    do_came = across_swap(do_across)
    do = [do_mine, pair_swap(do_pair), part_of(do_came, core, 2, 1), pair_swap(part_of(do_came, 1 - core, 2, 1))]
    so = rows_of(plus(grad_so, pair_swap(so_sent)))
    down = plus(part_of(down, row, 2, 1), down_came)
    do, so, late, down = lax.optimization_barrier((do, so, late, down))
    fold, unfold = fold_rows(down.shape[1], share, model)
    late = z_swap(jnp.concatenate([total(late), fold(down)], 2))
    so_came = across_swap(part_of(so, 1 - row, 2, 1))
    part_dn1, grad_self, dvec, grad_gain_one = self_backward(
        me, x_all, gain_one, qkv, do, self_lse, self_wt, vec, own_heads
    )
    part_dn1, grad_self, so_came, ffn, *early = lax.optimization_barrier((part_dn1, grad_self, so_came, ffn, *late[:-1]))
    late, ffn_sum = (*early, *late[-1:]), total(ffn)

    own_table = jnp.dot(hot, dvec[:own_heads].T, precision=FULL_ACCURACY)
    grad_table = lax.dynamic_update_slice_in_dim(
        jnp.zeros((BUCKETS, heads), F32), own_table, place * own_heads, 1
    )
    small = [g.reshape(wide, -1) for g in (grad_gain_one, grad_gain_two, grad_gain_three, grad_table)]
    small = jnp.concatenate(small, 1).astype(BF16)
    small_count = small.shape[1]
    small = jnp.pad(small, ((0, 0), (0, share // 2 * LANES - small_count))).reshape(wide, -1, LANES)
    so = plus(part_of(so, row, 2, 1), so_came)
    self_width = grad_self.shape[1]
    self_halves = grad_self.reshape(wide, 2, share // 2, self_width)
    last = x_swap(jnp.concatenate([self_halves[:, 0], self_halves[:, 1], so, small], 2))
    by_core = part_dn1.reshape(examples, 2, 2, own, model)
    column = plus(part_of(by_core, core, 2, 2).astype(F32), pair_swap(part_of(by_core, 1 - core, 2, 2)))
    dn1_sent = part_of(column, 1 - row, 2, 1).astype(BF16)
    enc_grad = plus(enc_mine, enc_came)
    sums = jnp.concatenate([ffn_sum, total(late)], 1)
    dn1_came, sums_came = across_swap(dn1_sent), across_swap(sums)
    last, dn1_sent, enc_grad, sums = lax.optimization_barrier((last, dn1_sent, enc_grad, sums))
    last = z_swap(total(last))
    last, dn1_came = lax.optimization_barrier((last, dn1_came))
    last_sum = total(last)
    last_came = across_swap(last_sum)
    dn1 = plus(part_of(column, row, 2, 1), dn1_came)
    grad_in, _ = norm_back(
        dec_input.reshape(tokens, model).astype(F32), gain_one, dn1.reshape(tokens, model)
    )
    input_grad = (dx1 + grad_in.reshape(x1.shape)).astype(BF16)

    bounds = np.cumsum([0, ffn_sum.shape[1], 4 * feats])
    low, high = in_order(row, sums, sums_came)
    sums = jnp.concatenate(
        [
            low[:, : bounds[1]],
            high[:, : bounds[1]],
            plus(sums[:, bounds[1] : bounds[2]], sums_came[:, bounds[1] : bounds[2]]),
            low[:, bounds[2] :],
            high[:, bounds[2] :],
        ],
        1,
    )
    parts = in_order(core, sums, pair_swap(sums))
    gate_sum, up_sum = (part[:, : 2 * bounds[1]] for part in parts)
    cq_sum, ck_sum, cv_sum, co_sum = (
        jnp.concatenate([part[:, 2 * bounds[1] + feats * i : 2 * bounds[1] + feats * (i + 1)] for part in parts], 1)
        for i in range(4)
    )
    down_sum = [jnp.split(part[:, 2 * bounds[1] + 4 * feats :], 2, 1) for part in parts]
    down_sum = jnp.concatenate([unfold(half) for part in down_sum for half in part], 0)

    last = jnp.stack(in_order(row, last_sum, last_came))
    low, high = in_order(core, last, pair_swap(last))
    halves = lambda part: jnp.concatenate([part[:, :self_width], part[:, self_width : 2 * self_width]], 0)
    self_sum = [halves(part[y]) for y in range(2) for part in (low, high)]
    q_sum, k_sum, v_sum = (
        jnp.concatenate([part[:, own_heads * HD * i : own_heads * HD * (i + 1)] for part in self_sum], 1)
        for i in range(3)
    )
    so_sum = jnp.concatenate(
        [part[:, :, 2 * self_width : 2 * self_width + feats].reshape(share, -1) for part in (low, high)], 1
    )
    small_sum = sum(part[y, :, 2 * self_width + feats :].astype(F32) for part in (low, high) for y in range(2))
    small_sum = small_sum.reshape(-1)[:small_count]
    f = lambda a: a.astype(F32)
    return (
        layer_out,
        input_grad,
        enc_grad,
        *(f(g) for g in (q_sum, k_sum, v_sum, so_sum, cq_sum, ck_sum, cv_sum, co_sum, gate_sum, up_sum, down_sum)),
        small_sum[:share],
        small_sum[share : 2 * share],
        small_sum[2 * share : 3 * share],
        small_sum[3 * share :],
    )


def solution(mesh):
    rows = P("wide", "narrow", None)
    weight, vector = P("wide", None), P("wide")
    return jax.shard_map(
        local,
        mesh=mesh,
        in_specs=(rows, rows, vector, rows, *[weight] * 11, *[vector] * 4),
        out_specs=(rows, rows, rows, *[weight] * 11, *[vector] * 4),
        check_vma=False,
    )
```

```python
import functools
import math

import jax
import jax.numpy as jnp
import numpy as np
from jax import lax
from jax.experimental import pallas as pl
from jax.experimental.pallas import tpu as pltpu
from jax.sharding import PartitionSpec as P

HD = 64
BUCKETS = 32
MAXDIST = 128
NORM_EPS = 1e-06
MASKED = -1e30
LANES = 128
ROW_BLOCK = 512
PEAK_FLOPS = 1.15e15
FULL_ACCURACY = lax.Precision.HIGHEST
F32 = jnp.float32
BF16 = jnp.bfloat16

PAIR = ((0, 1), (1, 0), (2, 3), (3, 2))
ACROSS = ((0, 2), (2, 0), (1, 3), (3, 1))


def bucket_table(length):
    exact = BUCKETS // 2
    hot = np.zeros((BUCKETS, length), np.float32)
    for distance in range(length):
        bucket = distance
        if distance >= exact:
            scaled = math.log(distance / exact) / math.log(MAXDIST / exact) * (BUCKETS - exact)
            bucket = min(exact + math.floor(scaled), BUCKETS - 1)
        hot[bucket, distance] = 1.0
    return hot


def dot(left, right, contract=(1, 0)):
    return lax.dot_general(
        left, right, (((contract[0],), (contract[1],)), ((), ())), preferred_element_type=F32
    )


def root_norm(values, gain):
    return values * lax.rsqrt(jnp.mean(values * values, axis=-1, keepdims=True) + NORM_EPS) * gain


def pair_swap(value):
    return lax.ppermute(value, "narrow", PAIR)


def across_swap(value):
    return lax.ppermute(value, "narrow", ACROSS)


def in_order(flag, mine, other):
    first = flag == 0
    return jnp.where(first, mine, other), jnp.where(first, other, mine)


def narrow_gather(value, axis, row, core):
    low, high = in_order(row, value, across_swap(value))
    column = jnp.stack([low, high], axis)
    low, high = in_order(core, column, pair_swap(column))
    full = jnp.stack([low, high], axis + 1)
    shape = list(value.shape)
    shape[axis] *= 4
    return full.reshape(shape)


def plus(mine, came):
    return (mine.astype(F32) + came.astype(F32)).astype(mine.dtype)


def part_of(value, index, parts, axis):
    size = value.shape[axis] // parts
    return lax.dynamic_slice_in_dim(value, index * size, size, axis)


LINE = 4
BESIDE = tuple((i, i ^ 1) for i in range(2 * LINE))


def along(step):
    return [(2 * z + x, 2 * ((z + step) % LINE) + x) for z in range(LINE) for x in range(2)]


def by_planes():
    return lax.axis_size("wide") == 2 * LINE


def assemble_kernel(widths, order_ref, *refs):
    pieces, outs = refs[: 2 * LINE], refs[2 * LINE :]
    for i, piece in enumerate(pieces):
        at = 0
        for width, out in zip(widths, outs):
            out[order_ref[i]] = piece[:, at : at + width]
            at += width


def after(value, *others):
    return lax.optimization_barrier((value, *others))[0]


def wide_gather(block, widths, first=()):
    rows = block.shape[0]
    if not by_planes():
        full = lax.all_gather(block, "wide", axis=0, tiled=True)
        bounds = np.cumsum([0, *widths])
        return [full[:, a:b] for a, b in zip(bounds[:-1], bounds[1:])]
    z, x = lax.axis_index("wide") // 2, lax.axis_index("wide") % 2
    line = [block] + [lax.ppermute(block, "wide", along(step)) for step in range(1, LINE)]
    line = after(line, *first)
    pieces = line + [lax.ppermute(piece, "wide", BESIDE) for piece in line]
    places = (z - np.arange(LINE)) % LINE * 2
    order = jnp.concatenate([places + x, places + 1 - x]).astype(jnp.int32)
    outs = pl.pallas_call(
        functools.partial(assemble_kernel, widths),
        in_specs=[pl.BlockSpec(memory_space=pltpu.SMEM)] + [pl.BlockSpec(memory_space=pltpu.VMEM)] * len(pieces),
        out_specs=[pl.BlockSpec(memory_space=pltpu.VMEM)] * len(widths),
        out_shape=[jax.ShapeDtypeStruct((2 * LINE, rows, width), block.dtype) for width in widths],
        compiler_params=pltpu.CompilerParams(vmem_limit_bytes=16 << 20),
        name="assemble",
    )(order, *pieces)
    return [out.reshape(2 * LINE * rows, out.shape[2]) for out in outs]


def shared_gather(block, row, first=()):
    rows, width = block.shape
    (full,) = wide_gather(part_of(block, row, 2, 0), (width,), first)
    halves = full.reshape(-1, rows // 2, width)
    return jnp.stack(in_order(row, halves, across_swap(halves)), 1).reshape(-1, width)


def pick(value, index, axis):
    return lax.dynamic_index_in_dim(value, index, axis, keepdims=False)


def x_swap(blocks):
    if not by_planes():
        return (blocks,)
    x = lax.axis_index("wide") % 2
    planes = blocks.reshape(LINE, 2, *blocks.shape[1:])
    return pick(planes, x, 1), lax.ppermute(pick(planes, 1 - x, 1), "wide", BESIDE)


def z_swap(planes):
    if not by_planes():
        shape = planes.shape
        return (
            lax.psum_scatter(
                planes.reshape(shape[0] * shape[1], *shape[2:]), "wide", scatter_dimension=0, tiled=True
            ),
        )
    z = lax.axis_index("wide") // 2
    sent = [pick(planes, (z + step) % LINE, 0) for step in range(1, LINE)]
    return pick(planes, z, 0), *(lax.ppermute(s, "wide", along(i + 1)) for i, s in enumerate(sent))


def total(parts):
    return sum((part.astype(F32) for part in parts[1:]), parts[0].astype(F32)).astype(parts[0].dtype)


def wide_scatter_x(blocks):
    return total(x_swap(blocks))


def wide_scatter_z(planes):
    return total(z_swap(planes))


def wide_scatter(blocks):
    return wide_scatter_z(wide_scatter_x(blocks))


def place_index(place_ref, flip):
    return jnp.bitwise_xor(place_ref[0], flip)


def strip(index, size):
    return pl.ds(pl.multiple_of(index * size, size), size)


def transpose_columns(weight_ref, out_ref):
    for i in range(0, weight_ref.shape[1], LANES):
        out_ref[i : i + LANES, :] = weight_ref[:, i : i + LANES].T


def cost(flops, moved):
    return pl.CostEstimate(flops=int(flops), bytes_accessed=int(moved), transcendentals=0)


def position_bias(vec_ref, bias_ref):
    heads, size, _ = bias_ref.shape
    key = lax.broadcasted_iota(jnp.int32, (size, size), 0)
    query = lax.broadcasted_iota(jnp.int32, (size, size), 1)
    for h in range(heads):
        rows = jnp.broadcast_to(vec_ref[h : h + 1, :], (size, size))
        rolled = pltpu.roll(rows, 0, 1, stride=1, stride_axis=0)
        bias_ref[h] = jnp.where(key <= query, rolled, MASKED)


def self_forward_kernel(
    x_ref, gain_ref, w_ref, vec_ref, qkv_ref, out_ref, lse_ref, wt_ref, bias_ref
):
    heads = bias_ref.shape[0]
    width = heads * HD

    @pl.when(pl.program_id(0) == 0)
    def _():
        transpose_columns(w_ref, wt_ref)
        position_bias(vec_ref, bias_ref)

    normed = root_norm(x_ref[0].astype(F32), gain_ref[...]).astype(BF16)
    qkv = dot(wt_ref[...], normed, (1, 1)).astype(BF16)
    qkv_ref[0] = qkv
    lse_ref[...] = jnp.zeros_like(lse_ref)
    piece = lambda part, h: qkv[width * part + HD * h : width * part + HD * (h + 1)]
    following = dot(piece(1, 0), piece(0, 0), (0, 0))
    for h in range(heads):
        s = following + bias_ref[h]
        if h + 1 < heads:
            following = dot(piece(1, h + 1), piece(0, h + 1), (0, 0))
        peak = jnp.max(s, axis=0, keepdims=True)
        raised = jnp.exp(s - peak)
        total = jnp.sum(raised, axis=0, keepdims=True)
        weight = (raised * (1.0 / total)).astype(BF16)
        out_ref[0, HD * h : HD * (h + 1), :] = dot(piece(2, h), weight).astype(BF16)
        lse_ref[0, h : h + 1, :] = peak + jnp.log(total)


def self_forward(x, gain, weight, vec, heads):
    examples, length, model = x.shape
    feats = weight.shape[1]
    whole = lambda *shape: pl.BlockSpec(shape, lambda e: (0,) * len(shape))
    per = lambda *shape: pl.BlockSpec((1, *shape), lambda e: (e, 0, 0))
    return pl.pallas_call(
        self_forward_kernel,
        grid=(examples,),
        in_specs=[
            per(length, model),
            whole(1, model),
            whole(*weight.shape),
            whole(*vec.shape),
        ],
        out_specs=[
            per(feats, length),
            per(heads * HD, length),
            per(8, length),
            whole(feats, model),
        ],
        out_shape=[
            jax.ShapeDtypeStruct((examples, feats, length), BF16),
            jax.ShapeDtypeStruct((examples, heads * HD, length), BF16),
            jax.ShapeDtypeStruct((examples, 8, length), F32),
            jax.ShapeDtypeStruct((feats, model), BF16),
        ],
        scratch_shapes=[pltpu.VMEM((heads, length, length), F32)],
        compiler_params=pltpu.CompilerParams(vmem_limit_bytes=48 << 20),
        cost_estimate=cost(9e-6 * PEAK_FLOPS, 8e6),
        name="self_forward",
    )(x, gain, weight, vec)


def self_backward_kernel(
    place_ref, x_ref, gain_ref, qkv_ref, do0_ref, do1_ref, do2_ref, do3_ref, lse_ref, wt_ref, vec_ref,
    dn_ref, gw_ref, dvec_ref, g_gain_ref,
    bias_ref, dsum_ref, dqkv_ref, do_ref, sum_ref,
):
    heads, size, _ = bias_ref.shape
    width = heads * HD
    e = pl.program_id(0)

    @pl.when(e == 0)
    def _():
        position_bias(vec_ref, bias_ref)
        dsum_ref[...] = jnp.zeros_like(dsum_ref)
        sum_ref[...] = jnp.zeros_like(sum_ref)
        dqkv_ref[...] = jnp.zeros_like(dqkv_ref)
        g_gain_ref[...] = jnp.zeros_like(g_gain_ref)

    for flip, piece_ref in enumerate((do0_ref, do1_ref, do2_ref, do3_ref)):
        do_ref[:, strip(place_index(place_ref, flip), piece_ref.shape[2])] = piece_ref[0]
    piece = lambda part, h: qkv_ref[0, width * part + HD * h : width * part + HD * (h + 1), :]
    out = lambda h: do_ref[HD * h : HD * (h + 1), :]
    products = lambda h: (dot(piece(1, h), piece(0, h), (0, 0)), dot(piece(2, h), out(h), (0, 0)))
    following = products(0)
    for h in range(heads):
        s, dp = following
        if h + 1 < heads:
            following = products(h + 1)
        p = jnp.exp(s + bias_ref[h] - lse_ref[0, h : h + 1, :])
        inner = jnp.sum(p * dp, axis=0, keepdims=True)
        ds = p * (dp - inner)
        dsum_ref[h] += ds
        ds = ds.astype(BF16)
        at = lambda part: slice(width * part + HD * h, width * part + HD * (h + 1))
        dqkv_ref[:, at(0)] = dot(piece(1, h), ds).T.astype(BF16)
        dqkv_ref[:, at(1)] = dot(ds, piece(0, h), (1, 1)).astype(BF16)
        dqkv_ref[:, at(2)] = dot(p.astype(BF16), out(h), (1, 1)).astype(BF16)
    dqkv = dqkv_ref[...]
    dn = dot(dqkv, wt_ref[...])
    dn_ref[0] = dn.astype(BF16)
    x = x_ref[0].astype(F32)
    scaled = x * lax.rsqrt(jnp.mean(x * x, axis=-1, keepdims=True) + NORM_EPS)
    g_gain_ref[...] += jnp.sum(dn * scaled, axis=0, keepdims=True)
    sum_ref[...] += dot((scaled * gain_ref[...]).astype(BF16), dqkv, (0, 0))

    @pl.when(e == pl.num_programs(0) - 1)
    def _():
        gw_ref[...] = sum_ref[...].astype(BF16)
        dvec_ref[...] = jnp.zeros_like(dvec_ref)
        for h in range(heads):
            back, count = dsum_ref[h], size
            while count > 8:
                count //= 2
                back = back[:count] + pltpu.roll(back[count:], size - count, 1)
            total = back[:1]
            for r in range(1, count):
                total = total + pltpu.roll(back[r : r + 1], size - r, 1)
            dvec_ref[h : h + 1, :] = total


def self_backward(place, x, gain, qkv, do, lse, wt, vec, heads):
    examples, length, model = x.shape
    feats = wt.shape[0]
    whole = lambda *shape: pl.BlockSpec(shape, lambda e: (0,) * len(shape))
    per = lambda *shape: pl.BlockSpec((1, *shape), lambda e: (e, 0, 0))
    return pl.pallas_call(
        self_backward_kernel,
        grid=(examples,),
        in_specs=[
            pl.BlockSpec(memory_space=pltpu.SMEM),
            per(length, model),
            whole(1, model),
            per(feats, length),
            *[per(heads * HD, length // 4)] * 4,
            per(8, length),
            whole(*wt.shape),
            whole(*vec.shape),
        ],
        out_specs=[per(length, model), whole(model, feats), whole(8, length), whole(1, model)],
        out_shape=[
            jax.ShapeDtypeStruct((examples, length, model), BF16),
            jax.ShapeDtypeStruct((model, feats), BF16),
            jax.ShapeDtypeStruct((8, length), F32),
            jax.ShapeDtypeStruct((1, model), F32),
        ],
        scratch_shapes=[
            pltpu.VMEM((heads, length, length), F32),
            pltpu.VMEM((heads, length, length), F32),
            pltpu.VMEM((length, feats), BF16),
            pltpu.VMEM((heads * HD, length), BF16),
            pltpu.VMEM((model, feats), F32),
        ],
        compiler_params=pltpu.CompilerParams(vmem_limit_bytes=48 << 20),
        cost_estimate=cost(16e-6 * PEAK_FLOPS, 12e6),
        name="self_backward",
    )(place, x, gain, qkv, *do, lse, wt, vec)


def work_list(live):
    examples, blocks = live.shape
    flat = live.reshape(-1)
    index = jnp.arange(flat.shape[0], dtype=jnp.int32)
    block = index % blocks
    visit = (flat > 0) | (block == 0)
    before = jnp.sum(jnp.where(visit[None, :] & (index[None, :] < index[:, None]), 1, 0), axis=1)
    ends = visit & ~jnp.any(
        visit[None, :] & (index[None, :] > index[:, None]) & (index[None, :] // blocks == index[:, None] // blocks), axis=1
    )
    chosen = (before[None, :] == index[:, None]) & visit[None, :]
    take = lambda values: jnp.sum(jnp.where(chosen, values[None, :], 0), axis=1)
    final = jnp.max(jnp.where(visit, index, 0))
    found = jnp.any(chosen, axis=1)
    at = jnp.where(found, take(index), final)
    rows = [at // blocks, at % blocks, take(flat), found & (at % blocks == 0), take(ends.astype(jnp.int32))]
    return jnp.stack([r.astype(jnp.int32) for r in rows])


def memory_project_kernel(work_ref, own_ref, other_ref, w_ref, k_ref, v_ref, wt_ref):
    i = pl.program_id(0)
    block, live = work_ref[1, i], work_ref[2, i]
    half = wt_ref.shape[0] // 2
    own_blocks = 2

    @pl.when(i == 0)
    def _():
        transpose_columns(w_ref, wt_ref)

    def project(rows):
        both = dot(wt_ref[...], rows, (1, 1)).astype(BF16)
        k_ref[0] = both[:half]
        v_ref[0] = both[half:]

    @pl.when((live > 0) & (block < own_blocks))
    def _():
        project(own_ref[0])

    @pl.when((live > 0) & (block >= own_blocks))
    def _():
        project(other_ref[0])


def memory_project(work, own, other, weight):
    examples, rows, model = own.shape
    half = rows // ROW_BLOCK
    feats = weight.shape[1] // 2
    row_spec = lambda first: pl.BlockSpec(
        (1, ROW_BLOCK, model), lambda i, work: (work[0, i], jnp.clip(work[1, i] - first, 0, half - 1), 0)
    )
    out_spec = pl.BlockSpec((1, feats, ROW_BLOCK), lambda i, work: (work[0, i], 0, work[1, i]))
    out = jax.ShapeDtypeStruct((examples, feats, 2 * rows), BF16)
    w_spec = lambda *shape: pl.BlockSpec(shape, lambda i, work: (0, 0))
    return pl.pallas_call(
        memory_project_kernel,
        grid_spec=pltpu.PrefetchScalarGridSpec(
            num_scalar_prefetch=1,
            grid=(work.shape[1],),
            in_specs=[row_spec(0), row_spec(half), w_spec(*weight.shape)],
            out_specs=[out_spec, out_spec, w_spec(2 * feats, model)],
        ),
        out_shape=[out, out, jax.ShapeDtypeStruct((2 * feats, model), BF16)],
        compiler_params=pltpu.CompilerParams(vmem_limit_bytes=48 << 20),
        cost_estimate=cost(12e-6 * PEAK_FLOPS, 12e6),
        name="memory_project",
    )(work, own, other, weight)


def cross_forward_kernel(work_ref, q_ref, k_ref, v_ref, o_ref, lse_ref, peak_ref, total_ref, acc_ref):
    i = pl.program_id(0)
    heads = acc_ref.shape[0] // HD
    live = work_ref[2, i]

    @pl.when(work_ref[3, i] == 1)
    def _():
        peak_ref[...] = jnp.full_like(peak_ref, MASKED)
        total_ref[...] = jnp.zeros_like(total_ref)
        acc_ref[...] = jnp.zeros_like(acc_ref)

    def scores(h):
        at = slice(HD * h, HD * (h + 1))
        return dot(k_ref[0, at, :], q_ref[0, at, :], (0, 0))

    def block(partial):
        following = scores(0)
        for h in range(heads):
            at = slice(HD * h, HD * (h + 1))
            s = following
            if h + 1 < heads:
                following = scores(h + 1)
            if partial:
                s = jnp.where(lax.broadcasted_iota(jnp.int32, s.shape, 0) < live, s, MASKED)
            before = peak_ref[h : h + 1, :]
            peak = jnp.maximum(before, jnp.max(s, axis=0, keepdims=True))
            p = jnp.exp(s - peak)
            shrink = jnp.exp(before - peak)
            peak_ref[h : h + 1, :] = peak
            total_ref[h : h + 1, :] = total_ref[h : h + 1, :] * shrink + jnp.sum(p, axis=0, keepdims=True)
            acc_ref[at, :] = acc_ref[at, :] * shrink + dot(v_ref[0, at, :], p.astype(BF16))

    @pl.when(live == ROW_BLOCK)
    def _():
        block(False)

    @pl.when((live > 0) & (live < ROW_BLOCK))
    def _():
        block(True)

    @pl.when(work_ref[4, i] == 1)
    def _():
        total = total_ref[...]
        some = total > 0
        inverse = jnp.where(some, 1.0 / jnp.where(some, total, 1.0), 0.0)
        lse_ref[0] = jnp.where(some, peak_ref[...] + jnp.log(jnp.where(some, total, 1.0)), MASKED)
        for h in range(heads):
            at = slice(HD * h, HD * (h + 1))
            o_ref[0, at, :] = (acc_ref[at, :] * inverse[h : h + 1, :]).astype(o_ref.dtype)


def cross_forward(work, q, k, v, first, count):
    _, feats, length = q.shape
    q_spec = pl.BlockSpec((1, feats, length), lambda i, work: (work[0, i] + first, 0, 0))
    o_spec = pl.BlockSpec((1, feats, length), lambda i, work: (work[0, i], 0, 0))
    k_spec = pl.BlockSpec((1, feats, ROW_BLOCK), lambda i, work: (work[0, i] + first, 0, work[1, i]))
    l_spec = pl.BlockSpec((1, 8, length), lambda i, work: (work[0, i], 0, 0))
    return pl.pallas_call(
        cross_forward_kernel,
        grid_spec=pltpu.PrefetchScalarGridSpec(
            num_scalar_prefetch=1,
            grid=(work.shape[1],),
            in_specs=[q_spec, k_spec, k_spec],
            out_specs=[o_spec, l_spec],
            scratch_shapes=[
                pltpu.VMEM((8, length), F32),
                pltpu.VMEM((8, length), F32),
                pltpu.VMEM((feats, length), F32),
            ],
        ),
        out_shape=[
            jax.ShapeDtypeStruct((count, feats, length), BF16),
            jax.ShapeDtypeStruct((count, 8, length), F32),
        ],
        compiler_params=pltpu.CompilerParams(vmem_limit_bytes=48 << 20),
        cost_estimate=cost(10e-6 * count * PEAK_FLOPS, 5e6 * count),
        name="cross_forward",
    )(work, q, k, v)


def cross_backward_kernel(
    work_ref, place_ref, q_ref, do0_ref, do1_ref, do2_ref, do3_ref, lse_ref, in0_ref, in1_ref, in2_ref, in3_ref,
    k_ref, v_ref, dq_ref, dkv_ref, acc_ref, do_ref, inner_ref,
):
    i = pl.program_id(0)
    feats = acc_ref.shape[0]
    heads = feats // HD
    live = work_ref[2, i]

    @pl.when(work_ref[3, i] == 1)
    def _():
        acc_ref[...] = jnp.zeros_like(acc_ref)
        for pieces, full_ref in (
            ((do0_ref, do1_ref, do2_ref, do3_ref), do_ref),
            ((in0_ref, in1_ref, in2_ref, in3_ref), inner_ref),
        ):
            for flip, piece_ref in enumerate(pieces):
                full_ref[:, strip(place_index(place_ref, flip), piece_ref.shape[2])] = piece_ref[0]

    def products(h):
        at = slice(HD * h, HD * (h + 1))
        return dot(k_ref[0, at, :], q_ref[0, at, :], (0, 0)), dot(v_ref[0, at, :], do_ref[at, :], (0, 0))

    def block(partial):
        following = products(0)
        for h in range(heads):
            at = slice(HD * h, HD * (h + 1))
            s, dp = following
            if h + 1 < heads:
                following = products(h + 1)
            p = jnp.exp(s - lse_ref[0, h : h + 1, :])
            if partial:
                p = jnp.where(lax.broadcasted_iota(jnp.int32, s.shape, 0) < live, p, 0.0)
            ds = (p * (dp - inner_ref[h : h + 1, :])).astype(BF16)
            acc_ref[at, :] += dot(k_ref[0, at, :], ds)
            dkv_ref[0, :, at] = dot(ds, q_ref[0, at, :], (1, 1)).astype(BF16)
            dkv_ref[0, :, feats + HD * h : feats + HD * (h + 1)] = dot(p.astype(BF16), do_ref[at, :], (1, 1)).astype(BF16)

    @pl.when(live == ROW_BLOCK)
    def _():
        block(False)

    @pl.when((live > 0) & (live < ROW_BLOCK))
    def _():
        block(True)

    @pl.when(work_ref[4, i] == 1)
    def _():
        dq_ref[0] = acc_ref[...].T.astype(BF16)


def cross_backward(work, place, q, do, lse, inner, k, v):
    examples, feats, length = q.shape
    rows = k.shape[2]
    of_example = lambda *shape: pl.BlockSpec((1, *shape), lambda i, work, place: (work[0, i], 0, 0))
    k_spec = pl.BlockSpec((1, feats, ROW_BLOCK), lambda i, work, place: (work[0, i], 0, work[1, i]))
    d_spec = pl.BlockSpec((1, ROW_BLOCK, 2 * feats), lambda i, work, place: (work[0, i], work[1, i], 0))
    return pl.pallas_call(
        cross_backward_kernel,
        grid_spec=pltpu.PrefetchScalarGridSpec(
            num_scalar_prefetch=2,
            grid=(work.shape[1],),
            in_specs=[
                of_example(feats, length),
                *[of_example(feats, length // 4)] * 4,
                of_example(8, length),
                *[of_example(8, length // 4)] * 4,
                k_spec,
                k_spec,
            ],
            out_specs=[of_example(length, feats), d_spec],
            scratch_shapes=[
                pltpu.VMEM((feats, length), F32),
                pltpu.VMEM((feats, length), BF16),
                pltpu.VMEM((8, length), F32),
            ],
        ),
        out_shape=[
            jax.ShapeDtypeStruct((examples, length, feats), BF16),
            jax.ShapeDtypeStruct((examples, rows, 2 * feats), BF16),
        ],
        compiler_params=pltpu.CompilerParams(vmem_limit_bytes=48 << 20),
        cost_estimate=cost(45e-6 * PEAK_FLOPS, 24e6),
        name="cross_backward",
    )(work, place, q, *do, lse, *inner, k, v)


def memory_backward_kernel(
    live_ref, own_ref, other_ref, dkv_ref, wt_ref, out_ref, out_other_ref, g_ref, sum_ref
):
    e, j = pl.program_id(0), pl.program_id(1)
    own_blocks = pl.num_programs(1) // 2

    @pl.when((e == 0) & (j == 0))
    def _():
        sum_ref[...] = jnp.zeros_like(sum_ref)

    for mine, rows_ref, to_ref in ((j < own_blocks, own_ref, out_ref), (j >= own_blocks, other_ref, out_other_ref)):

        @pl.when(mine & (live_ref[e, j] > 0))
        def _():
            dkv = dkv_ref[0]
            sum_ref[...] += dot(rows_ref[0], dkv, (0, 0))
            to_ref[0] = dot(dkv, wt_ref[...]).astype(BF16)

        @pl.when(mine & (live_ref[e, j] == 0))
        def _():
            to_ref[0] = jnp.zeros_like(to_ref[0])

    @pl.when((e == pl.num_programs(0) - 1) & (j == pl.num_programs(1) - 1))
    def _():
        g_ref[...] = sum_ref[...].astype(BF16)


def memory_backward(live, own, other, dkv, wt):
    examples, count, model = own.shape
    width = dkv.shape[2]
    half = count // ROW_BLOCK
    row_spec = lambda first: pl.BlockSpec(
        (1, ROW_BLOCK, model), lambda e, j, live: (e, jnp.clip(j - first, 0, half - 1), 0)
    )
    d_spec = pl.BlockSpec((1, ROW_BLOCK, width), lambda e, j, live: (e, j, 0))
    w_spec = pl.BlockSpec(wt.shape, lambda e, j, live: (0, 0))
    return pl.pallas_call(
        memory_backward_kernel,
        grid_spec=pltpu.PrefetchScalarGridSpec(
            num_scalar_prefetch=1,
            grid=(examples, 2 * half),
            in_specs=[row_spec(0), row_spec(half), d_spec, w_spec],
            out_specs=[row_spec(0), row_spec(half), pl.BlockSpec((model, width), lambda e, j, live: (0, 0))],
            scratch_shapes=[pltpu.VMEM((model, width), F32)],
        ),
        out_shape=[
            jax.ShapeDtypeStruct(own.shape, BF16),
            jax.ShapeDtypeStruct(own.shape, BF16),
            jax.ShapeDtypeStruct((model, width), BF16),
        ],
        compiler_params=pltpu.CompilerParams(vmem_limit_bytes=48 << 20),
        cost_estimate=cost(18e-6 * PEAK_FLOPS, 30e6),
        name="memory_backward",
    )(live, own, other, dkv, wt)


def self_output_kernel(
    place_ref, x_ref, o0_ref, o1_ref, o2_ref, o3_ref, mine_ref, other_ref, gain_ref,
    n2_ref, q_ref, x1_ref, own_o_ref, wo_ref, wq_ref,
    rows_ref,
):
    core = jnp.bitwise_and(place_ref[0], 1)
    feats = wq_ref.shape[1]
    width = o0_ref.shape[1]
    own = x1_ref.shape[1]

    @pl.when(pl.program_id(0) == 0)
    def _():
        for i, from_ref in ((core, mine_ref), (1 - core, other_ref)):
            wo_ref[:, strip(i, feats)] = from_ref[:, feats:]
        for i, from_ref in enumerate((mine_ref, other_ref)):
            for at in range(0, feats, LANES):
                wq_ref[i, at : at + LANES, :] = from_ref[:, at : at + LANES].T

    x1 = x_ref[0].astype(F32)
    for flip, o_ref in enumerate((o0_ref, o1_ref, o2_ref, o3_ref)):
        heads = strip(place_index(place_ref, flip), width)
        x1 += dot(o_ref[0], wo_ref[heads, :], (0, 0))
        own_o_ref[0, heads, :] = o_ref[0, :, strip(place_ref[0], own)]
    n2 = root_norm(x1, gain_ref[...]).astype(BF16)
    n2_ref[0] = n2
    q_ref[0] = dot(wq_ref[0], n2, (1, 1)).astype(BF16)
    rows_ref[...] = x1
    x1_ref[0] = rows_ref[strip(place_ref[0], own), :]


def self_output_stage(place, x, pieces, mine, other, gain):
    examples, length, model = x.shape
    own, feats, width = length // 4, model // 2, pieces[0].shape[1]
    whole = lambda *shape: pl.BlockSpec(shape, lambda e: (0,) * len(shape))
    per = lambda *shape: pl.BlockSpec((1, *shape), lambda e: (e, 0, 0))
    array = jax.ShapeDtypeStruct
    return pl.pallas_call(
        self_output_kernel,
        grid=(examples,),
        in_specs=[pl.BlockSpec(memory_space=pltpu.SMEM), per(length, model)]
        + [per(width, length)] * 4
        + [whole(*mine.shape), whole(*other.shape), whole(1, model)],
        out_specs=[
            per(length, model),
            per(feats, length),
            per(own, model),
            per(model, own),
            whole(model, model),
            whole(2, feats, model),
        ],
        out_shape=[
            array((examples, length, model), BF16),
            array((examples, feats, length), BF16),
            array((examples, own, model), F32),
            array((examples, model, own), BF16),
            array((model, model), BF16),
            array((2, feats, model), BF16),
        ],
        scratch_shapes=[pltpu.VMEM((length, model), F32)],
        compiler_params=pltpu.CompilerParams(vmem_limit_bytes=48 << 20),
        cost_estimate=cost(6e-6 * PEAK_FLOPS, 10e6),
        name="self_output_stage",
    )(place, x, *pieces, mine, other, gain)


def combine_kernel(place_ref, o_ref, came_ref, lse_ref, other_lse_ref, chip_ref, total_ref):
    row = lax.shift_right_logical(place_ref[0], 1)
    here = strip(row, came_ref.shape[2])
    one, two = lse_ref[0], other_lse_ref[0]
    peak = jnp.maximum(one, two)
    total_ref[0] = peak + jnp.log(jnp.exp(one - peak) + jnp.exp(two - peak))
    own_weight = jnp.exp(lse_ref[0, :, here] - total_ref[0, :, here])
    other_weight = jnp.exp(other_lse_ref[0, :, here] - total_ref[0, :, here])
    for h in range(o_ref.shape[1] // HD):
        at = slice(HD * h, HD * (h + 1))
        one = o_ref[0, at, here].astype(F32) * own_weight[h : h + 1, :]
        chip_ref[0, at, :] = (one + came_ref[0, at, :].astype(F32) * other_weight[h : h + 1, :]).astype(BF16)


def combine(place, o, came, lse, other_lse):
    examples, feats, length = o.shape
    per = lambda *shape: pl.BlockSpec((1, *shape), lambda e: (e, 0, 0))
    return pl.pallas_call(
        combine_kernel,
        grid=(examples,),
        in_specs=[
            pl.BlockSpec(memory_space=pltpu.SMEM),
            per(feats, length),
            per(feats, length // 2),
            per(8, length),
            per(8, length),
        ],
        out_specs=[per(feats, length // 2), per(8, length)],
        out_shape=[
            jax.ShapeDtypeStruct((examples, feats, length // 2), BF16),
            jax.ShapeDtypeStruct((examples, 8, length), F32),
        ],
        compiler_params=pltpu.CompilerParams(vmem_limit_bytes=24 << 20),
        cost_estimate=cost(2e-6 * PEAK_FLOPS, 3e6),
        name="combine",
    )(place, o, came, lse, other_lse)


def norm_back(values, gain, grad):
    scale = lax.rsqrt(jnp.mean(values * values, axis=-1, keepdims=True) + NORM_EPS)
    pulled = grad * gain
    inner = jnp.mean(values * pulled, axis=-1, keepdims=True)
    back = scale * pulled - values * (scale * scale * scale * inner)
    return back, jnp.sum(grad * values * scale, axis=0, keepdims=True)


def feed_forward_kernel(
    place_ref, x1_ref, mine_ref, other_ref, dy_ref, gain_ref, wo_ref, gate_ref, up_ref, down_ref,
    out_ref, dx2_ref, doc_mine_ref, doc_other_ref, inner_mine_ref, inner_other_ref,
    g_ref, g_sent_ref, g_down_ref, g_down_sent_ref, g_out_ref, g_out_sent_ref, g_gain_ref,
    x2_ref, n3_ref, sum_ref, dn3_ref, g_full_ref, *, piece,
):
    i = pl.program_id(0)
    core = jnp.bitwise_and(place_ref[0], 1)
    examples, feats, own = mine_ref.shape

    def deal(low, high, keep_ref, sent_ref):
        keep_ref[...] = jnp.where(core == 0, low, high).astype(BF16)
        sent_ref[...] = jnp.where(core == 0, high, low).astype(BF16)
    sides = ((core, mine_ref, doc_mine_ref, inner_mine_ref), (1 - core, other_ref, doc_other_ref, inner_other_ref))

    @pl.when(i == 0)
    def _():
        for e in range(examples):
            x2 = x1_ref[own * e : own * (e + 1), :]
            for side, o_ref, *_ in sides:
                x2 += dot(o_ref[e], wo_ref[strip(side, feats), :], (0, 0))
            x2_ref[own * e : own * (e + 1), :] = x2
        n3_ref[...] = root_norm(x2_ref[...], gain_ref[...]).astype(BF16)
        sum_ref[...] = jnp.zeros_like(sum_ref)
        dn3_ref[...] = jnp.zeros_like(dn3_ref)

    n3, dy = n3_ref[...], dy_ref[...]
    a, u = dot(n3, gate_ref[...]), dot(n3, up_ref[...])
    dh = dot(dy, down_ref[...], (1, 1))
    root = math.sqrt(2 / math.pi)
    bent = jnp.tanh(root * (a + 0.044715 * (a * a * a)))
    rise = 0.5 * (1.0 + bent)
    gelu = a * rise
    slope = rise + 0.5 * a * (1.0 - bent * bent) * (root * (1.0 + 3 * 0.044715 * (a * a)))
    hidden = (gelu * u).astype(BF16)
    da = (dh * u * slope).astype(BF16)
    du = (dh * gelu).astype(BF16)
    sum_ref[...] += dot(hidden, down_ref[...])
    g_down = dot(hidden, dy, (0, 0))
    pieces = g_down.reshape(g_down.shape[0] // (2 * piece), 2, piece, g_down.shape[1])
    deal(*(pieces[:, side].reshape(g_down_ref.shape) for side in range(2)), g_down_ref, g_down_sent_ref)
    deal(dot(n3, da, (0, 0)), dot(n3, du, (0, 0)), g_ref, g_sent_ref)
    dn3_ref[...] += dot(da, gate_ref[...], (1, 1)) + dot(du, up_ref[...], (1, 1))

    @pl.when(i == pl.num_programs(0) - 1)
    def _():
        x2 = x2_ref[...]
        out_ref[...] = (x2 + sum_ref[...]).astype(BF16)
        back, g_gain = norm_back(x2, gain_ref[...], dn3_ref[...])
        g_gain_ref[...] = g_gain
        dx2 = dy_ref[...].astype(F32) + back
        dx2_ref[...] = dx2
        n3_ref[...] = dx2.astype(BF16)
        for side, o_ref, doc_ref, inner_ref in sides:
            heads = strip(side, feats)
            total = jnp.zeros((feats, wo_ref.shape[1]), F32)
            inner_ref[...] = jnp.zeros_like(inner_ref)
            for e in range(examples):
                dx2r = n3_ref[own * e : own * (e + 1), :]
                total += dot(o_ref[e], dx2r)
                doc = dot(wo_ref[heads, :], dx2r, (1, 1)).astype(BF16)
                doc_ref[e] = doc
                product = doc.astype(F32) * o_ref[e].astype(F32)
                for h in range(feats // HD):
                    inner_ref[e, h : h + 1, :] = jnp.sum(product[HD * h : HD * (h + 1)], axis=0, keepdims=True)
            g_full_ref[heads, :] = total
        deal(g_full_ref[:, :feats], g_full_ref[:, feats:], g_out_ref, g_out_sent_ref)


def feed_forward(place, x1, mine, other, dy, gain, wide_w, down, piece):
    tokens, model = x1.shape
    examples, feats, own = mine.shape
    hidden = down.shape[0]
    part = 256
    whole = lambda *shape: pl.BlockSpec(shape, lambda i: (0,) * len(shape))
    first = model // part
    array = jax.ShapeDtypeStruct
    return pl.pallas_call(
        functools.partial(feed_forward_kernel, piece=piece),
        grid=(hidden // part,),
        in_specs=[
            pl.BlockSpec(memory_space=pltpu.SMEM),
            whole(tokens, model),
            whole(*mine.shape),
            whole(*other.shape),
            whole(tokens, model),
            whole(1, model),
            whole(model, model),
            pl.BlockSpec((model, part), lambda i: (0, first + i)),
            pl.BlockSpec((model, part), lambda i: (0, first + hidden // part + i)),
            pl.BlockSpec((part, model), lambda i: (i, 0)),
        ],
        out_specs=[
            whole(tokens, model),
            whole(tokens, model),
            whole(*mine.shape),
            whole(*mine.shape),
            whole(examples, 8, own),
            whole(examples, 8, own),
            *[pl.BlockSpec((model, part), lambda i: (0, i))] * 2,
            *[pl.BlockSpec((part // 2, model), lambda i: (i, 0))] * 2,
            *[whole(model, feats)] * 2,
            whole(1, model),
        ],
        out_shape=[
            array((tokens, model), BF16),
            array((tokens, model), F32),
            array(mine.shape, BF16),
            array(mine.shape, BF16),
            array((examples, 8, own), F32),
            array((examples, 8, own), F32),
            *[array((model, hidden), BF16)] * 2,
            *[array((hidden // 2, model), BF16)] * 2,
            *[array((model, feats), BF16)] * 2,
            array((1, model), F32),
        ],
        scratch_shapes=[
            pltpu.VMEM((tokens, model), F32),
            pltpu.VMEM((tokens, model), BF16),
            pltpu.VMEM((tokens, model), F32),
            pltpu.VMEM((tokens, model), F32),
            pltpu.VMEM((model, model), F32),
        ],
        compiler_params=pltpu.CompilerParams(vmem_limit_bytes=48 << 20),
        cost_estimate=cost(20e-6 * PEAK_FLOPS, 24e6),
        name="feed_forward",
    )(place, x1, mine, other, dy, gain, wide_w, wide_w, wide_w, down)


def self_output_back_kernel(
    place_ref, mine_ref, other_ref, wq_ref, x1_ref, gain_ref, dx2_ref, own_o_ref, wo_ref,
    dx1_ref, do_mine_ref, do_pair_ref, do_across_ref, g_keep_ref, g_sent_ref, g_gain_ref,
    sum_ref, do_ref,
):
    e = pl.program_id(0)
    core, row = jnp.bitwise_and(place_ref[0], 1), lax.shift_right_logical(place_ref[0], 1)
    width, feats = do_mine_ref.shape[1], do_across_ref.shape[1]

    @pl.when(e == 0)
    def _():
        sum_ref[...] = jnp.zeros_like(sum_ref)
        g_gain_ref[...] = jnp.zeros_like(g_gain_ref)

    dn2 = dot(mine_ref[0], wq_ref[0]) + dot(other_ref[0], wq_ref[1])
    back, g_gain = norm_back(x1_ref[0], gain_ref[...], dn2)
    g_gain_ref[...] += g_gain
    dx1 = dx2_ref[0] + back
    dx1_ref[0] = dx1
    dx1r = dx1.astype(BF16)
    do_ref[...] = dot(wo_ref[...], dx1r, (1, 1)).astype(BF16)
    do_mine_ref[0] = do_ref[strip(place_ref[0], width), :]
    do_pair_ref[0] = do_ref[strip(place_index(place_ref, 1), width), :]
    do_across_ref[0] = do_ref[strip(1 - row, feats), :]
    sum_ref[...] += dot(own_o_ref[0], dx1r)

    @pl.when(e == pl.num_programs(0) - 1)
    def _():
        g_keep_ref[...] = sum_ref[:, strip(core, feats)].astype(BF16)
        g_sent_ref[...] = sum_ref[:, strip(1 - core, feats)].astype(BF16)


def self_output_back(place, mine, other, wq, x1, gain, dx2, own_o, wo):
    examples, own, model = x1.shape
    feats = mine.shape[2]
    whole = lambda *shape: pl.BlockSpec(shape, lambda e: (0,) * len(shape))
    per = lambda *shape: pl.BlockSpec((1, *shape), lambda e: (e, 0, 0))
    array = jax.ShapeDtypeStruct
    return pl.pallas_call(
        self_output_back_kernel,
        grid=(examples,),
        in_specs=[
            pl.BlockSpec(memory_space=pltpu.SMEM),
            per(own, feats),
            per(own, feats),
            whole(*wq.shape),
            per(own, model),
            whole(1, model),
            per(own, model),
            per(model, own),
            whole(model, model),
        ],
        out_specs=[
            per(own, model),
            *[per(model // 4, own)] * 2,
            per(feats, own),
            *[whole(model, feats)] * 2,
            whole(1, model),
        ],
        out_shape=[
            array((examples, own, model), F32),
            *[array((examples, model // 4, own), BF16)] * 2,
            array((examples, feats, own), BF16),
            *[array((model, feats), BF16)] * 2,
            array((1, model), F32),
        ],
        scratch_shapes=[pltpu.VMEM((model, model), F32), pltpu.VMEM((model, own), BF16)],
        compiler_params=pltpu.CompilerParams(vmem_limit_bytes=48 << 20),
        cost_estimate=cost(4e-6 * PEAK_FLOPS, 8e6),
        name="self_output_back",
    )(place, mine, other, wq, x1, gain, dx2, own_o, wo)


def fold_rows(rows, target, columns):
    rest = rows * columns // target
    tile = 16
    if rows % tile or rows // tile * LANES != rest or columns // LANES * tile != target:
        return (lambda b: b.reshape(*b.shape[:-2], target, rest)), (lambda b: b.reshape(rows, columns))

    def swap(b, down, across):
        b = b.reshape(*b.shape[:-2], down, tile, across, LANES)
        return jnp.swapaxes(b, -4, -2).reshape(*b.shape[:-4], across * tile, down * LANES)

    return (lambda b: swap(b, rows // tile, columns // LANES)), (lambda b: swap(b, target // tile, rest // LANES))


def local(
    dec_input,
    enc_out,
    enc_len,
    cotangent,
    self_query,
    self_key,
    self_value,
    self_output,
    cross_query,
    cross_key,
    cross_value,
    cross_output,
    ffn_gate,
    ffn_up,
    ffn_down,
    self_gain,
    cross_gain,
    ffn_gain,
    bias_table,
):
    place = lax.axis_index("narrow")
    row, core = place // 2, place % 2
    wide = lax.axis_size("wide")
    examples, own, model = dec_input.shape
    length = 4 * own
    heads = model // HD
    own_heads = heads // 4
    memory_rows = enc_out.shape[1]
    share = self_query.shape[0]

    half = lambda w: part_of(w.astype(BF16), core, 2, 1)
    own_qkv = jnp.concatenate(
        [part_of(w.astype(BF16), place, 4, 1) for w in (self_query, self_key, self_value)], 1
    )
    own_qkv = jnp.pad(own_qkv, ((0, 0), (0, -own_qkv.shape[1] % LANES)))
    small = jnp.stack([self_gain, cross_gain, ffn_gain, jnp.pad(bias_table, (0, share - bias_table.shape[0]))], 1)
    small = jnp.pad(small.astype(BF16), ((0, 0), (0, LANES - 4)))
    feats = model // 2
    self_w, small = wide_gather(jnp.concatenate([own_qkv, small], 1), (own_qkv.shape[1], LANES))
    small_rows = small[:, :4].astype(F32).T
    gain_one, gain_two, gain_three = (small_rows[i : i + 1] for i in range(3))
    table = small_rows[3].reshape(wide, share)[:, : bias_table.shape[0]].reshape(BUCKETS, heads)

    both = ("wide", "narrow")
    quarter = lambda w: part_of(w.astype(BF16), place, 4, 0)
    ffn_in = lax.all_gather(
        jnp.concatenate([quarter(cross_output), quarter(ffn_gate), quarter(ffn_up)], 1), both, axis=0, tiled=True
    )
    down_w = lax.all_gather(quarter(ffn_down), both, axis=0, tiled=True)

    enc_other = pair_swap(enc_out)
    starts = (place * memory_rows + np.arange(memory_rows // ROW_BLOCK) * ROW_BLOCK).astype(jnp.int32)
    other_starts = starts + (1 - 2 * core) * memory_rows
    block_starts = jnp.concatenate([starts, other_starts])
    live = jnp.clip(enc_len[:, None] - block_starts[None, :], 0, ROW_BLOCK)

    x_all = narrow_gather(dec_input, 1, row, core)
    hot = jnp.asarray(bucket_table(length))
    distance_bias = jnp.dot(table.T, hot, precision=FULL_ACCURACY)
    vec = jnp.pad(part_of(distance_bias, place, 4, 0), ((0, 8 - own_heads), (0, 0)))
    qkv, self_o, self_lse, self_wt = self_forward(x_all, gain_one, self_w, vec, own_heads)
    across_o = across_swap(self_o)
    pieces = [self_o, pair_swap(self_o), across_o, pair_swap(across_o)]
    memory_w = shared_gather(jnp.concatenate([half(cross_key), half(cross_value)], 1), row, first=(self_o,))
    work = work_list(live)
    keys, values, memory_wt = memory_project(work, enc_out, enc_other, memory_w)
    query_out = after(jnp.concatenate([half(cross_query), half(self_output)], 1), self_o)
    (mine_w,) = wide_gather(query_out, (query_out.shape[1],))
    mine_w = after(mine_w, keys)
    other_w = pair_swap(mine_w)
    me = place.reshape(1).astype(jnp.int32)
    n2, cross_q, x1, own_o, self_out_w, cross_query_wt = self_output_stage(
        me, x_all, pieces, mine_w, other_w, gain_two
    )

    apart = examples - 1
    part_o, part_lse = cross_forward(work_list(live[:apart]), cross_q, keys, values, 0, apart)
    came, came_lse = across_swap(part_of(part_o, 1 - row, 2, 2)), across_swap(part_lse)
    last_work = after(work_list(live[apart:]), part_o)
    last_o, last_lse = cross_forward(last_work, cross_q, keys, values, apart, examples - apart)
    last_o, last_lse, came, came_lse = lax.optimization_barrier((last_o, last_lse, came, came_lse))
    last_came, last_came_lse = across_swap(part_of(last_o, 1 - row, 2, 2)), across_swap(last_lse)
    chips = [
        combine(me, part_o, came, part_lse, came_lse),
        combine(me, last_o, last_came, last_lse, last_came_lse),
    ]
    lse = jnp.concatenate([chip_lse for _, chip_lse in chips])
    mine_o = jnp.concatenate([part_of(chip_o, core, 2, 2) for chip_o, _ in chips])
    other_o = jnp.concatenate([pair_swap(part_of(chip_o, 1 - core, 2, 2)) for chip_o, _ in chips])

    tokens = examples * own
    down_rows = ffn_down.shape[0] // 2
    (
        layer_out, dx2, doc_mine, doc_other, inner_mine, inner_other,
        gate_up, gate_up_sent, down, down_sent, grad_co, co_sent, grad_gain_three,
    ) = feed_forward(
        me, x1.reshape(tokens, model), mine_o, other_o, cotangent.reshape(tokens, model), gain_three,
        ffn_in, down_w, down_rows,
    )
    layer_out, dx2 = layer_out.reshape(x1.shape), dx2.reshape(x1.shape)

    rows_of = lambda g: g.reshape(wide, share, -1)

    def from_all(mine, other):
        pair = pair_swap(other)
        return [mine, pair, across_swap(mine), across_swap(pair)]

    doc, inner = from_all(doc_mine, doc_other), from_all(inner_mine, inner_other)
    ffn = gate_up, pair_swap(gate_up_sent)
    by_y = lambda y: [part_of(g, y, 2, 1).astype(F32) for g in ffn]
    ffn_sent = sum(by_y(1 - row)).astype(BF16)
    down = plus(down, pair_swap(down_sent)).reshape(wide, down_rows, model)
    co = plus(grad_co, pair_swap(co_sent))
    doc, inner, ffn_sent, down, co = lax.optimization_barrier((doc, inner, ffn_sent, down, co))
    ffn_came, down = across_swap(ffn_sent), wide_scatter_x(down)
    part_dq, dkv = cross_backward(work, me, cross_q, doc, lse, inner, keys, values)
    part_dq, dkv, ffn_came, down = lax.optimization_barrier((part_dq, dkv, ffn_came, down))
    ffn = wide_scatter_x(rows_of(sum(by_y(row), ffn_came.astype(F32)).astype(BF16)))

    dq_came = across_swap(part_of(part_dq, 1 - row, 2, 1))
    enc_mine, enc_swapped, grad_memory = memory_backward(live, enc_out, enc_other, dkv, memory_wt)
    enc_came = pair_swap(enc_swapped)
    dq_came, grad_memory, ffn = lax.optimization_barrier((dq_came, grad_memory, ffn))
    down_came = across_swap(part_of(down, 1 - row, 2, 1))
    chip_dq = plus(part_of(part_dq, row, 2, 1), dq_came)
    dq_mine, dq_other = part_of(chip_dq, core, 2, 1), pair_swap(part_of(chip_dq, 1 - core, 2, 1))
    grad_cross_query = jnp.einsum("etd,etf->df", n2, part_dq, preferred_element_type=F32).astype(BF16)
    late = x_swap(jnp.concatenate([rows_of(g) for g in (grad_cross_query, grad_memory, co)], 2))
    dx1, do_mine, do_pair, do_across, grad_so, so_sent, grad_gain_two = self_output_back(
        me, dq_mine, dq_other, cross_query_wt, x1, gain_two, dx2, own_o, self_out_w
    )

    ffn = z_swap(after(ffn, do_across))

    do_came = across_swap(do_across)
    do = [do_mine, pair_swap(do_pair), part_of(do_came, core, 2, 1), pair_swap(part_of(do_came, 1 - core, 2, 1))]
    so = rows_of(plus(grad_so, pair_swap(so_sent)))
    down = plus(part_of(down, row, 2, 1), down_came)
    do, so, late, down = lax.optimization_barrier((do, so, late, down))
    fold, unfold = fold_rows(down.shape[1], share, model)
    late = z_swap(jnp.concatenate([total(late), fold(down)], 2))
    so_came = across_swap(part_of(so, 1 - row, 2, 1))
    part_dn1, grad_self, dvec, grad_gain_one = self_backward(
        me, x_all, gain_one, qkv, do, self_lse, self_wt, vec, own_heads
    )
    part_dn1, grad_self, so_came, ffn, *early = lax.optimization_barrier((part_dn1, grad_self, so_came, ffn, *late[:-1]))
    late, ffn_sum = (*early, *late[-1:]), total(ffn)

    own_table = jnp.dot(hot, dvec[:own_heads].T, precision=FULL_ACCURACY)
    grad_table = lax.dynamic_update_slice_in_dim(
        jnp.zeros((BUCKETS, heads), F32), own_table, place * own_heads, 1
    )
    small = [g.reshape(wide, -1) for g in (grad_gain_one, grad_gain_two, grad_gain_three, grad_table)]
    small = jnp.concatenate(small, 1).astype(BF16)
    small_count = small.shape[1]
    small = jnp.pad(small, ((0, 0), (0, share // 2 * LANES - small_count))).reshape(wide, -1, LANES)
    so = plus(part_of(so, row, 2, 1), so_came)
    self_width = grad_self.shape[1]
    self_halves = grad_self.reshape(wide, 2, share // 2, self_width)
    last = x_swap(jnp.concatenate([self_halves[:, 0], self_halves[:, 1], so, small], 2))
    by_core = part_dn1.reshape(examples, 2, 2, own, model)
    column = plus(part_of(by_core, core, 2, 2).astype(F32), pair_swap(part_of(by_core, 1 - core, 2, 2)))
    dn1_sent = part_of(column, 1 - row, 2, 1).astype(BF16)
    enc_grad = plus(enc_mine, enc_came)
    sums = jnp.concatenate([ffn_sum, total(late)], 1)
    dn1_came, sums_came = across_swap(dn1_sent), across_swap(sums)
    last, dn1_sent, enc_grad, sums = lax.optimization_barrier((last, dn1_sent, enc_grad, sums))
    last = z_swap(total(last))
    last, dn1_came = lax.optimization_barrier((last, dn1_came))
    last_sum = total(last)
    last_came = across_swap(last_sum)
    dn1 = plus(part_of(column, row, 2, 1), dn1_came)
    grad_in, _ = norm_back(
        dec_input.reshape(tokens, model).astype(F32), gain_one, dn1.reshape(tokens, model)
    )
    input_grad = (dx1 + grad_in.reshape(x1.shape)).astype(BF16)

    bounds = np.cumsum([0, ffn_sum.shape[1], 4 * feats])
    low, high = in_order(row, sums, sums_came)
    sums = jnp.concatenate(
        [
            low[:, : bounds[1]],
            high[:, : bounds[1]],
            plus(sums[:, bounds[1] : bounds[2]], sums_came[:, bounds[1] : bounds[2]]),
            low[:, bounds[2] :],
            high[:, bounds[2] :],
        ],
        1,
    )
    parts = in_order(core, sums, pair_swap(sums))
    gate_sum, up_sum = (part[:, : 2 * bounds[1]] for part in parts)
    cq_sum, ck_sum, cv_sum, co_sum = (
        jnp.concatenate([part[:, 2 * bounds[1] + feats * i : 2 * bounds[1] + feats * (i + 1)] for part in parts], 1)
        for i in range(4)
    )
    down_sum = [jnp.split(part[:, 2 * bounds[1] + 4 * feats :], 2, 1) for part in parts]
    down_sum = jnp.concatenate([unfold(half) for part in down_sum for half in part], 0)

    last = jnp.stack(in_order(row, last_sum, last_came))
    low, high = in_order(core, last, pair_swap(last))
    halves = lambda part: jnp.concatenate([part[:, :self_width], part[:, self_width : 2 * self_width]], 0)
    self_sum = [halves(part[y]) for y in range(2) for part in (low, high)]
    q_sum, k_sum, v_sum = (
        jnp.concatenate([part[:, own_heads * HD * i : own_heads * HD * (i + 1)] for part in self_sum], 1)
        for i in range(3)
    )
    so_sum = jnp.concatenate(
        [part[:, :, 2 * self_width : 2 * self_width + feats].reshape(share, -1) for part in (low, high)], 1
    )
    small_sum = sum(part[y, :, 2 * self_width + feats :].astype(F32) for part in (low, high) for y in range(2))
    small_sum = small_sum.reshape(-1)[:small_count]
    f = lambda a: a.astype(F32)
    return (
        layer_out,
        input_grad,
        enc_grad,
        *(f(g) for g in (q_sum, k_sum, v_sum, so_sum, cq_sum, ck_sum, cv_sum, co_sum, gate_sum, up_sum, down_sum)),
        small_sum[:share],
        small_sum[share : 2 * share],
        small_sum[2 * share : 3 * share],
        small_sum[3 * share :],
    )


def solution(mesh):
    rows = P("wide", "narrow", None)
    weight, vector = P("wide", None), P("wide")
    return jax.shard_map(
        local,
        mesh=mesh,
        in_specs=(rows, rows, vector, rows, *[weight] * 11, *[vector] * 4),
        out_specs=(rows, rows, rows, *[weight] * 11, *[vector] * 4),
        check_vma=False,
    )
```
